128 devices in a mesh: seq: 32 (over y, z, core), head: 4 (over x).
Axes of the slice: x: 4, y: 4, z: 4, core: 2. Of those that a mesh axis runs over, the one named last changes fastest.
Arguments:
- image_patches: bfloat16 [32, 256, 1152], P('seq', None, 'head'), may hold values from -6 to 6
- text_embed: bfloat16 [8192, 2048], P('seq', 'head'), may hold values from -6 to 6
- image_start: int32 [32], replicated, may hold values from 0 to 126, as said below
- image_forget: float32 [32], replicated, may hold values from 0.001 to 0.3
- adapter: bfloat16 [1152, 2048], P('head'), may hold values from -0.1875 to 0.1875
- norm_gain: float32 [2048], replicated, may hold values from 0.5 to 1.5
- in_proj: bfloat16 [2048, 4, 2048], P(None, None, 'head'), may hold values from -0.125 to 0.125
- decay_proj: bfloat16 [2048, 16], P(None, 'head'), may hold values from -0.125 to 0.125
- head_decay_ceiling: float32 [16], P('head'), may hold values from 0 to 1, as said below
- out_gain: float32 [16, 128], P('head'), may hold values from 0.5 to 1.5
- out_proj: bfloat16 [2048, 2048], P('head'), may hold values from -0.125 to 0.125
Outputs:
- image_out: bfloat16 [32, 256, 2048], P('seq', None, 'head')
- text_out: bfloat16 [8192, 2048], P('seq', 'head')
The draws below stay inside these ranges and needn't reach their ends.
Inputs may be any that keep to these rules, and one draw needn't show every extreme that they name: `image_start`: each entry is even; the images take distinct pairs of blocks. The merged piece of 512 tokens on one device of seq never holds both the image and the text that one device of seq holds in the source layout. `head_decay_ceiling`: Positive.
All inputs are finite; a program needn't handle non-finite values.
Results may differ from the reference program's by a relative error of at most 0.0095.
Values may be sent and summed in bfloat16 or wider, within the bound.
No kernel may reach another device: no remote copies, remote signals or barrier semaphores. Data moves between devices by JAX's collectives and lax.ppermute only.
A program may use at most 128 MiB of HBM per device.

```python
import math
import jax
import jax.numpy as jnp
from jax import lax

H = 16
HD = 128
PIN = 1152
PATCH_COUNT = 256
D = 2048
TOK_DEV = 512
IMAGES = 32
TEXT = 8192
LENGTH = 16384
N_SEQ = 32


def draw_image_start(key, part):
    first_key = jax.random.fold_in(key, 11)
    second_key = jax.random.fold_in(key, 12)
    unit_count = 2 * IMAGES
    shuffled = jax.random.permutation(first_key, unit_count)
    flags = (shuffled < IMAGES).astype(jnp.int32)
    ranking = jnp.argsort((1 - flags) * unit_count + jnp.arange(unit_count, dtype=jnp.int32))
    image_units = ranking[:IMAGES].astype(jnp.int32)
    rotation = 2 * jax.random.randint(second_key, (), 0, IMAGES // 2) + 1
    ordinal = (jnp.arange(IMAGES, dtype=jnp.int32) - rotation) % IMAGES
    return (2 * jnp.take(image_units, ordinal)).astype(jnp.int32)


def draw_head_decay_ceiling(key, part):
    slow_key = jax.random.fold_in(key, 21)
    fast_key = jax.random.fold_in(key, 22)
    pick_key = jax.random.fold_in(key, 23)
    slow = jnp.exp(jax.random.uniform(slow_key, (H,), minval=math.log(0.2 / LENGTH), maxval=math.log(1.5 / LENGTH)))
    fast = jnp.exp(jax.random.uniform(fast_key, (H,), minval=math.log(0.02), maxval=math.log(0.1)))
    share = 0.5
    keeping = jax.random.uniform(pick_key, (H,)) < share
    return jnp.where(keeping, slow, fast).astype(jnp.float32)


def levels(own_key, extent, shards, low, largest):
    gain = 1.0
    for axis_at, shards_of in shards:
        heights = jax.random.uniform(jax.random.fold_in(jax.random.fold_in(own_key, 6), axis_at), (shards_of,), jnp.float32, low / len(shards), largest / len(shards))
        gain = gain * jnp.repeat(jnp.exp(heights), extent[axis_at] // shards_of).reshape((-1,) + (1,) * (len(extent) - 1 - axis_at))
    return gain


def centred(stream_key, extent, spread, bound, shards=(), kind=jnp.bfloat16):
    level = levels(stream_key, extent, shards, -0.22, 0.18) if shards else 1.0
    values = jax.random.normal(stream_key, extent, jnp.float32) * spread * level
    return jnp.minimum(jnp.maximum(values, -bound), bound).astype(kind)


def setup_inputs(seed: int = 0) -> dict:
    streams_of = jax.random.split(jax.random.key(seed), 12)
    return {
        "image_patches": centred(streams_of[0], (IMAGES, PATCH_COUNT, PIN), 1.0, 6.0, ((0, 32), (2, 4))),
        "text_embed": centred(streams_of[1], (TEXT, D), 1.0, 6.0, ((0, 32), (1, 4))),
        "image_start": draw_image_start(jax.random.fold_in(streams_of[11], 71), 0),
        "image_forget": jnp.clip(jnp.exp(jax.random.uniform(streams_of[3], (IMAGES,), jnp.float32, math.log(0.001), math.log(0.3))), 0.001, 0.3),
        "adapter": centred(streams_of[4], (PIN, D), PIN ** -0.5, 0.1875, ((0, 4),)),
        "norm_gain": jnp.clip(1.0 + 0.1 * jax.random.normal(streams_of[5], (D,), jnp.float32), 0.5, 1.5),
        "in_proj": centred(streams_of[6], (D, 4, D), D ** -0.5, 0.125, ((2, 4),)),
        "decay_proj": centred(streams_of[7], (D, H), D ** -0.5, 0.125, ((1, 4),)),
        "head_decay_ceiling": draw_head_decay_ceiling(jax.random.fold_in(streams_of[11], 71), 0),
        "out_gain": jnp.clip(1.0 + 0.1 * jax.random.normal(streams_of[9], (H, HD), jnp.float32), 0.5, 1.5),
        "out_proj": centred(streams_of[10], (D, D), D ** -0.5, 0.125, ((0, 4),)),
    }


EPSILON = 1e-06

def rms_scale(values, gain_row):
    mean_square = lax.optimization_barrier(jnp.mean(values * values, axis=-1, keepdims=True))
    return values * lax.rsqrt(mean_square + EPSILON) * gain_row

def group_step(state_in, inputs):
    queries, key_rows, value_rows, decay_logarithm = inputs
    row_count = queries.shape[0]
    within = jnp.cumsum(decay_logarithm, axis=0)
    span_decay = within[-1]
    query_f = queries.astype(jnp.float32)
    key_f = key_rows.astype(jnp.float32)
    value_f = value_rows.astype(jnp.float32)
    scores = jnp.einsum('thd,shd->hts', query_f, key_f)
    lagged = within.T[:, :, None] - within.T[:, None, :]
    row_ids = jnp.arange(row_count, dtype=jnp.int32)
    causal = (row_ids[:, None] >= row_ids[None, :])[None]
    weights = jnp.where(causal, scores * jnp.exp(jnp.where(causal, lagged, 0.0)), 0.0).astype(jnp.bfloat16)
    inner_part = jnp.einsum('hts,shd->thd', weights.astype(jnp.float32), value_f)
    carried = jnp.exp(within)[:, :, None] * jnp.einsum('thd,hde->the', query_f, state_in, precision=lax.Precision.HIGHEST)
    weighted_keys = key_f * jnp.exp(span_decay[None, :] - within)[:, :, None]
    local_state = jnp.einsum('thd,the->hde', weighted_keys, value_f, precision=lax.Precision.HIGHEST)
    new_state = jnp.exp(span_decay)[:, None, None] * state_in + local_state
    return (new_state, inner_part + carried)

def by_device(values):
    return values.reshape((N_SEQ, TOK_DEV) + values.shape[1:])

def reference(image_patches, text_embed, image_start, image_forget, adapter, norm_gain, in_proj, decay_proj, head_decay_ceiling, out_gain, out_proj):
    unit_count = 2 * IMAGES
    image_rows = jnp.dot(image_patches.reshape(IMAGES * PATCH_COUNT, PIN), adapter, preferred_element_type=jnp.float32)
    image_embed = image_rows.astype(jnp.bfloat16).reshape(IMAGES, PATCH_COUNT, D)
    unit_of_image = (image_start // 2).astype(jnp.int32)
    unit_ids = jnp.arange(unit_count, dtype=jnp.int32)
    image_ids = jnp.arange(IMAGES, dtype=jnp.int32)
    image_hits = (unit_of_image[:, None] == unit_ids[None, :]).astype(jnp.int32)
    is_image = lax.optimization_barrier(jnp.sum(image_hits, axis=0)).astype(jnp.int32)
    image_here = lax.optimization_barrier(jnp.sum(image_hits * image_ids[:, None], axis=0)).astype(jnp.int32)
    is_text = (1 - is_image).astype(jnp.int32)
    text_here = (jnp.cumsum(is_text) - is_text).astype(jnp.int32)
    source = jnp.where(is_image == 1, image_here, IMAGES + text_here).astype(jnp.int32)
    pieces = jnp.concatenate([image_embed, text_embed.reshape(IMAGES, PATCH_COUNT, D)], axis=0)
    merged = jnp.take(pieces, source, axis=0).reshape(LENGTH, D)
    forget_element = jnp.where(is_image == 1, jnp.log1p(-jnp.take(image_forget, image_here)), 0.0)
    start_offsets = jnp.arange(LENGTH, dtype=jnp.int32) % PATCH_COUNT == 0
    surge_logarithm = jnp.where(start_offsets, jnp.repeat(forget_element, PATCH_COUNT), 0.0)
    normed = rms_scale(merged.astype(jnp.float32), norm_gain).astype(jnp.bfloat16)
    projected = jnp.dot(normed, in_proj.reshape(D, 4 * D), preferred_element_type=jnp.float32)
    projected = projected.astype(jnp.bfloat16).reshape(LENGTH, 4, H, HD)
    gate_preactivation = jnp.dot(normed, decay_proj, preferred_element_type=jnp.float32)
    decay_logarithm = -head_decay_ceiling[None, :] * jax.nn.sigmoid(gate_preactivation) + surge_logarithm[:, None]
    start_state = jnp.zeros((H, HD, HD), jnp.float32)
    last_state, attended = lax.scan(group_step, start_state, (by_device(projected[:, 0]), by_device(projected[:, 1]), by_device(projected[:, 2]), by_device(decay_logarithm)))
    attended = attended.reshape(LENGTH, H, HD)
    gated = rms_scale(attended, out_gain) * jax.nn.silu(projected[:, 3].astype(jnp.float32))
    gated = gated.astype(jnp.bfloat16).reshape(LENGTH, D)
    result = (merged.astype(jnp.float32) + jnp.dot(gated, out_proj, preferred_element_type=jnp.float32)).astype(jnp.bfloat16)
    out_units = result.reshape(unit_count, PATCH_COUNT, D)
    image_out = jnp.take(out_units, unit_of_image, axis=0)
    text_pick = ((is_text[None, :] == 1) & (text_here[None, :] == image_ids[:, None])).astype(jnp.int32)
    text_unit = lax.optimization_barrier(jnp.sum(text_pick * unit_ids[None, :], axis=1)).astype(jnp.int32)
    text_out = jnp.take(out_units, text_unit, axis=0).reshape(TEXT, D)
    return (image_out, text_out)
```

```python
import jax
import jax.numpy as jnp
from jax import lax
from jax.experimental import pallas as pl
from jax.experimental.pallas import tpu as pltpu
from jax.sharding import Mesh
from jax.sharding import PartitionSpec as P

SEQ = ("seq_0", "seq_1", "seq_2")
EPSILON = 1e-06
F32 = jnp.float32
BF16 = jnp.bfloat16


VMEM = pl.BlockSpec(memory_space=pltpu.VMEM)
SMEM = pl.BlockSpec(memory_space=pltpu.SMEM)


def shape_of(*dims, dtype=BF16):
    return jax.ShapeDtypeStruct(dims, dtype)


def columns_of(place, step, count, width):
    return pl.ds(pl.multiple_of(lax.rem(place + step, count) * width, width), width)


def adapter_kernel(
    place_ref, patches_ref, adapter_ref, own, next_a, next_b, far_a, far_b, last_a, last_b
):
    width = own.shape[1]
    half = next_a.shape[0]
    patches = patches_ref[0]
    for step, outs in ((2, (far_a, far_b)), (1, (next_a, next_b)), (3, (last_a, last_b)), (0, None)):
        block = jnp.dot(
            patches,
            adapter_ref[:, columns_of(place_ref[0], step, 4, width)],
            preferred_element_type=F32,
        )
        if outs is None:
            own[...] = block
        else:
            outs[0][...] = block[:half].astype(BF16)
            outs[1][...] = block[half:].astype(BF16)


def adapter_sums(place, patches, adapter):
    rows = patches.shape[1]
    width = adapter.shape[1] // 4
    half = shape_of(rows // 2, width)
    return pl.pallas_call(
        adapter_kernel,
        out_shape=(shape_of(rows, width, dtype=F32),) + (half,) * 6,
        in_specs=[SMEM, VMEM, VMEM],
        out_specs=(VMEM,) * 7,
        name="adapter_sums",
    )(place, patches, adapter)


def unit_kernel(
    image,
    place_ref,
    burst_ref,
    own_a,
    own_b,
    left_a,
    left_b,
    right_a,
    right_b,
    far_a,
    far_b,
    gain_ref,
    weight_ref,
    decay_ref,
    ceiling_ref,
    *rest,
):
    if image:
        other_state, other_span, query_out, gate_out, inner_out, state_out, normed, parts = rest
    else:
        query_out, gate_out, inner_out, state_out, span_out, normed, parts = rest
    part = pl.program_id(0)
    place = place_ref[0]
    half, width = own_a.shape
    rows = 2 * half
    head_width = 128
    head_count = width // head_width
    chunks = ((0, own_a, own_b), (3, left_a, left_b), (1, right_a, right_b), (2, far_a, far_b))

    @pl.when(part == 0)
    def _():
        for at, pair in ((0, [c[1] for c in chunks]), (half, [c[2] for c in chunks])):
            total = 0.0
            for ref in pair:
                value = ref[...].astype(F32)
                total += jnp.sum(value * value, axis=-1, keepdims=True)
            scale = lax.rsqrt(total / (4 * width) + EPSILON)
            for index, ref in enumerate(pair):
                gain = gain_ref[:, columns_of(place, chunks[index][0], 4, width)]
                value = ref[...].astype(F32) * scale * gain
                normed[pl.ds(at, half), pl.ds(index * width, width)] = value.astype(BF16)

    def product(ref):
        total = None
        for index, chunk in enumerate(chunks):
            term = jnp.dot(
                normed[:, index * width : (index + 1) * width],
                ref[columns_of(place, chunk[0], 4, width), :],
                preferred_element_type=F32,
            )
            total = term if total is None else total + term
        return total

    parts[part] = product(weight_ref).astype(BF16)

    @pl.when(part == 3)
    def _():
        row_ids = lax.broadcasted_iota(jnp.int32, (rows, rows), 0)
        column_ids = lax.broadcasted_iota(jnp.int32, (rows, rows), 1)
        causal = row_ids >= column_ids
        decay = -ceiling_ref[...] * jax.nn.sigmoid(product(decay_ref))
        if image:
            first = lax.broadcasted_iota(jnp.int32, decay.shape, 0) == 0
            decay += jnp.where(first, burst_ref[0], 0.0)
        within = jnp.dot(
            causal.astype(F32),
            decay,
            precision=lax.Precision.HIGHEST,
            preferred_element_type=F32,
        )
        within_row = within.T
        span = within[rows - 1 :, :]
        gate_out[...] = parts[3]
        for head in range(head_count):
            lanes = slice(head * head_width, (head + 1) * head_width)
            query = parts[0, :, lanes]
            key = parts[1, :, lanes]
            value = parts[2, :, lanes]
            column = within[:, head : head + 1]
            lagged = column - within_row[head : head + 1, :]
            scores = lax.dot_general(
                query, key, (((1,), (1,)), ((), ())), preferred_element_type=F32
            )
            weights = jnp.where(causal, scores * jnp.exp(jnp.minimum(lagged, 0.0)), 0.0)
            inner_out[:, lanes] = jnp.dot(
                weights.astype(BF16), value, preferred_element_type=F32
            )
            head_span = span[:, head : head + 1]
            weighted = (key.astype(F32) * jnp.exp(head_span - column)).astype(BF16)
            state = lax.dot_general(
                weighted, value, (((0,), (0,)), ((), ())), preferred_element_type=F32
            )
            state = state.astype(BF16).reshape(8, 16, head_width)
            query_out[:, lanes] = (query.astype(F32) * jnp.exp(column)).astype(BF16)
            targets = slice(head * 8, (head + 1) * 8)
            if image:
                state_out[targets, 16:32, :] = state
                ids = lax.broadcasted_iota(jnp.int32, (8, head_width), 0)
                tile = jnp.zeros((8, head_width), F32)
                spans = (other_span[:, head : head + 1], head_span)
                for kind in range(2):
                    upper = spans[kind].astype(BF16).astype(F32)
                    tile = jnp.where(ids == 2 * kind, upper, tile)
                    tile = jnp.where(ids == 2 * kind + 1, spans[kind] - upper, tile)
                state_out[targets, 32:40, :] = jnp.broadcast_to(
                    tile.astype(BF16)[None], (8, 8, head_width)
                )
            else:
                state_out[targets, :, :] = state
        if image:
            state_out[:, 0:16, :] = other_state[...]
        else:
            span_out[...] = span


def unit_call(image, place, burst, chunks, gain, weight, decay, ceiling, others=()):
    half, width = chunks[0].shape
    rows = 2 * half
    model_width = weight.shape[0]
    fixed = lambda *dims: pl.BlockSpec(dims, lambda p: (0,) * len(dims))
    outs = [shape_of(rows, width), shape_of(rows, width), shape_of(rows, width, dtype=F32)]
    outs += [shape_of(32, 40, 128)] if image else [shape_of(32, 16, 128), shape_of(1, 128, dtype=F32)]
    return pl.pallas_call(
        lambda *refs: unit_kernel(image, *refs),
        grid=(4,),
        out_shape=tuple(outs),
        in_specs=[SMEM, SMEM]
        + [fixed(half, width)] * 8
        + [
            fixed(1, model_width),
            pl.BlockSpec((model_width, width), lambda p: (0, p)),
            fixed(model_width, 128),
            fixed(1, 128),
        ]
        + [fixed(*o.shape) for o in others],
        out_specs=tuple(fixed(*o.shape) for o in outs),
        scratch_shapes=[pltpu.VMEM((rows, model_width), BF16), pltpu.VMEM((4, rows, width), BF16)],
        compiler_params=pltpu.CompilerParams(
            dimension_semantics=("arbitrary",), vmem_limit_bytes=40 << 20
        ),
        cost_estimate=pl.CostEstimate(
            flops=2 * rows * model_width * 4 * width,
            bytes_accessed=model_width * 4 * width * 2,
            transcendentals=0,
        ),
        name="image_unit" if image else "text_unit",
    )(place, burst, *chunks, gain, weight, decay, ceiling, *others)


def scan_kernel(order_ref, states, out, decay):
    for kind in range(2):
        spans = states[:, 32:40, :].astype(F32)
        span = spans[:, 2 * kind : 2 * kind + 1, :] + spans[:, 2 * kind + 1 : 2 * kind + 2, :]
        decay[:, kind] = jnp.broadcast_to(jnp.exp(span), (decay.shape[0], 16, 128))
    carry = jnp.zeros((16, 128), F32)
    for position in range(order_ref.shape[0]):
        unit = order_ref[position]
        source = lax.shift_right_logical(unit, 1)
        kind = lax.bitwise_and(unit, 1)
        rows = pl.ds(pl.multiple_of(kind * 16, 16), 16)
        out[source, rows, :] = carry.astype(BF16)
        carry = decay[source, kind] * carry + states[source, rows, :].astype(F32)


def scan_call(order, states):
    count = states.shape[0]
    return pl.pallas_call(
        scan_kernel,
        out_shape=shape_of(count, 32, 128),
        in_specs=[SMEM, VMEM],
        out_specs=VMEM,
        scratch_shapes=[pltpu.VMEM((count, 2, 16, 128), F32)],
        name="state_scan",
    )(order, states)


def output_kernel(
    place_ref, entering, out_gain, out_proj, query_t, gate_t, inner_t, query_i, gate_i, inner_i, *outs
):
    gated_refs = outs[8:]
    outs = outs[:8]
    rows, width = query_t.shape
    head_width = 128
    refs = ((query_t, gate_t, inner_t), (query_i, gate_i, inner_i))
    for kind, (query, gate, inner) in enumerate(refs):
        for head in range(width // head_width):
            lanes = slice(head * head_width, (head + 1) * head_width)
            state = entering[head * 8 : (head + 1) * 8, kind * 16 : (kind + 1) * 16, :]
            attended = inner[:, lanes] + jnp.dot(
                query[:, lanes], state.reshape(head_width, head_width), preferred_element_type=F32
            )
            scale = lax.rsqrt(jnp.mean(attended * attended, axis=-1, keepdims=True) + EPSILON)
            gates = gate[:, lanes].astype(F32)
            value = attended * scale * out_gain[:, lanes] * (gates * jax.nn.sigmoid(gates))
            gated_refs[kind][:, lanes] = value.astype(BF16)
    for slot, step in enumerate((2, 1, 3, 0)):
        weight = out_proj[:, columns_of(place_ref[0], step, 4, width)]
        for kind in range(2):
            block = jnp.dot(gated_refs[kind][...], weight, preferred_element_type=F32)
            ref = outs[2 * slot + kind]
            ref[...] = block.astype(ref.dtype)


def output_call(place, entering, out_gain, out_proj, text_parts, image_parts):
    rows, width = text_parts[0].shape
    block = shape_of(rows, width)
    own = shape_of(rows, width, dtype=F32)
    return pl.pallas_call(
        output_kernel,
        out_shape=(block,) * 6 + (own,) * 2,
        in_specs=[SMEM] + [VMEM] * 9,
        out_specs=(VMEM,) * 8,
        scratch_shapes=[pltpu.VMEM((rows, width), BF16)] * 2,
        compiler_params=pltpu.CompilerParams(vmem_limit_bytes=40 << 20),
        name="output_blocks",
    )(place, entering, out_gain, out_proj, *text_parts, *image_parts)


def moved(array, step):
    return lax.ppermute(array, "head", [(i, (i + step) % 4) for i in range(4)])


def gathered(first, second):
    left_a = moved(first, 1)
    right_b = moved(second, 3)
    left_b = moved(second, 1)
    right_a = moved(first, 3)
    far_a = moved(left_a, 1)
    far_b = moved(right_b, 3)
    return (first, second, left_a, left_b, right_a, right_b, far_a, far_b)


def added(one, two):
    return (one.astype(F32) + two.astype(F32)).astype(BF16)


def shards(
    image_patches,
    text_embed,
    image_start,
    image_forget,
    adapter,
    norm_gain,
    in_proj,
    decay_proj,
    head_decay_ceiling,
    out_gain,
    out_proj,
):
    my_index = lax.axis_index(SEQ)
    place = lax.axis_index("head").astype(jnp.int32).reshape(1)
    images = image_start.shape[0]
    rows = text_embed.shape[0]
    model_width = in_proj.shape[0]
    half = rows // 2

    unit_ids = jnp.arange(2 * images, dtype=jnp.int32)
    hits = (image_start[:, None] // 2 == unit_ids[None, :]).astype(jnp.int32)
    is_image = jnp.sum(hits, axis=0)
    image_here = jnp.sum(hits * jnp.arange(images, dtype=jnp.int32)[:, None], axis=0)
    earlier = (unit_ids[:, None] < unit_ids[None, :]).astype(jnp.int32)
    text_here = jnp.sum(earlier * (1 - is_image)[:, None], axis=0)
    order = jnp.where(is_image == 1, 2 * image_here + 1, 2 * text_here)
    mine = jnp.arange(images, dtype=jnp.int32) == my_index
    burst = jnp.log1p(-jnp.sum(jnp.where(mine, image_forget, 0.0))).reshape(1)

    pad = 128 - head_decay_ceiling.shape[0]
    decay = jnp.pad(decay_proj, ((0, 0), (0, pad)))
    ceiling = jnp.pad(head_decay_ceiling, (0, pad))[None]
    gain = norm_gain[None]
    weight = in_proj.reshape(model_width, -1)

    own, next_a, next_b, far_a, far_b, last_a, last_b = adapter_sums(place, image_patches, adapter)
    text_chunks = gathered(text_embed[:half], text_embed[half:])

    far_from_left = moved(far_a, 1)
    far_from_right = moved(far_b, 3)
    left_b = moved(next_b, 1)
    right_a = moved(last_a, 3)
    left_a = moved(added(next_a, far_from_left), 1)
    right_b = moved(added(last_b, far_from_right), 3)
    embed_a = (own[:half] + left_a.astype(F32) + right_a.astype(F32)).astype(BF16)
    embed_b = (own[half:] + left_b.astype(F32) + right_b.astype(F32)).astype(BF16)
    image_chunks = gathered(embed_a, embed_b)

    *text_parts, text_state, text_span = unit_call(
        False, place, burst, text_chunks, gain, weight, decay, ceiling
    )
    *image_parts, states = unit_call(
        True, place, burst, image_chunks, gain, weight, decay, ceiling, (text_state, text_span)
    )
    slices = lax.all_to_all(states, SEQ, 0, 0, tiled=True)
    entering = lax.all_to_all(scan_call(order, slices), SEQ, 0, 0, tiled=True)

    far_t, far_i, next_t, next_i, last_t, last_i, own_t, own_i = output_call(
        place, entering, out_gain.reshape(1, -1), out_proj, text_parts, image_parts
    )
    far_from_left = moved(far_t, 1)
    far_from_right = moved(far_i, 3)
    left_i = moved(next_i, 1)
    right_t = moved(last_t, 3)
    left_t = moved(added(next_t, far_from_left), 1)
    right_i = moved(added(last_i, far_from_right), 3)
    text_out = text_embed.astype(F32) + (own_t + left_t.astype(F32) + right_t.astype(F32))
    embed = jnp.concatenate([embed_a, embed_b])
    image_out = embed.astype(F32) + (own_i + left_i.astype(F32) + right_i.astype(F32))
    return (image_out.astype(BF16)[None], text_out.astype(BF16))


def solution(mesh):
    split = Mesh(
        mesh.devices.reshape(4, 4, 2, mesh.shape["head"]), ("seq_0", "seq_1", "seq_2", "head")
    )
    return jax.shard_map(
        shards,
        mesh=split,
        in_specs=(
            P(SEQ, None, "head"),
            P(SEQ, "head"),
            P(),
            P(),
            P("head", None),
            P(),
            P(None, None, "head"),
            P(None, "head"),
            P("head"),
            P("head", None),
            P("head", None),
        ),
        out_specs=(P(SEQ, None, "head"), P(SEQ, "head")),
        check_vma=False,
    )
```

```python
import jax
import jax.numpy as jnp
from jax import lax
from jax.experimental import pallas as pl
from jax.experimental.pallas import tpu as pltpu
from jax.sharding import Mesh
from jax.sharding import PartitionSpec as P

SEQ = ("seq_0", "seq_1", "seq_2")
EPSILON = 1e-06
F32 = jnp.float32
BF16 = jnp.bfloat16
HEAD_WIDTH = 128


VMEM = pl.BlockSpec(memory_space=pltpu.VMEM)
SMEM = pl.BlockSpec(memory_space=pltpu.SMEM)


def shape_of(*dims, dtype=BF16):
    return jax.ShapeDtypeStruct(dims, dtype)


def hbm_of(*dims, dtype=BF16):
    return pltpu.HBM(dims, dtype)


def in_hbm(*arrays):
    return [pltpu.with_memory_space_constraint(a, pltpu.HBM) for a in arrays]


def limit(mebibytes, *semantics):
    return pltpu.CompilerParams(
        dimension_semantics=semantics or None, vmem_limit_bytes=mebibytes << 20
    )


def fixed(*dims):
    return pl.BlockSpec(dims, lambda *_: (0,) * len(dims))


def columns_of(place, step, count, width):
    return pl.ds(pl.multiple_of(lax.rem(place + step, count) * width, width), width)


def adapter_kernel(place_ref, patches_ref, adapter_ref, to_next, to_last, near_next, near_last, own):
    step = pl.program_id(0)
    half = near_next.shape[0]
    block = lax.dot_general(
        patches_ref[0], adapter_ref[...], (((0,), (0,)), ((), ())), preferred_element_type=F32
    )
    small = block.astype(BF16)

    @pl.when(step == 0)
    def _():
        to_next[:half] = small[:half]
        to_last[half:] = small[half:]

    @pl.when(step == 1)
    def _():
        near_next[...] = small[:half]
        to_next[half:] = small[half:]

    @pl.when(step == 2)
    def _():
        to_last[:half] = small[:half]
        near_last[...] = small[half:]

    @pl.when(step == 3)
    def _():
        own[...] = block


def adapter_sums(place, patches, adapter):
    depth, rows = patches.shape[1:]
    width = adapter.shape[1] // 4
    outs = (
        shape_of(rows, width),
        shape_of(rows, width),
        shape_of(rows // 2, width),
        shape_of(rows // 2, width),
        shape_of(rows, width, dtype=F32),
    )

    def block_of(step, place_ref):
        ahead = jnp.where(step == 0, 2, jnp.where(step == 2, 3, jnp.where(step == 1, 1, 0)))
        return (0, lax.rem(place_ref[0] + ahead, 4))

    return pl.pallas_call(
        adapter_kernel,
        out_shape=outs,
        grid_spec=pltpu.PrefetchScalarGridSpec(
            num_scalar_prefetch=1,
            grid=(4,),
            in_specs=[fixed(*patches.shape), pl.BlockSpec((depth, width), block_of)],
            out_specs=tuple(fixed(*o.shape) for o in outs),
        ),
        compiler_params=limit(8, "arbitrary"),
        name="adapter_sums",
    )(place, patches, adapter)


def pass_kernel(from_left, from_right, near_next, near_last, next_out, last_out):
    half = near_next.shape[0]
    next_out[...] = (near_next[...].astype(F32) + from_left[:half].astype(F32)).astype(BF16)
    last_out[...] = (near_last[...].astype(F32) + from_right[half:].astype(F32)).astype(BF16)


def pass_call(*arrays):
    half = shape_of(*arrays[2].shape)
    return pl.pallas_call(
        pass_kernel,
        out_shape=(half, half),
        in_specs=[VMEM] * 4,
        out_specs=(VMEM, VMEM),
        compiler_params=limit(4),
        name="pass_on",
    )(*arrays)


def embed_kernel(own, from_left, from_right, left, right, out):
    half = left.shape[0]
    first = own[:half] + left[...].astype(F32) + from_right[:half].astype(F32)
    second = own[half:] + from_left[half:].astype(F32) + right[...].astype(F32)
    out[:half] = first.astype(BF16)
    out[half:] = second.astype(BF16)


def embed_call(own, *arrays):
    return pl.pallas_call(
        embed_kernel,
        out_shape=shape_of(*own.shape),
        in_specs=[VMEM] * 5,
        out_specs=VMEM,
        compiler_params=limit(4),
        name="embed",
    )(own, *arrays)


def normalize(place, chunks, gain_ref, normed):
    own, left, right, far_a, far_b = chunks
    rows, width = own.shape
    half = rows // 2
    for at, far in ((0, far_a), (half, far_b)):
        span = slice(at, at + half)
        values = ((0, own[span]), (3, left[span]), (1, right[span]), (2, far[...]))
        total = 0.0
        for _, value in values:
            value = value.astype(F32)
            total += jnp.sum(value * value, axis=-1, keepdims=True)
        scale = lax.rsqrt(total / (4 * width) + EPSILON)
        for step, value in values:
            columns = columns_of(place, step, 4, width)
            normed[span, columns] = (value.astype(F32) * scale * gain_ref[:, columns]).astype(BF16)


def product(normed, weight):
    return jnp.dot(normed[...], weight[...], preferred_element_type=F32)


def decay_sums(normed, decay_ref, columns, lanes):
    rows = normed.shape[0]
    values = normed[...]
    decay = decay_ref[...]
    by_row = lax.dot_general(values, decay, (((1,), (1,)), ((), ())), preferred_element_type=F32)
    by_lane = lax.dot_general(decay, values, (((1,), (1,)), ((), ())), preferred_element_type=F32)
    row_ids = lax.broadcasted_iota(jnp.int32, (rows, rows), 0)
    column_ids = lax.broadcasted_iota(jnp.int32, (rows, rows), 1)
    exact = dict(precision=lax.Precision.HIGHEST, preferred_element_type=F32)
    columns[...] = jnp.dot((row_ids >= column_ids).astype(F32), jax.nn.sigmoid(by_row), **exact)
    lanes[...] = jnp.dot(jax.nn.sigmoid(by_lane), (row_ids <= column_ids).astype(F32), **exact)


def chunk_state(head, key, value, columns, ceiling, burst):
    rows = columns.shape[0]
    lanes = slice(head * HEAD_WIDTH, (head + 1) * HEAD_WIDTH)
    column = columns[:, head : head + 1]
    last = columns[rows - 1 :, head : head + 1]
    weighted = key[:, lanes].astype(F32) * jnp.exp(ceiling * (column - last))
    state = lax.dot_general(
        weighted.astype(BF16), value[:, lanes], (((0,), (0,)), ((), ())), preferred_element_type=F32
    )
    return state.astype(BF16).reshape(8, 16, HEAD_WIDTH), burst - ceiling * last


def attend(head, query, key, value, columns, lanes_ref, ceiling, burst, query_out, inner_out):
    rows = columns.shape[0]
    lanes = slice(head * HEAD_WIDTH, (head + 1) * HEAD_WIDTH)
    column = columns[:, head : head + 1]
    lagged = ceiling * (lanes_ref[head : head + 1, :] - column)
    row_ids = lax.broadcasted_iota(jnp.int32, (rows, rows), 0)
    column_ids = lax.broadcasted_iota(jnp.int32, (rows, rows), 1)
    scores = lax.dot_general(
        query[:, lanes], key[:, lanes], (((1,), (1,)), ((), ())), preferred_element_type=F32
    )
    weights = jnp.where(row_ids >= column_ids, scores * jnp.exp(jnp.minimum(lagged, 0.0)), 0.0)
    inner_out[:, lanes] = jnp.dot(weights.astype(BF16), value[:, lanes], preferred_element_type=F32)
    entry = jnp.exp(burst - ceiling * column)
    query_out[:, lanes] = (query[:, lanes].astype(F32) * entry).astype(BF16)


def text_kernel(
    place_ref,
    ceiling_ref,
    own,
    left,
    right,
    far_a,
    far_b,
    gain_ref,
    weight,
    decay_ref,
    query_out,
    gate_out,
    inner_out,
    state_out,
    span_out,
    normed,
    parts,
    columns,
    lanes,
):
    part = pl.program_id(0)

    @pl.when(part == 0)
    def _():
        normalize(place_ref[0], (own, left, right, far_a, far_b), gain_ref, normed)

    parts[part] = product(normed, weight).astype(BF16)

    @pl.when(part == 3)
    def _():
        decay_sums(normed, decay_ref, columns, lanes)
        gate_out[...] = parts[3]
        for head in range(4):
            ceiling = ceiling_ref[head]
            state, span = chunk_state(head, parts.at[1], parts.at[2], columns, ceiling, 0.0)
            state_out[head * 8 : (head + 1) * 8] = state
            span_out[head : head + 1] = jnp.broadcast_to(span, (1, HEAD_WIDTH))
            attend(
                head,
                parts.at[0],
                parts.at[1],
                parts.at[2],
                columns,
                lanes,
                ceiling,
                0.0,
                query_out,
                inner_out,
            )


def image_state_kernel(
    place_ref,
    ceiling_ref,
    forget_ref,
    own,
    left,
    right,
    far_a,
    far_b,
    gain_ref,
    weight,
    decay_ref,
    other_state,
    other_span,
    normed,
    key_value,
    columns,
    lanes,
    state_out,
):
    part = pl.program_id(0)

    @pl.when(part == 0)
    def _():
        normalize(place_ref[0], (own, left, right, far_a, far_b), gain_ref, normed)
        state_out[:, 0:16, :] = other_state[...]

    key_value[part] = product(normed, weight).astype(BF16)

    @pl.when(part == 1)
    def _():
        decay_sums(normed, decay_ref, columns, lanes)
        burst = jnp.log1p(jnp.full((1, 1), -forget_ref[place_ref[1]], F32))
        ids = lax.broadcasted_iota(jnp.int32, (8, HEAD_WIDTH), 0)
        for head in range(4):
            state, span = chunk_state(
                head, key_value.at[0], key_value.at[1], columns, ceiling_ref[head], burst
            )
            targets = slice(head * 8, (head + 1) * 8)
            state_out[targets, 16:32, :] = state
            tile = jnp.zeros((8, HEAD_WIDTH), F32)
            for kind, value in enumerate((other_span[head : head + 1, 0:1], span)):
                upper = value.astype(BF16).astype(F32)
                tile = jnp.where(ids == 2 * kind, upper, tile)
                tile = jnp.where(ids == 2 * kind + 1, value - upper, tile)
            state_out[targets, 32:40, :] = jnp.broadcast_to(
                tile.astype(BF16)[None], (8, 8, HEAD_WIDTH)
            )


def image_attend_kernel(
    place_ref,
    ceiling_ref,
    forget_ref,
    normed,
    key_value,
    columns,
    lanes,
    weight,
    query_out,
    gate_out,
    inner_out,
    query,
):
    part = pl.program_id(0)
    block = product(normed, weight).astype(BF16)

    @pl.when(part == 0)
    def _():
        query[...] = block

    @pl.when(part == 1)
    def _():
        gate_out[...] = block
        burst = jnp.log1p(jnp.full((1, 1), -forget_ref[place_ref[1]], F32))
        for head in range(4):
            attend(
                head,
                query,
                key_value.at[0],
                key_value.at[1],
                columns,
                lanes,
                ceiling_ref[head],
                burst,
                query_out,
                inner_out,
            )


def cost_of(rows, depth, width):
    return pl.CostEstimate(
        flops=2 * rows * depth * width, bytes_accessed=depth * width * 2, transcendentals=0
    )


def weight_spec(weight, column):
    return [pl.BlockSpec((weight.shape[0], weight.shape[1] // 4), lambda p: (0, column(p)))]


def relay_kernel(source, out):
    width = source.shape[2]
    moved_rows = jnp.swapaxes(source[...], 0, 1)
    for part in range(4):
        out[:, part * width : (part + 1) * width] = moved_rows[part]


def relay_call(in_proj):
    depth, parts, width = in_proj.shape
    rows = 256
    return pl.pallas_call(
        relay_kernel,
        grid=(depth // rows,),
        out_shape=hbm_of(depth, parts * width),
        in_specs=[pl.BlockSpec((rows, parts, width), lambda b: (b, 0, 0))],
        out_specs=pl.BlockSpec((rows, parts * width), lambda b: (b, 0)),
        compiler_params=limit(8, "arbitrary"),
        name="relay",
    )(*in_hbm(in_proj))


def text_call(place, ceiling, chunks, gain, weights, decay):
    rows, width = chunks[0].shape
    depth = gain.shape[1]
    outs = (
        hbm_of(rows, width),
        hbm_of(rows, width),
        hbm_of(rows, width, dtype=F32),
        shape_of(32, 16, HEAD_WIDTH),
        shape_of(4, HEAD_WIDTH, dtype=F32),
    )
    return pl.pallas_call(
        text_kernel,
        grid=(4,),
        out_shape=outs,
        in_specs=[SMEM, SMEM]
        + [fixed(*c.shape) for c in chunks]
        + [fixed(1, depth)]
        + weight_spec(weights, lambda p: p)
        + [fixed(*decay.shape)],
        out_specs=tuple(fixed(*o.shape) for o in outs),
        scratch_shapes=[
            pltpu.VMEM((rows, depth), BF16),
            pltpu.VMEM((4, rows, width), BF16),
            pltpu.VMEM((rows, 4), F32),
            pltpu.VMEM((4, rows), F32),
        ],
        compiler_params=limit(20, "arbitrary"),
        cost_estimate=cost_of(rows, depth, 4 * width),
        name="text_unit",
    )(place, ceiling, *chunks, gain, *in_hbm(weights), decay)


def image_state_call(place, ceiling, forget, chunks, gain, weights, decay, state, span):
    rows, width = chunks[0].shape
    depth = gain.shape[1]
    outs = (
        hbm_of(rows, depth),
        hbm_of(2, rows, width),
        shape_of(rows, 4, dtype=F32),
        shape_of(4, rows, dtype=F32),
        shape_of(32, 40, HEAD_WIDTH),
    )
    return pl.pallas_call(
        image_state_kernel,
        grid=(2,),
        out_shape=outs,
        in_specs=[SMEM] * 3
        + [fixed(*c.shape) for c in chunks]
        + [fixed(1, depth)]
        + weight_spec(weights, lambda p: p + 1)
        + [fixed(*decay.shape), fixed(*state.shape), fixed(*span.shape)],
        out_specs=tuple(fixed(*o.shape) for o in outs),
        compiler_params=limit(20, "arbitrary"),
        cost_estimate=cost_of(rows, depth, 2 * width),
        name="image_state",
    )(place, ceiling, forget, *chunks, gain, *in_hbm(weights), decay, state, span)


def image_attend_call(place, ceiling, forget, weights, normed, key_value, columns, lanes):
    rows, depth = normed.shape
    width = key_value.shape[2]
    outs = (
        hbm_of(rows, width),
        hbm_of(rows, width),
        hbm_of(rows, width, dtype=F32),
    )
    held = (*in_hbm(normed, key_value), columns, lanes)
    return pl.pallas_call(
        image_attend_kernel,
        grid=(2,),
        out_shape=outs,
        in_specs=[SMEM] * 3
        + [fixed(*h.shape) for h in held]
        + weight_spec(weights, lambda p: 3 * p),
        out_specs=tuple(fixed(*o.shape) for o in outs),
        scratch_shapes=[pltpu.VMEM((rows, width), BF16)],
        compiler_params=limit(20, "arbitrary"),
        cost_estimate=cost_of(rows, depth, 2 * width),
        name="image_attend",
    )(place, ceiling, forget, *held, *in_hbm(weights))


def scan_kernel(start_ref, states, out, decay, image_at):
    count = start_ref.shape[0]
    for kind in range(2):
        spans = states[:, 32:40, :].astype(F32)
        span = spans[:, 2 * kind : 2 * kind + 1, :] + spans[:, 2 * kind + 1 : 2 * kind + 2, :]
        decay[:, kind] = jnp.broadcast_to(jnp.exp(span), (count, 16, HEAD_WIDTH))
    for position in range(2 * count):
        image_at[position] = -1
    for image in range(count):
        image_at[lax.shift_right_logical(start_ref[image], 1)] = image
    carry = jnp.zeros((16, HEAD_WIDTH), F32)
    texts = jnp.int32(0)
    for position in range(2 * count):
        found = image_at[position]
        kind = (found >= 0).astype(jnp.int32)
        source = jnp.where(found >= 0, found, jnp.minimum(texts, count - 1))
        texts += 1 - kind
        rows = pl.ds(pl.multiple_of(kind * 16, 16), 16)
        out[source, rows, :] = carry.astype(BF16)
        carry = decay[source, kind] * carry + states[source, rows, :].astype(F32)


def scan_call(starts, states):
    count = states.shape[0]
    return pl.pallas_call(
        scan_kernel,
        out_shape=shape_of(count, 32, HEAD_WIDTH),
        in_specs=[SMEM, VMEM],
        out_specs=VMEM,
        scratch_shapes=[
            pltpu.VMEM((count, 2, 16, HEAD_WIDTH), F32),
            pltpu.SMEM((2 * count,), jnp.int32),
        ],
        compiler_params=limit(6),
        name="state_scan",
    )(starts, states)


def output_kernel(
    place_ref,
    entering,
    out_gain,
    out_proj,
    query_t,
    gate_t,
    inner_t,
    query_i,
    gate_i,
    inner_i,
    *outs,
):
    gated_refs = outs[8:]
    outs = outs[:8]
    _, width = query_t.shape
    refs = ((query_t, gate_t, inner_t), (query_i, gate_i, inner_i))
    for kind, (query, gate, inner) in enumerate(refs):
        for head in range(width // HEAD_WIDTH):
            lanes = slice(head * HEAD_WIDTH, (head + 1) * HEAD_WIDTH)
            state = entering[head * 8 : (head + 1) * 8, kind * 16 : (kind + 1) * 16, :]
            attended = inner[:, lanes] + jnp.dot(
                query[:, lanes], state.reshape(HEAD_WIDTH, HEAD_WIDTH), preferred_element_type=F32
            )
            scale = lax.rsqrt(jnp.mean(attended * attended, axis=-1, keepdims=True) + EPSILON)
            gates = gate[:, lanes].astype(F32)
            value = attended * scale * out_gain[head : head + 1, :] * (gates * jax.nn.sigmoid(gates))
            gated_refs[kind][:, lanes] = value.astype(BF16)
    for slot, step in enumerate((2, 1, 3, 0)):
        weight = out_proj[:, columns_of(place_ref[0], step, 4, width)]
        for kind in range(2):
            block = jnp.dot(gated_refs[kind][...], weight, preferred_element_type=F32)
            ref = outs[2 * slot + kind]
            ref[...] = block.astype(ref.dtype)


def output_call(place, entering, out_gain, out_proj, text_parts, image_parts):
    rows, width = text_parts[0].shape
    outs = (shape_of(rows, width),) * 6 + (shape_of(rows, width, dtype=F32),) * 2
    arrays = (entering, out_gain, out_proj, *in_hbm(*text_parts, *image_parts))
    return pl.pallas_call(
        output_kernel,
        grid=(1,),
        out_shape=outs,
        in_specs=[SMEM] + [fixed(*a.shape) for a in arrays],
        out_specs=tuple(fixed(*o.shape) for o in outs),
        scratch_shapes=[pltpu.VMEM((rows, width), BF16)] * 2,
        compiler_params=limit(20, "arbitrary"),
        name="output_blocks",
    )(place, *arrays)


def moved(array, step):
    return lax.ppermute(array, "head", [(i, (i + step) % 4) for i in range(4)])


def gathered(rows):
    half = rows.shape[0] // 2
    left = moved(rows, 1)
    right = moved(rows, 3)
    far_a = moved(left[:half], 1)
    far_b = moved(right[half:], 3)
    return (rows, left, right, far_a, far_b)


def added(one, two):
    return (one.astype(F32) + two.astype(F32)).astype(BF16)


def steps(
    image_patches,
    text_embed,
    image_start,
    image_forget,
    adapter,
    norm_gain,
    in_proj,
    decay_proj,
    head_decay_ceiling,
    out_gain,
    out_proj,
):
    place = jnp.stack([lax.axis_index("head"), lax.axis_index(SEQ)]).astype(jnp.int32)
    decay = decay_proj.T
    gain = norm_gain[None]
    ceiling = head_decay_ceiling

    text_chunks = gathered(text_embed)
    to_next, to_last, near_next, near_last, own = adapter_sums(
        place, image_patches.transpose(0, 2, 1), adapter
    )
    weights = relay_call(in_proj)
    from_left = moved(to_next, 1)
    from_right = moved(to_last, 3)
    next_sum, last_sum = pass_call(from_left, from_right, near_next, near_last)
    left = moved(next_sum, 1)
    right = moved(last_sum, 3)
    embed = embed_call(own, from_left, from_right, left, right)
    image_chunks = gathered(embed)

    *text_parts, text_state, text_span = text_call(
        place, ceiling, text_chunks, gain, weights, decay
    )
    *held, states = image_state_call(
        place, ceiling, image_forget, image_chunks, gain, weights, decay, text_state, text_span
    )
    slices = lax.all_to_all(states, SEQ, 0, 0, tiled=True)
    image_parts = image_attend_call(place, ceiling, image_forget, weights, *held)
    entering = lax.all_to_all(scan_call(image_start, slices), SEQ, 0, 0, tiled=True)

    far_t, far_i, next_t, next_i, last_t, last_i, own_t, own_i = output_call(
        place, entering, out_gain, out_proj, text_parts, image_parts
    )
    far_from_left = moved(far_t, 1)
    far_from_right = moved(far_i, 3)
    left_i = moved(next_i, 1)
    right_t = moved(last_t, 3)
    left_t = moved(added(next_t, far_from_left), 1)
    right_i = moved(added(last_i, far_from_right), 3)
    text_out = text_embed.astype(F32) + (own_t + left_t.astype(F32) + right_t.astype(F32))
    image_out = embed.astype(F32) + (own_i + left_i.astype(F32) + right_i.astype(F32))
    return (image_out.astype(BF16)[None], text_out.astype(BF16))


def solution(mesh):
    split = Mesh(
        mesh.devices.reshape(4, 4, 2, mesh.shape["head"]), ("seq_0", "seq_1", "seq_2", "head")
    )
    return jax.shard_map(
        steps,
        mesh=split,
        in_specs=(
            P(SEQ, None, "head"),
            P(SEQ, "head"),
            P(),
            P(),
            P("head", None),
            P(),
            P(None, None, "head"),
            P(None, "head"),
            P("head"),
            P("head", None),
            P("head", None),
        ),
        out_specs=(P(SEQ, None, "head"), P(SEQ, "head")),
        check_vma=False,
    )
```

```python
import jax
import jax.numpy as jnp
from jax import lax
from jax.experimental import pallas as pl
from jax.experimental.pallas import tpu as pltpu
from jax.sharding import Mesh
from jax.sharding import PartitionSpec as P

SEQ = ("seq_0", "seq_1", "seq_2")
EPSILON = 1e-06
F32 = jnp.float32
BF16 = jnp.bfloat16
HEAD_WIDTH = 128


VMEM = pl.BlockSpec(memory_space=pltpu.VMEM)
SMEM = pl.BlockSpec(memory_space=pltpu.SMEM)
HBM = pl.BlockSpec(memory_space=pltpu.HBM)


def shape_of(*dims, dtype=BF16):
    return jax.ShapeDtypeStruct(dims, dtype)


def hbm_of(*dims, dtype=BF16):
    return pltpu.HBM(dims, dtype)


def in_hbm(*arrays):
    return [pltpu.with_memory_space_constraint(a, pltpu.HBM) for a in arrays]


def limit(mebibytes, *semantics):
    return pltpu.CompilerParams(
        dimension_semantics=semantics or None, vmem_limit_bytes=mebibytes << 20
    )


def fixed(*dims):
    return pl.BlockSpec(dims, lambda *_: (0,) * len(dims))


def columns_of(place, step, count, width):
    return pl.ds(pl.multiple_of(lax.rem(place + step, count) * width, width), width)


def adapter_kernel(place_ref, patches_ref, adapter_ref, to_next, to_last, near_next, near_last, own):
    step = pl.program_id(0)
    half = near_next.shape[0]
    block = lax.dot_general(
        patches_ref[0], adapter_ref[...], (((0,), (0,)), ((), ())), preferred_element_type=F32
    )
    small = block.astype(BF16)

    @pl.when(step == 0)
    def _():
        to_next[:half] = small[:half]
        to_last[half:] = small[half:]

    @pl.when(step == 1)
    def _():
        near_next[...] = small[:half]
        to_next[half:] = small[half:]

    @pl.when(step == 2)
    def _():
        to_last[:half] = small[:half]
        near_last[...] = small[half:]

    @pl.when(step == 3)
    def _():
        own[...] = block


def adapter_sums(place, patches, adapter):
    depth, rows = patches.shape[1:]
    width = adapter.shape[1] // 4
    outs = (
        shape_of(rows, width),
        shape_of(rows, width),
        shape_of(rows // 2, width),
        shape_of(rows // 2, width),
        shape_of(rows, width, dtype=F32),
    )

    def block_of(step, place_ref):
        ahead = jnp.where(step == 0, 2, jnp.where(step == 2, 3, jnp.where(step == 1, 1, 0)))
        return (0, lax.rem(place_ref[0] + ahead, 4))

    return pl.pallas_call(
        adapter_kernel,
        out_shape=outs,
        grid_spec=pltpu.PrefetchScalarGridSpec(
            num_scalar_prefetch=1,
            grid=(4,),
            in_specs=[fixed(*patches.shape), pl.BlockSpec((depth, width), block_of)],
            out_specs=tuple(fixed(*o.shape) for o in outs),
        ),
        compiler_params=limit(8, "arbitrary"),
        name="adapter_sums",
    )(place, *in_hbm(patches, adapter))


def pass_kernel(from_left, from_right, near_next, near_last, next_out, last_out):
    half = near_next.shape[0]
    next_out[...] = (near_next[...].astype(F32) + from_left[:half].astype(F32)).astype(BF16)
    last_out[...] = (near_last[...].astype(F32) + from_right[half:].astype(F32)).astype(BF16)


def pass_call(*arrays):
    half = shape_of(*arrays[2].shape)
    return pl.pallas_call(
        pass_kernel,
        out_shape=(half, half),
        in_specs=[VMEM] * 4,
        out_specs=(VMEM, VMEM),
        compiler_params=limit(4),
        name="pass_on",
    )(*arrays)


def embed_kernel(own, from_left, from_right, left, right, out):
    half = left.shape[0]
    first = own[:half] + left[...].astype(F32) + from_right[:half].astype(F32)
    second = own[half:] + from_left[half:].astype(F32) + right[...].astype(F32)
    out[:half] = first.astype(BF16)
    out[half:] = second.astype(BF16)


def embed_call(own, *arrays):
    return pl.pallas_call(
        embed_kernel,
        out_shape=shape_of(*own.shape),
        in_specs=[VMEM] * 5,
        out_specs=VMEM,
        compiler_params=limit(4),
        name="embed",
    )(own, *arrays)


def normalize(place, chunks, gain_ref, normed):
    own, left, right, far_a, far_b = chunks
    rows, width = own.shape
    half = rows // 2
    for at, far in ((0, far_a), (half, far_b)):
        span = slice(at, at + half)
        values = ((0, own[span]), (3, left[span]), (1, right[span]), (2, far[...]))
        total = 0.0
        for _, value in values:
            value = value.astype(F32)
            total += jnp.sum(value * value, axis=-1, keepdims=True)
        scale = lax.rsqrt(total / (4 * width) + EPSILON)
        for step, value in values:
            columns = columns_of(place, step, 4, width)
            normed[span, columns] = (value.astype(F32) * scale * gain_ref[:, columns]).astype(BF16)


def product(normed, weight):
    return jnp.dot(normed[...], weight, preferred_element_type=F32)


def decay_sums(normed, decay_ref, columns, lanes):
    rows = normed.shape[0]
    decay = decay_ref[...].astype(F32)
    decay = jnp.concatenate([decay] * 4, axis=0).astype(BF16)
    decay = jnp.concatenate([decay, jnp.zeros((HEAD_WIDTH - 16, decay.shape[1]), BF16)], axis=0)
    gates = jax.nn.sigmoid(
        lax.dot_general(normed[...], decay, (((1,), (1,)), ((), ())), preferred_element_type=F32)
    )
    ids = lax.broadcasted_iota(jnp.int32, gates.shape, 1)
    upper = gates.astype(BF16).astype(F32)
    middle = (gates - upper).astype(BF16).astype(F32)
    terms = jnp.where(ids < 4, upper, jnp.where(ids < 8, middle, gates - upper - middle))
    row_ids = lax.broadcasted_iota(jnp.int32, (rows, rows), 0)
    column_ids = lax.broadcasted_iota(jnp.int32, (rows, rows), 1)
    sums = jnp.dot(
        (row_ids >= column_ids).astype(BF16), terms.astype(BF16), preferred_element_type=F32
    )
    columns[...] = sums[:, 0:4] + sums[:, 4:8] + sums[:, 8:12]
    by_row = sums.T
    lanes[...] = by_row[0:4] + by_row[4:8] + by_row[8:12]


def silu_of(gates):
    gates = gates.astype(BF16).astype(F32)
    return (gates * jax.nn.sigmoid(gates)).astype(BF16)


def chunk_state(head, key, value, columns, ceiling, burst):
    rows = columns.shape[0]
    lanes = slice(head * HEAD_WIDTH, (head + 1) * HEAD_WIDTH)
    column = columns[:, head : head + 1]
    last = columns[rows - 1 :, head : head + 1]
    weighted = key[:, lanes].astype(F32) * jnp.exp(ceiling * (column - last))
    state = lax.dot_general(
        weighted.astype(BF16), value[:, lanes], (((0,), (0,)), ((), ())), preferred_element_type=F32
    )
    return state.astype(BF16).reshape(8, 16, HEAD_WIDTH), burst - ceiling * last


def attend(head, query, key, value, columns, lanes_ref, ceiling, burst, query_out, inner_out):
    rows = columns.shape[0]
    lanes = slice(head * HEAD_WIDTH, (head + 1) * HEAD_WIDTH)
    column = columns[:, head : head + 1]
    lagged = ceiling * (lanes_ref[head : head + 1, :] - column)
    row_ids = lax.broadcasted_iota(jnp.int32, (rows, rows), 0)
    column_ids = lax.broadcasted_iota(jnp.int32, (rows, rows), 1)
    scores = lax.dot_general(
        query[:, lanes], key[:, lanes], (((1,), (1,)), ((), ())), preferred_element_type=F32
    )
    weights = jnp.where(row_ids >= column_ids, scores * jnp.exp(jnp.minimum(lagged, 0.0)), 0.0)
    inner_out[:, lanes] = jnp.dot(weights.astype(BF16), value[:, lanes], preferred_element_type=F32)
    entry = jnp.exp(burst - ceiling * column)
    query_out[:, lanes] = (query[:, lanes].astype(F32) * entry).astype(BF16)


def text_kernel(
    place_ref,
    ceiling_ref,
    own,
    left,
    right,
    far_a,
    far_b,
    gain_ref,
    weight,
    decay_ref,
    query_out,
    gate_out,
    inner_out,
    state_out,
    span_out,
    normed,
    parts,
    columns,
    lanes,
):
    normalize(place_ref[0], (own, left, right, far_a, far_b), gain_ref, normed)
    decay_sums(normed, decay_ref, columns, lanes)
    for part in range(3):
        parts[part] = product(normed, weight[part]).astype(BF16)
    gate_out[...] = silu_of(product(normed, weight[3]))
    for head in range(4):
        ceiling = ceiling_ref[head]
        state, span = chunk_state(head, parts.at[1], parts.at[2], columns, ceiling, 0.0)
        state_out[head * 8 : (head + 1) * 8] = state
        span_out[head : head + 1] = jnp.broadcast_to(span, (1, HEAD_WIDTH))
        attend(
            head,
            parts.at[0],
            parts.at[1],
            parts.at[2],
            columns,
            lanes,
            ceiling,
            0.0,
            query_out,
            inner_out,
        )


def image_state_kernel(
    place_ref,
    ceiling_ref,
    forget_ref,
    own,
    left,
    right,
    far_a,
    far_b,
    gain_ref,
    weight,
    decay_ref,
    other_state,
    other_span,
    normed_out,
    key_value_out,
    columns,
    lanes,
    state_out,
    normed,
    key_value,
    sems,
):
    normalize(place_ref[0], (own, left, right, far_a, far_b), gain_ref, normed)
    key_value[0] = product(normed, weight[1]).astype(BF16)
    normed_copy = pltpu.make_async_copy(normed, normed_out, sems.at[0])
    normed_copy.start()
    key_value[1] = product(normed, weight[2]).astype(BF16)
    decay_sums(normed, decay_ref, columns, lanes)
    key_value_copy = pltpu.make_async_copy(key_value, key_value_out, sems.at[1])
    key_value_copy.start()
    state_out[:, 0:16, :] = other_state[...]
    burst = jnp.log1p(jnp.full((1, 1), -forget_ref[place_ref[1]], F32))
    ids = lax.broadcasted_iota(jnp.int32, (8, HEAD_WIDTH), 0)
    for head in range(4):
        state, span = chunk_state(
            head, key_value.at[0], key_value.at[1], columns, ceiling_ref[head], burst
        )
        targets = slice(head * 8, (head + 1) * 8)
        state_out[targets, 16:32, :] = state
        tile = jnp.zeros((8, HEAD_WIDTH), F32)
        for kind, value in enumerate((other_span[head : head + 1, 0:1], span)):
            upper = value.astype(BF16).astype(F32)
            tile = jnp.where(ids == 2 * kind, upper, tile)
            tile = jnp.where(ids == 2 * kind + 1, value - upper, tile)
        state_out[targets, 32:40, :] = jnp.broadcast_to(
            tile.astype(BF16)[None], (8, 8, HEAD_WIDTH)
        )
    normed_copy.wait()
    key_value_copy.wait()


def image_attend_kernel(
    place_ref,
    ceiling_ref,
    forget_ref,
    normed,
    key_value,
    columns,
    lanes,
    weight,
    query_out,
    gate_out,
    inner_out,
    query,
):
    part = pl.program_id(0)
    block = product(normed, weight[0])

    @pl.when(part == 0)
    def _():
        query[...] = block.astype(BF16)

    @pl.when(part == 1)
    def _():
        gate_out[...] = silu_of(block)
        burst = jnp.log1p(jnp.full((1, 1), -forget_ref[place_ref[1]], F32))
        for head in range(4):
            attend(
                head,
                query,
                key_value.at[0],
                key_value.at[1],
                columns,
                lanes,
                ceiling_ref[head],
                burst,
                query_out,
                inner_out,
            )


def cost_of(rows, depth, width):
    return pl.CostEstimate(
        flops=2 * rows * depth * width, bytes_accessed=depth * width * 2, transcendentals=0
    )


def relay_kernel(source, out, late):
    rows = source.shape[0]
    moved_rows = jnp.swapaxes(source[...], 0, 1)
    out[:, pl.ds(pl.multiple_of(pl.program_id(0) * rows, rows), rows), :] = moved_rows
    late[0] = moved_rows[0]
    late[1] = moved_rows[3]


def relay_call(in_proj):
    depth, parts, width = in_proj.shape
    rows = 256
    return pl.pallas_call(
        relay_kernel,
        grid=(depth // rows,),
        out_shape=(pltpu.VMEM((parts, depth, width), BF16), hbm_of(2, depth, width)),
        in_specs=[pl.BlockSpec((rows, parts, width), lambda b: (b, 0, 0))],
        out_specs=(VMEM, pl.BlockSpec((2, rows, width), lambda b: (0, b, 0))),
        compiler_params=limit(18, "arbitrary"),
        name="relay",
    )(*in_hbm(in_proj))


def text_call(place, ceiling, chunks, gain, weights, decay):
    rows, width = chunks[0].shape
    depth = gain.shape[1]
    outs = (
        hbm_of(rows, width),
        hbm_of(rows, width),
        hbm_of(rows, width, dtype=F32),
        shape_of(32, 16, HEAD_WIDTH),
        shape_of(4, HEAD_WIDTH, dtype=F32),
    )
    arrays = (*chunks, gain, weights, decay)
    return pl.pallas_call(
        text_kernel,
        grid=(1,),
        out_shape=outs,
        in_specs=[SMEM, SMEM] + [VMEM] * len(arrays),
        out_specs=tuple(fixed(*o.shape) for o in outs),
        scratch_shapes=[
            pltpu.VMEM((rows, depth), BF16),
            pltpu.VMEM((3, rows, width), BF16),
            pltpu.VMEM((rows, 4), F32),
            pltpu.VMEM((4, rows), F32),
        ],
        compiler_params=limit(24, "arbitrary"),
        cost_estimate=cost_of(rows, depth, 4 * width),
        name="text_unit",
    )(place, ceiling, *arrays)


def image_state_call(place, ceiling, forget, chunks, gain, weights, decay, state, span):
    rows, width = chunks[0].shape
    depth = gain.shape[1]
    outs = (
        hbm_of(rows, depth),
        hbm_of(2, rows, width),
        shape_of(rows, 4, dtype=F32),
        shape_of(4, rows, dtype=F32),
        shape_of(32, 40, HEAD_WIDTH),
    )
    arrays = (*chunks, gain, weights, decay, state, span)
    return pl.pallas_call(
        image_state_kernel,
        out_shape=outs,
        in_specs=[SMEM] * 3 + [VMEM] * len(arrays),
        out_specs=(HBM, HBM, VMEM, VMEM, VMEM),
        scratch_shapes=[
            pltpu.VMEM((rows, depth), BF16),
            pltpu.VMEM((2, rows, width), BF16),
            pltpu.SemaphoreType.DMA((2,)),
        ],
        compiler_params=limit(24),
        cost_estimate=cost_of(rows, depth, 2 * width),
        name="image_state",
    )(place, ceiling, forget, *arrays)


def image_attend_call(place, ceiling, forget, weights, normed, key_value, columns, lanes):
    rows, depth = normed.shape
    width = key_value.shape[2]
    outs = (
        hbm_of(rows, width),
        hbm_of(rows, width),
        hbm_of(rows, width, dtype=F32),
    )
    held = (*in_hbm(normed, key_value), columns, lanes)
    return pl.pallas_call(
        image_attend_kernel,
        grid=(2,),
        out_shape=outs,
        in_specs=[SMEM] * 3
        + [fixed(*h.shape) for h in held]
        + [pl.BlockSpec((1, depth, width), lambda p: (p, 0, 0))],
        out_specs=tuple(fixed(*o.shape) for o in outs),
        scratch_shapes=[pltpu.VMEM((rows, width), BF16)],
        compiler_params=limit(20, "arbitrary"),
        cost_estimate=cost_of(rows, depth, 2 * width),
        name="image_attend",
    )(place, ceiling, forget, *held, *in_hbm(weights))


def scan_kernel(start_ref, states, out, decay, image_at):
    count = start_ref.shape[0]
    for kind in range(2):
        spans = states[:, 32:40, :].astype(F32)
        span = spans[:, 2 * kind : 2 * kind + 1, :] + spans[:, 2 * kind + 1 : 2 * kind + 2, :]
        decay[:, kind] = jnp.broadcast_to(jnp.exp(span), (count, 16, HEAD_WIDTH))
    for position in range(2 * count):
        image_at[position] = -1
    for image in range(count):
        image_at[lax.shift_right_logical(start_ref[image], 1)] = image
    carry = jnp.zeros((16, HEAD_WIDTH), F32)
    texts = jnp.int32(0)
    for position in range(2 * count):
        found = image_at[position]
        kind = (found >= 0).astype(jnp.int32)
        source = jnp.where(found >= 0, found, jnp.minimum(texts, count - 1))
        texts += 1 - kind
        rows = pl.ds(pl.multiple_of(kind * 16, 16), 16)
        out[source, rows, :] = carry.astype(BF16)
        carry = decay[source, kind] * carry + states[source, rows, :].astype(F32)


def scan_call(starts, states):
    count = states.shape[0]
    return pl.pallas_call(
        scan_kernel,
        out_shape=shape_of(count, 32, HEAD_WIDTH),
        in_specs=[SMEM, VMEM],
        out_specs=VMEM,
        scratch_shapes=[
            pltpu.VMEM((count, 2, 16, HEAD_WIDTH), F32),
            pltpu.SMEM((2 * count,), jnp.int32),
        ],
        compiler_params=limit(6),
        name="state_scan",
    )(starts, states)


def gate_kernel(place_ref, entering, out_gain, out_proj, *refs):
    sources, (far_text, far_image, gated), buffers, sems = refs[:6], refs[6:9], refs[9:15], refs[15]
    copies = [
        pltpu.make_async_copy(source, buffer, sems.at[at])
        for at, (source, buffer) in enumerate(zip(sources, buffers))
    ]
    for copy in copies:
        copy.start()
    rows, width = far_text.shape
    for kind in range(2):
        for copy in copies[3 * kind : 3 * kind + 3]:
            copy.wait()
        query, gate, inner = buffers[3 * kind : 3 * kind + 3]
        for head in range(width // HEAD_WIDTH):
            lanes = slice(head * HEAD_WIDTH, (head + 1) * HEAD_WIDTH)
            state = entering[head * 8 : (head + 1) * 8, kind * 16 : (kind + 1) * 16, :]
            attended = inner[:, lanes] + jnp.dot(
                query[:, lanes], state.reshape(HEAD_WIDTH, HEAD_WIDTH), preferred_element_type=F32
            )
            scale = lax.rsqrt(jnp.mean(attended * attended, axis=-1, keepdims=True) + EPSILON)
            value = attended * scale * out_gain[head : head + 1, :] * gate[:, lanes].astype(F32)
            gated[kind * rows : (kind + 1) * rows, lanes] = value.astype(BF16)
    weight = out_proj[:, columns_of(place_ref[0], 2, 4, width)]
    block = jnp.dot(gated[...], weight, preferred_element_type=F32).astype(BF16)
    far_text[...] = block[:rows]
    far_image[...] = block[rows:]


def gate_call(place, entering, out_gain, out_proj, text_parts, image_parts):
    rows, width = text_parts[0].shape
    outs = (shape_of(rows, width), shape_of(rows, width), shape_of(2 * rows, width))
    parts = in_hbm(*text_parts, *image_parts)
    return pl.pallas_call(
        gate_kernel,
        out_shape=outs,
        in_specs=[SMEM] + [VMEM] * 3 + [HBM] * 6,
        out_specs=(VMEM,) * 3,
        scratch_shapes=[pltpu.VMEM(p.shape, p.dtype) for p in parts]
        + [pltpu.SemaphoreType.DMA((6,))],
        compiler_params=limit(16),
        name="gate_far",
    )(place, entering, out_gain, out_proj, *parts)


def near_kernel(place_ref, gated, out_proj, next_t, next_i, last_t, last_i, own_t, own_i):
    rows, width = next_t.shape
    for step, text, image in ((1, next_t, next_i), (3, last_t, last_i), (0, own_t, own_i)):
        weight = out_proj[:, columns_of(place_ref[0], step, 4, width)]
        block = jnp.dot(gated[...], weight, preferred_element_type=F32)
        text[...] = block[:rows].astype(text.dtype)
        image[...] = block[rows:].astype(image.dtype)


def near_call(place, gated, out_proj):
    rows, width = gated.shape[0] // 2, gated.shape[1]
    outs = (shape_of(rows, width),) * 4 + (shape_of(rows, width, dtype=F32),) * 2
    return pl.pallas_call(
        near_kernel,
        out_shape=outs,
        in_specs=[SMEM, VMEM, VMEM],
        out_specs=(VMEM,) * 6,
        compiler_params=limit(16),
        cost_estimate=cost_of(2 * rows, width, 3 * width),
        name="near_blocks",
    )(place, gated, out_proj)


def moved(array, step):
    return lax.ppermute(array, "head", [(i, (i + step) % 4) for i in range(4)])


def gathered(rows):
    half = rows.shape[0] // 2
    left = moved(rows, 1)
    right = moved(rows, 3)
    far_a = moved(left[:half], 1)
    far_b = moved(right[half:], 3)
    return (rows, left, right, far_a, far_b)


def added(one, two):
    return (one.astype(F32) + two.astype(F32)).astype(BF16)


def steps(
    image_patches,
    text_embed,
    image_start,
    image_forget,
    adapter,
    norm_gain,
    in_proj,
    decay_proj,
    head_decay_ceiling,
    out_gain,
    out_proj,
):
    place = jnp.stack([lax.axis_index("head"), lax.axis_index(SEQ)]).astype(jnp.int32)
    decay = decay_proj.T
    gain = norm_gain[None]
    ceiling = head_decay_ceiling

    text_chunks = gathered(text_embed)
    to_next, to_last, near_next, near_last, own = adapter_sums(
        place, image_patches.transpose(0, 2, 1), adapter
    )
    weights, late_weights = relay_call(in_proj)
    from_left = moved(to_next, 1)
    from_right = moved(to_last, 3)
    next_sum, last_sum = pass_call(from_left, from_right, near_next, near_last)
    left = moved(next_sum, 1)
    right = moved(last_sum, 3)
    embed = embed_call(own, from_left, from_right, left, right)
    image_chunks = gathered(embed)

    *text_parts, text_state, text_span = text_call(
        place, ceiling, text_chunks, gain, weights, decay
    )
    *held, states = image_state_call(
        place, ceiling, image_forget, image_chunks, gain, weights, decay, text_state, text_span
    )
    slices = lax.all_to_all(states, SEQ, 0, 0, tiled=True)
    image_parts = image_attend_call(
        place, ceiling, image_forget, late_weights, *held
    )
    entering = lax.all_to_all(scan_call(image_start, slices), SEQ, 0, 0, tiled=True)

    far_t, far_i, gated = gate_call(
        place, entering, out_gain, out_proj, text_parts, image_parts
    )
    next_t, next_i, last_t, last_i, own_t, own_i = near_call(place, gated, out_proj)
    far_from_left = moved(far_t, 1)
    far_from_right = moved(far_i, 3)
    left_i = moved(next_i, 1)
    right_t = moved(last_t, 3)
    left_t = moved(added(next_t, far_from_left), 1)
    right_i = moved(added(last_i, far_from_right), 3)
    text_out = text_embed.astype(F32) + (own_t + left_t.astype(F32) + right_t.astype(F32))
    image_out = embed.astype(F32) + (own_i + left_i.astype(F32) + right_i.astype(F32))
    return (image_out.astype(BF16)[None], text_out.astype(BF16))


def solution(mesh):
    split = Mesh(
        mesh.devices.reshape(4, 4, 2, mesh.shape["head"]), ("seq_0", "seq_1", "seq_2", "head")
    )
    return jax.shard_map(
        steps,
        mesh=split,
        in_specs=(
            P(SEQ, None, "head"),
            P(SEQ, "head"),
            P(),
            P(),
            P("head", None),
            P(),
            P(None, None, "head"),
            P(None, "head"),
            P("head"),
            P("head", None),
            P("head", None),
        ),
        out_specs=(P(SEQ, None, "head"), P(SEQ, "head")),
        check_vma=False,
    )
```

```python
import jax
import jax.numpy as jnp
from jax import lax
from jax.experimental import pallas as pl
from jax.experimental.pallas import tpu as pltpu
from jax.sharding import Mesh
from jax.sharding import PartitionSpec as P

SEQ = ("seq_0", "seq_1", "seq_2")
EPSILON = 1e-06
F32 = jnp.float32
BF16 = jnp.bfloat16
HEAD_WIDTH = 128


VMEM = pl.BlockSpec(memory_space=pltpu.VMEM)
SMEM = pl.BlockSpec(memory_space=pltpu.SMEM)
HBM = pl.BlockSpec(memory_space=pltpu.HBM)


def shape_of(*dims, dtype=BF16):
    return jax.ShapeDtypeStruct(dims, dtype)


def hbm_of(*dims, dtype=BF16):
    return pltpu.HBM(dims, dtype)


def in_hbm(*arrays):
    return [pltpu.with_memory_space_constraint(a, pltpu.HBM) for a in arrays]


def limit(mebibytes, *semantics):
    return pltpu.CompilerParams(
        dimension_semantics=semantics or None, vmem_limit_bytes=mebibytes << 20
    )


def fixed(*dims):
    return pl.BlockSpec(dims, lambda *_: (0,) * len(dims))


def columns_of(place, step, count, width):
    return pl.ds(pl.multiple_of(lax.rem(place + step, count) * width, width), width)


def adapter_kernel(
    place_ref,
    patches_ref,
    adapter_ref,
    to_next,
    to_last,
    near_next,
    near_last,
    own,
    patches,
    blocks,
    sems,
):
    half = near_next.shape[0]
    width = own.shape[1]
    patches_copy = pltpu.make_async_copy(patches_ref.at[0], patches, sems.at[0])
    patches_copy.start()
    copies = []
    for at, step in enumerate((2, 1, 3, 0)):
        columns = columns_of(place_ref[0], step, 4, width)
        copies.append(
            pltpu.make_async_copy(adapter_ref.at[:, columns], blocks.at[at], sems.at[at + 1])
        )
        copies[at].start()
    patches_copy.wait()
    rows = patches[...].T
    for at in range(4):
        copies[at].wait()
        block = jnp.dot(rows, blocks[at], preferred_element_type=F32)
        small = block.astype(BF16)
        if at == 0:
            to_next[:half] = small[:half]
            to_last[half:] = small[half:]
        elif at == 1:
            near_next[...] = small[:half]
            to_next[half:] = small[half:]
        elif at == 2:
            to_last[:half] = small[:half]
            near_last[...] = small[half:]
        else:
            own[...] = block


def adapter_sums(place, patches, adapter):
    depth, rows = patches.shape[1:]
    width = adapter.shape[1] // 4
    outs = (
        shape_of(rows, width),
        shape_of(rows, width),
        shape_of(rows // 2, width),
        shape_of(rows // 2, width),
        shape_of(rows, width, dtype=F32),
    )
    return pl.pallas_call(
        adapter_kernel,
        out_shape=outs,
        in_specs=[SMEM, HBM, HBM],
        out_specs=(VMEM,) * 5,
        scratch_shapes=[
            pltpu.VMEM((depth, rows), BF16),
            pltpu.VMEM((4, depth, width), BF16),
            pltpu.SemaphoreType.DMA((5,)),
        ],
        compiler_params=limit(8),
        name="adapter_sums",
    )(place, *in_hbm(patches, adapter))


def pass_kernel(from_left, from_right, near_next, near_last, next_out, last_out):
    half = near_next.shape[0]
    next_out[...] = (near_next[...].astype(F32) + from_left[:half].astype(F32)).astype(BF16)
    last_out[...] = (near_last[...].astype(F32) + from_right[half:].astype(F32)).astype(BF16)


def pass_call(*arrays):
    half = shape_of(*arrays[2].shape)
    return pl.pallas_call(
        pass_kernel,
        out_shape=(half, half),
        in_specs=[VMEM] * 4,
        out_specs=(VMEM, VMEM),
        compiler_params=limit(4),
        name="pass_on",
    )(*arrays)


def embed_kernel(own, from_left, from_right, left, right, out):
    half = left.shape[0]
    first = own[:half] + left[...].astype(F32) + from_right[:half].astype(F32)
    second = own[half:] + from_left[half:].astype(F32) + right[...].astype(F32)
    out[:half] = first.astype(BF16)
    out[half:] = second.astype(BF16)


def embed_call(own, *arrays):
    return pl.pallas_call(
        embed_kernel,
        out_shape=shape_of(*own.shape),
        in_specs=[VMEM] * 5,
        out_specs=VMEM,
        compiler_params=limit(4),
        name="embed",
    )(own, *arrays)


def normalize(place, chunks, gain_ref, normed):
    own, left, right, far_a, far_b = chunks
    rows, width = own.shape
    half = rows // 2
    for at, far in ((0, far_a), (half, far_b)):
        span = slice(at, at + half)
        values = ((0, own[span]), (3, left[span]), (1, right[span]), (2, far[...]))
        total = 0.0
        for _, value in values:
            value = value.astype(F32)
            total += jnp.sum(value * value, axis=-1, keepdims=True)
        scale = lax.rsqrt(total / (4 * width) + EPSILON)
        for step, value in values:
            columns = columns_of(place, step, 4, width)
            normed[span, columns] = (value.astype(F32) * scale * gain_ref[:, columns]).astype(BF16)


def product(normed, weight):
    return jnp.dot(normed[...], weight, preferred_element_type=F32)


def decay_sums(normed, decay_ref, columns, lanes):
    rows = normed.shape[0]
    decay = decay_ref[...].astype(F32)
    decay = jnp.concatenate([decay] * 4, axis=0).astype(BF16)
    decay = jnp.concatenate([decay, jnp.zeros((HEAD_WIDTH - 16, decay.shape[1]), BF16)], axis=0)
    gates = jax.nn.sigmoid(
        lax.dot_general(normed[...], decay, (((1,), (1,)), ((), ())), preferred_element_type=F32)
    )
    ids = lax.broadcasted_iota(jnp.int32, gates.shape, 1)
    upper = gates.astype(BF16).astype(F32)
    middle = (gates - upper).astype(BF16).astype(F32)
    terms = jnp.where(ids < 4, upper, jnp.where(ids < 8, middle, gates - upper - middle))
    row_ids = lax.broadcasted_iota(jnp.int32, (rows, rows), 0)
    column_ids = lax.broadcasted_iota(jnp.int32, (rows, rows), 1)
    sums = jnp.dot(
        (row_ids >= column_ids).astype(BF16), terms.astype(BF16), preferred_element_type=F32
    )
    columns[...] = sums[:, 0:4] + sums[:, 4:8] + sums[:, 8:12]
    by_row = sums.T
    lanes[...] = by_row[0:4] + by_row[4:8] + by_row[8:12]


def silu_of(gates):
    gates = gates.astype(BF16).astype(F32)
    return (gates * jax.nn.sigmoid(gates)).astype(BF16)


def chunk_state(head, key, value, columns, ceiling, burst):
    rows = columns.shape[0]
    lanes = slice(head * HEAD_WIDTH, (head + 1) * HEAD_WIDTH)
    column = columns[:, head : head + 1]
    last = columns[rows - 1 :, head : head + 1]
    weighted = key[:, lanes].astype(F32) * jnp.exp(ceiling * (column - last))
    state = lax.dot_general(
        weighted.astype(BF16), value[:, lanes], (((0,), (0,)), ((), ())), preferred_element_type=F32
    )
    return state.astype(BF16).reshape(8, 16, HEAD_WIDTH), burst - ceiling * last


def attend(head, query, key, value, columns, lanes_ref, ceiling, burst, query_out, inner_out):
    rows = columns.shape[0]
    lanes = slice(head * HEAD_WIDTH, (head + 1) * HEAD_WIDTH)
    column = columns[:, head : head + 1]
    lagged = ceiling * (lanes_ref[head : head + 1, :] - column)
    row_ids = lax.broadcasted_iota(jnp.int32, (rows, rows), 0)
    column_ids = lax.broadcasted_iota(jnp.int32, (rows, rows), 1)
    scores = lax.dot_general(
        query[:, lanes], key[:, lanes], (((1,), (1,)), ((), ())), preferred_element_type=F32
    )
    weights = jnp.where(row_ids >= column_ids, scores * jnp.exp(jnp.minimum(lagged, 0.0)), 0.0)
    inner_out[:, lanes] = jnp.dot(weights.astype(BF16), value[:, lanes], preferred_element_type=F32)
    entry = jnp.exp(burst - ceiling * column)
    query_out[:, lanes] = (query[:, lanes].astype(F32) * entry).astype(BF16)


def text_kernel(
    place_ref,
    ceiling_ref,
    own,
    left,
    right,
    far_a,
    far_b,
    gain_ref,
    weight,
    decay_ref,
    query_out,
    gate_out,
    inner_out,
    state_out,
    span_out,
    late_out,
    normed,
    parts,
    columns,
    lanes,
    sems,
):
    copies = [
        pltpu.make_async_copy(weight.at[3 * at], late_out.at[at], sems.at[at]) for at in range(2)
    ]
    for copy in copies:
        copy.start()
    normalize(place_ref[0], (own, left, right, far_a, far_b), gain_ref, normed)
    decay_sums(normed, decay_ref, columns, lanes)
    for part in range(3):
        parts[part] = product(normed, weight[part]).astype(BF16)
    gate_out[...] = silu_of(product(normed, weight[3]))
    for head in range(4):
        ceiling = ceiling_ref[head]
        state, span = chunk_state(head, parts.at[1], parts.at[2], columns, ceiling, 0.0)
        state_out[head * 8 : (head + 1) * 8] = state
        span_out[head : head + 1] = jnp.broadcast_to(span, (1, HEAD_WIDTH))
        attend(
            head,
            parts.at[0],
            parts.at[1],
            parts.at[2],
            columns,
            lanes,
            ceiling,
            0.0,
            query_out,
            inner_out,
        )
    for copy in copies:
        copy.wait()


def image_state_kernel(
    place_ref,
    ceiling_ref,
    forget_ref,
    own,
    left,
    right,
    far_a,
    far_b,
    gain_ref,
    weight,
    decay_ref,
    other_state,
    other_span,
    normed_out,
    key_value_out,
    columns,
    lanes,
    state_out,
    normed,
    key_value,
    sems,
):
    normalize(place_ref[0], (own, left, right, far_a, far_b), gain_ref, normed)
    key_value[0] = product(normed, weight[1]).astype(BF16)
    normed_copy = pltpu.make_async_copy(normed, normed_out, sems.at[0])
    normed_copy.start()
    key_value[1] = product(normed, weight[2]).astype(BF16)
    decay_sums(normed, decay_ref, columns, lanes)
    key_value_copy = pltpu.make_async_copy(key_value, key_value_out, sems.at[1])
    key_value_copy.start()
    state_out[:, 0:16, :] = other_state[...]
    burst = jnp.log1p(jnp.full((1, 1), -forget_ref[place_ref[1]], F32))
    ids = lax.broadcasted_iota(jnp.int32, (8, HEAD_WIDTH), 0)
    for head in range(4):
        state, span = chunk_state(
            head, key_value.at[0], key_value.at[1], columns, ceiling_ref[head], burst
        )
        targets = slice(head * 8, (head + 1) * 8)
        state_out[targets, 16:32, :] = state
        tile = jnp.zeros((8, HEAD_WIDTH), F32)
        for kind, value in enumerate((other_span[head : head + 1, 0:1], span)):
            upper = value.astype(BF16).astype(F32)
            tile = jnp.where(ids == 2 * kind, upper, tile)
            tile = jnp.where(ids == 2 * kind + 1, value - upper, tile)
        state_out[targets, 32:40, :] = jnp.broadcast_to(
            tile.astype(BF16)[None], (8, 8, HEAD_WIDTH)
        )
    normed_copy.wait()
    key_value_copy.wait()


def image_attend_kernel(
    place_ref,
    ceiling_ref,
    forget_ref,
    normed,
    key_value,
    columns,
    lanes,
    weight,
    query_out,
    gate_out,
    inner_out,
    query,
):
    part = pl.program_id(0)
    block = product(normed, weight[0])

    @pl.when(part == 0)
    def _():
        query[...] = block.astype(BF16)

    @pl.when(part == 1)
    def _():
        gate_out[...] = silu_of(block)
        burst = jnp.log1p(jnp.full((1, 1), -forget_ref[place_ref[1]], F32))
        for head in range(4):
            attend(
                head,
                query,
                key_value.at[0],
                key_value.at[1],
                columns,
                lanes,
                ceiling_ref[head],
                burst,
                query_out,
                inner_out,
            )


def cost_of(rows, depth, width):
    return pl.CostEstimate(
        flops=2 * rows * depth * width, bytes_accessed=depth * width * 2, transcendentals=0
    )


def relay_kernel(source, out, blocks, sems):
    count, rows = blocks.shape[:2]
    copies = [
        pltpu.make_async_copy(source.at[pl.ds(at * rows, rows)], blocks.at[at], sems.at[at])
        for at in range(count)
    ]
    for copy in copies:
        copy.start()
    for at in range(count):
        copies[at].wait()
        out[:, at * rows : (at + 1) * rows, :] = jnp.swapaxes(blocks[at], 0, 1)


def relay_call(in_proj):
    depth, parts, width = in_proj.shape
    count = 8
    return pl.pallas_call(
        relay_kernel,
        out_shape=pltpu.VMEM((parts, depth, width), BF16),
        in_specs=[HBM],
        out_specs=VMEM,
        scratch_shapes=[
            pltpu.VMEM((count, depth // count, parts, width), BF16),
            pltpu.SemaphoreType.DMA((count,)),
        ],
        compiler_params=limit(20),
        cost_estimate=pl.CostEstimate(
            flops=0, bytes_accessed=2 * depth * parts * width, transcendentals=0
        ),
        name="relay",
    )(*in_hbm(in_proj))


def text_call(place, ceiling, chunks, gain, weights, decay):
    rows, width = chunks[0].shape
    depth = gain.shape[1]
    outs = (
        hbm_of(rows, width),
        hbm_of(rows, width),
        hbm_of(rows, width, dtype=F32),
        shape_of(32, 16, HEAD_WIDTH),
        shape_of(4, HEAD_WIDTH, dtype=F32),
        hbm_of(2, depth, width),
    )
    arrays = (*chunks, gain, weights, decay)
    return pl.pallas_call(
        text_kernel,
        grid=(1,),
        out_shape=outs,
        in_specs=[SMEM, SMEM] + [VMEM] * len(arrays),
        out_specs=tuple(fixed(*o.shape) for o in outs[:-1]) + (HBM,),
        scratch_shapes=[
            pltpu.VMEM((rows, depth), BF16),
            pltpu.VMEM((3, rows, width), BF16),
            pltpu.VMEM((rows, 4), F32),
            pltpu.VMEM((4, rows), F32),
            pltpu.SemaphoreType.DMA((2,)),
        ],
        compiler_params=limit(24, "arbitrary"),
        cost_estimate=cost_of(rows, depth, 4 * width),
        name="text_unit",
    )(place, ceiling, *arrays)


def image_state_call(place, ceiling, forget, chunks, gain, weights, decay, state, span):
    rows, width = chunks[0].shape
    depth = gain.shape[1]
    outs = (
        hbm_of(rows, depth),
        hbm_of(2, rows, width),
        shape_of(rows, 4, dtype=F32),
        shape_of(4, rows, dtype=F32),
        shape_of(32, 40, HEAD_WIDTH),
    )
    arrays = (*chunks, gain, weights, decay, state, span)
    return pl.pallas_call(
        image_state_kernel,
        out_shape=outs,
        in_specs=[SMEM] * 3 + [VMEM] * len(arrays),
        out_specs=(HBM, HBM, VMEM, VMEM, VMEM),
        scratch_shapes=[
            pltpu.VMEM((rows, depth), BF16),
            pltpu.VMEM((2, rows, width), BF16),
            pltpu.SemaphoreType.DMA((2,)),
        ],
        compiler_params=limit(24),
        cost_estimate=cost_of(rows, depth, 2 * width),
        name="image_state",
    )(place, ceiling, forget, *arrays)


def image_attend_call(place, ceiling, forget, weights, normed, key_value, columns, lanes):
    rows, depth = normed.shape
    width = key_value.shape[2]
    outs = (
        hbm_of(rows, width),
        hbm_of(rows, width),
        hbm_of(rows, width, dtype=F32),
    )
    held = (*in_hbm(normed, key_value), columns, lanes)
    return pl.pallas_call(
        image_attend_kernel,
        grid=(2,),
        out_shape=outs,
        in_specs=[SMEM] * 3
        + [fixed(*h.shape) for h in held]
        + [pl.BlockSpec((1, depth, width), lambda p: (p, 0, 0))],
        out_specs=tuple(fixed(*o.shape) for o in outs),
        scratch_shapes=[pltpu.VMEM((rows, width), BF16)],
        compiler_params=limit(20, "arbitrary"),
        cost_estimate=cost_of(rows, depth, 2 * width),
        name="image_attend",
    )(place, ceiling, forget, *held, *in_hbm(weights))


def scan_kernel(start_ref, states, out, decay, image_at):
    count = start_ref.shape[0]
    for kind in range(2):
        spans = states[:, 32:40, :].astype(F32)
        span = spans[:, 2 * kind : 2 * kind + 1, :] + spans[:, 2 * kind + 1 : 2 * kind + 2, :]
        decay[:, kind] = jnp.broadcast_to(jnp.exp(span), (count, 16, HEAD_WIDTH))
    for position in range(2 * count):
        image_at[position] = -1
    for image in range(count):
        image_at[lax.shift_right_logical(start_ref[image], 1)] = image
    carry = jnp.zeros((16, HEAD_WIDTH), F32)
    texts = jnp.int32(0)
    for position in range(2 * count):
        found = image_at[position]
        kind = (found >= 0).astype(jnp.int32)
        source = jnp.where(found >= 0, found, jnp.minimum(texts, count - 1))
        texts += 1 - kind
        rows = pl.ds(pl.multiple_of(kind * 16, 16), 16)
        out[source, rows, :] = carry.astype(BF16)
        carry = decay[source, kind] * carry + states[source, rows, :].astype(F32)


def scan_call(starts, states):
    count = states.shape[0]
    return pl.pallas_call(
        scan_kernel,
        out_shape=shape_of(count, 32, HEAD_WIDTH),
        in_specs=[SMEM, VMEM],
        out_specs=VMEM,
        scratch_shapes=[
            pltpu.VMEM((count, 2, 16, HEAD_WIDTH), F32),
            pltpu.SMEM((2 * count,), jnp.int32),
        ],
        compiler_params=limit(6),
        name="state_scan",
    )(starts, states)


def gate_kernel(place_ref, entering, out_gain, out_proj, *refs):
    sources, (far_text, far_image, gated), buffers, sems = refs[:6], refs[6:9], refs[9:15], refs[15]
    copies = [
        pltpu.make_async_copy(source, buffer, sems.at[at])
        for at, (source, buffer) in enumerate(zip(sources, buffers))
    ]
    for copy in copies:
        copy.start()
    rows, width = far_text.shape
    for kind in range(2):
        for copy in copies[3 * kind : 3 * kind + 3]:
            copy.wait()
        query, gate, inner = buffers[3 * kind : 3 * kind + 3]
        for head in range(width // HEAD_WIDTH):
            lanes = slice(head * HEAD_WIDTH, (head + 1) * HEAD_WIDTH)
            state = entering[head * 8 : (head + 1) * 8, kind * 16 : (kind + 1) * 16, :]
            attended = inner[:, lanes] + jnp.dot(
                query[:, lanes], state.reshape(HEAD_WIDTH, HEAD_WIDTH), preferred_element_type=F32
            )
            scale = lax.rsqrt(jnp.mean(attended * attended, axis=-1, keepdims=True) + EPSILON)
            value = attended * scale * out_gain[head : head + 1, :] * gate[:, lanes].astype(F32)
            gated[kind * rows : (kind + 1) * rows, lanes] = value.astype(BF16)
    weight = out_proj[:, columns_of(place_ref[0], 2, 4, width)]
    block = jnp.dot(gated[...], weight, preferred_element_type=F32).astype(BF16)
    far_text[...] = block[:rows]
    far_image[...] = block[rows:]


def gate_call(place, entering, out_gain, out_proj, text_parts, image_parts):
    rows, width = text_parts[0].shape
    outs = (shape_of(rows, width), shape_of(rows, width), shape_of(2 * rows, width))
    parts = in_hbm(*text_parts, *image_parts)
    return pl.pallas_call(
        gate_kernel,
        out_shape=outs,
        in_specs=[SMEM] + [VMEM] * 3 + [HBM] * 6,
        out_specs=(VMEM,) * 3,
        scratch_shapes=[pltpu.VMEM(p.shape, p.dtype) for p in parts]
        + [pltpu.SemaphoreType.DMA((6,))],
        compiler_params=limit(16),
        name="gate_far",
    )(place, entering, out_gain, out_proj, *parts)


def near_kernel(place_ref, gated, out_proj, next_t, next_i, last_t, last_i, own_t, own_i):
    rows, width = next_t.shape
    for step, text, image in ((1, next_t, next_i), (3, last_t, last_i), (0, own_t, own_i)):
        weight = out_proj[:, columns_of(place_ref[0], step, 4, width)]
        block = jnp.dot(gated[...], weight, preferred_element_type=F32)
        text[...] = block[:rows].astype(text.dtype)
        image[...] = block[rows:].astype(image.dtype)


def near_call(place, gated, out_proj):
    rows, width = gated.shape[0] // 2, gated.shape[1]
    outs = (shape_of(rows, width),) * 4 + (shape_of(rows, width, dtype=F32),) * 2
    return pl.pallas_call(
        near_kernel,
        out_shape=outs,
        in_specs=[SMEM, VMEM, VMEM],
        out_specs=(VMEM,) * 6,
        compiler_params=limit(16),
        cost_estimate=cost_of(2 * rows, width, 3 * width),
        name="near_blocks",
    )(place, gated, out_proj)


def moved(array, step):
    return lax.ppermute(array, "head", [(i, (i + step) % 4) for i in range(4)])


def gathered(rows):
    half = rows.shape[0] // 2
    left = moved(rows, 1)
    right = moved(rows, 3)
    far_a = moved(left[:half], 1)
    far_b = moved(right[half:], 3)
    return (rows, left, right, far_a, far_b)


def added(one, two):
    return (one.astype(F32) + two.astype(F32)).astype(BF16)


def steps(
    image_patches,
    text_embed,
    image_start,
    image_forget,
    adapter,
    norm_gain,
    in_proj,
    decay_proj,
    head_decay_ceiling,
    out_gain,
    out_proj,
):
    place = jnp.stack([lax.axis_index("head"), lax.axis_index(SEQ)]).astype(jnp.int32)
    decay = decay_proj.T
    gain = norm_gain[None]
    ceiling = head_decay_ceiling

    text_chunks = gathered(text_embed)
    to_next, to_last, near_next, near_last, own = adapter_sums(
        place, image_patches.transpose(0, 2, 1), adapter
    )
    weights = relay_call(in_proj)
    from_left = moved(to_next, 1)
    from_right = moved(to_last, 3)
    next_sum, last_sum = pass_call(from_left, from_right, near_next, near_last)
    left = moved(next_sum, 1)
    right = moved(last_sum, 3)
    embed = embed_call(own, from_left, from_right, left, right)
    image_chunks = gathered(embed)

    *text_parts, text_state, text_span, late_weights = text_call(
        place, ceiling, text_chunks, gain, weights, decay
    )
    *held, states = image_state_call(
        place, ceiling, image_forget, image_chunks, gain, weights, decay, text_state, text_span
    )
    slices = lax.all_to_all(states, SEQ, 0, 0, tiled=True)
    image_parts = image_attend_call(
        place, ceiling, image_forget, late_weights, *held
    )
    entering = lax.all_to_all(scan_call(image_start, slices), SEQ, 0, 0, tiled=True)

    far_t, far_i, gated = gate_call(
        place, entering, out_gain, out_proj, text_parts, image_parts
    )
    next_t, next_i, last_t, last_i, own_t, own_i = near_call(place, gated, out_proj)
    far_from_left = moved(far_t, 1)
    far_from_right = moved(far_i, 3)
    left_i = moved(next_i, 1)
    right_t = moved(last_t, 3)
    left_t = moved(added(next_t, far_from_left), 1)
    right_i = moved(added(last_i, far_from_right), 3)
    text_out = text_embed.astype(F32) + (own_t + left_t.astype(F32) + right_t.astype(F32))
    image_out = embed.astype(F32) + (own_i + left_i.astype(F32) + right_i.astype(F32))
    return (image_out.astype(BF16)[None], text_out.astype(BF16))


def solution(mesh):
    split = Mesh(
        mesh.devices.reshape(4, 4, 2, mesh.shape["head"]), ("seq_0", "seq_1", "seq_2", "head")
    )
    return jax.shard_map(
        steps,
        mesh=split,
        in_specs=(
            P(SEQ, None, "head"),
            P(SEQ, "head"),
            P(),
            P(),
            P("head", None),
            P(),
            P(None, None, "head"),
            P(None, "head"),
            P("head"),
            P("head", None),
            P("head", None),
        ),
        out_specs=(P(SEQ, None, "head"), P(SEQ, "head")),
        check_vma=False,
    )
```

```python
import jax
import jax.numpy as jnp
from jax import lax
from jax.experimental import pallas as pl
from jax.experimental.pallas import tpu as pltpu
from jax.sharding import Mesh
from jax.sharding import PartitionSpec as P

SEQ = ("seq_0", "seq_1", "seq_2")
EPSILON = 1e-06
F32 = jnp.float32
BF16 = jnp.bfloat16
HEAD_WIDTH = 128


VMEM = pl.BlockSpec(memory_space=pltpu.VMEM)
SMEM = pl.BlockSpec(memory_space=pltpu.SMEM)
HBM = pl.BlockSpec(memory_space=pltpu.HBM)


def shape_of(*dims, dtype=BF16):
    return jax.ShapeDtypeStruct(dims, dtype)


def hbm_of(*dims, dtype=BF16):
    return pltpu.HBM(dims, dtype)


def in_hbm(*arrays):
    return [pltpu.with_memory_space_constraint(a, pltpu.HBM) for a in arrays]


def limit(mebibytes, *semantics):
    return pltpu.CompilerParams(
        dimension_semantics=semantics or None, vmem_limit_bytes=mebibytes << 20
    )


def fixed(*dims):
    return pl.BlockSpec(dims, lambda *_: (0,) * len(dims))


def columns_of(place, step, count, width):
    return pl.ds(pl.multiple_of(lax.rem(place + step, count) * width, width), width)


def adapter_blocks(place_ref, patches_ref, adapter_ref, patches, blocks, sems, steps):
    patches_copy = pltpu.make_async_copy(patches_ref.at[0], patches, sems.at[0])
    patches_copy.start()
    copies = []
    for at, step in enumerate(steps):
        columns = columns_of(place_ref[0], step, 4, blocks.shape[2])
        copies.append(
            pltpu.make_async_copy(adapter_ref.at[:, columns], blocks.at[at], sems.at[at + 1])
        )
        copies[at].start()
    patches_copy.wait()
    rows = patches[...].T
    for at in range(len(steps)):
        copies[at].wait()
        yield jnp.dot(rows, blocks[at], preferred_element_type=F32)


def adapter_kernel(place_ref, patches_ref, adapter_ref, *refs):
    to_next, to_last, near_next, near_last, patches, blocks, sems = refs
    half = near_next.shape[0]
    steps = (2, 1, 3)
    made = adapter_blocks(place_ref, patches_ref, adapter_ref, patches, blocks, sems, steps)
    for step, block in zip(steps, made):
        small = block.astype(BF16)
        if step == 2:
            to_next[:half] = small[:half]
            to_last[half:] = small[half:]
        elif step == 1:
            near_next[...] = small[:half]
            to_next[half:] = small[half:]
        else:
            to_last[:half] = small[:half]
            near_last[...] = small[half:]


def own_kernel(place_ref, patches_ref, adapter_ref, own, patches, blocks, sems):
    for block in adapter_blocks(place_ref, patches_ref, adapter_ref, patches, blocks, sems, (0,)):
        own[...] = block


def adapter_call(kernel, outs, count, place, patches, adapter):
    depth, rows = patches.shape[1:]
    return pl.pallas_call(
        kernel,
        out_shape=outs,
        in_specs=[SMEM, HBM, HBM],
        out_specs=jax.tree.map(lambda _: VMEM, outs),
        scratch_shapes=[
            pltpu.VMEM((depth, rows), BF16),
            pltpu.VMEM((count, depth, adapter.shape[1] // 4), BF16),
            pltpu.SemaphoreType.DMA((count + 1,)),
        ],
        compiler_params=limit(8),
        cost_estimate=cost_of(rows, depth, count * adapter.shape[1] // 4),
    )(place, *in_hbm(patches, adapter))


def adapter_sums(*arrays):
    rows, width = arrays[1].shape[2], arrays[2].shape[1] // 4
    outs = (shape_of(rows, width),) * 2 + (shape_of(rows // 2, width),) * 2
    return adapter_call(adapter_kernel, outs, 3, *arrays)


def adapter_own(*arrays):
    rows, width = arrays[1].shape[2], arrays[2].shape[1] // 4
    outs = shape_of(rows, width, dtype=F32)
    return adapter_call(own_kernel, outs, 1, *arrays)


def pass_kernel(from_left, from_right, near_next, near_last, next_out, last_out):
    half = near_next.shape[0]
    next_out[...] = (near_next[...].astype(F32) + from_left[:half].astype(F32)).astype(BF16)
    last_out[...] = (near_last[...].astype(F32) + from_right[half:].astype(F32)).astype(BF16)


def pass_call(*arrays):
    half = shape_of(*arrays[2].shape)
    return pl.pallas_call(
        pass_kernel,
        out_shape=(half, half),
        in_specs=[VMEM] * 4,
        out_specs=(VMEM, VMEM),
        compiler_params=limit(4),
        name="pass_on",
    )(*arrays)


def embed_kernel(own, from_left, from_right, left, right, out):
    half = left.shape[0]
    first = own[:half] + left[...].astype(F32) + from_right[:half].astype(F32)
    second = own[half:] + from_left[half:].astype(F32) + right[...].astype(F32)
    out[:half] = first.astype(BF16)
    out[half:] = second.astype(BF16)


def embed_call(own, *arrays):
    return pl.pallas_call(
        embed_kernel,
        out_shape=shape_of(*own.shape),
        in_specs=[VMEM] * 5,
        out_specs=VMEM,
        compiler_params=limit(4),
        name="embed",
    )(own, *arrays)


def normalize(place, chunks, gain_ref, normed):
    own, left, right, far_a, far_b = chunks
    rows, width = own.shape
    half = rows // 2
    for at, far in ((0, far_a), (half, far_b)):
        span = slice(at, at + half)
        values = ((0, own[span]), (3, left[span]), (1, right[span]), (2, far[...]))
        total = 0.0
        for _, value in values:
            value = value.astype(F32)
            total += jnp.sum(value * value, axis=-1, keepdims=True)
        scale = lax.rsqrt(total / (4 * width) + EPSILON)
        for step, value in values:
            columns = columns_of(place, step, 4, width)
            normed[span, columns] = (value.astype(F32) * scale * gain_ref[:, columns]).astype(BF16)


def product(normed, weight):
    return jnp.dot(normed[...], weight, preferred_element_type=F32)


def decay_logits(values, decay):
    decay = jnp.concatenate([decay.astype(F32)] * 4, axis=0).astype(BF16)
    decay = jnp.concatenate([decay, jnp.zeros((HEAD_WIDTH - 16, decay.shape[1]), BF16)], axis=0)
    return lax.dot_general(values, decay, (((1,), (1,)), ((), ())), preferred_element_type=F32)


def decay_sums(logits, columns, lanes):
    rows = logits.shape[0]
    gates = jax.nn.sigmoid(logits)
    ids = lax.broadcasted_iota(jnp.int32, gates.shape, 1)
    upper = gates.astype(BF16).astype(F32)
    middle = (gates - upper).astype(BF16).astype(F32)
    terms = jnp.where(ids < 4, upper, jnp.where(ids < 8, middle, gates - upper - middle))
    row_ids = lax.broadcasted_iota(jnp.int32, (rows, rows), 0)
    column_ids = lax.broadcasted_iota(jnp.int32, (rows, rows), 1)
    sums = jnp.dot(
        (row_ids >= column_ids).astype(BF16), terms.astype(BF16), preferred_element_type=F32
    )
    columns[...] = sums[:, 0:4] + sums[:, 4:8] + sums[:, 8:12]
    by_row = sums.T
    lanes[...] = by_row[0:4] + by_row[4:8] + by_row[8:12]


def silu_of(gates):
    gates = gates.astype(BF16).astype(F32)
    return (gates * jax.nn.sigmoid(gates)).astype(BF16)


def chunk_state(head, key, value, columns, ceiling, burst):
    rows = columns.shape[0]
    lanes = slice(head * HEAD_WIDTH, (head + 1) * HEAD_WIDTH)
    column = columns[:, head : head + 1]
    last = columns[rows - 1 :, head : head + 1]
    weighted = key[:, lanes].astype(F32) * jnp.exp(ceiling * (column - last))
    state = lax.dot_general(
        weighted.astype(BF16), value[:, lanes], (((0,), (0,)), ((), ())), preferred_element_type=F32
    )
    return state.astype(BF16).reshape(8, 16, HEAD_WIDTH), burst - ceiling * last


def attend(head, query, key, value, columns, lanes_ref, ceiling, burst, query_out, inner_out):
    rows = columns.shape[0]
    lanes = slice(head * HEAD_WIDTH, (head + 1) * HEAD_WIDTH)
    column = columns[:, head : head + 1]
    lagged = ceiling * (lanes_ref[head : head + 1, :] - column)
    row_ids = lax.broadcasted_iota(jnp.int32, (rows, rows), 0)
    column_ids = lax.broadcasted_iota(jnp.int32, (rows, rows), 1)
    scores = lax.dot_general(
        query[:, lanes], key[:, lanes], (((1,), (1,)), ((), ())), preferred_element_type=F32
    )
    weights = jnp.where(row_ids >= column_ids, scores * jnp.exp(jnp.minimum(lagged, 0.0)), 0.0)
    inner_out[:, lanes] = jnp.dot(weights.astype(BF16), value[:, lanes], preferred_element_type=F32)
    entry = jnp.exp(burst - ceiling * column)
    query_out[:, lanes] = (query[:, lanes].astype(F32) * entry).astype(BF16)


def text_kernel(
    place_ref,
    ceiling_ref,
    own,
    left,
    right,
    far_a,
    far_b,
    gain_ref,
    weight,
    decay_ref,
    query_out,
    gate_out,
    inner_out,
    state_out,
    span_out,
    late_out,
    normed,
    parts,
    columns,
    lanes,
    sems,
):
    copies = [
        pltpu.make_async_copy(weight.at[3 * at], late_out.at[at], sems.at[at]) for at in range(2)
    ]
    for copy in copies:
        copy.start()
    normalize(place_ref[0], (own, left, right, far_a, far_b), gain_ref, normed)
    decay_sums(decay_logits(normed[...], decay_ref[...]), columns, lanes)
    for part in range(3):
        parts[part] = product(normed, weight[part]).astype(BF16)
    gate_out[...] = silu_of(product(normed, weight[3]))
    for head in range(4):
        ceiling = ceiling_ref[head]
        state, span = chunk_state(head, parts.at[1], parts.at[2], columns, ceiling, 0.0)
        state_out[head * 8 : (head + 1) * 8] = state
        span_out[head : head + 1] = jnp.broadcast_to(span, (1, HEAD_WIDTH))
        attend(
            head,
            parts.at[0],
            parts.at[1],
            parts.at[2],
            columns,
            lanes,
            ceiling,
            0.0,
            query_out,
            inner_out,
        )
    for copy in copies:
        copy.wait()


def image_near_kernel(
    place_ref, own, left, right, gain_ref, weight, decay_ref, scaled_out, total, logits, squares, scaled, sems
):
    copies = []
    for at, (step, ref) in enumerate(((0, own), (3, left), (1, right))):
        columns = columns_of(place_ref[0], step, 4, own.shape[1])
        value = ref[...].astype(F32)
        square = jnp.sum(value * value, axis=-1, keepdims=True)
        small = (value * gain_ref[:, columns]).astype(BF16)
        scaled[at] = small
        gates = decay_logits(small, decay_ref[:, columns])
        terms = [
            jnp.dot(small, weight[part, columns, :], preferred_element_type=F32)
            for part in (1, 2)
        ]
        copies.append(pltpu.make_async_copy(scaled.at[at], scaled_out.at[at], sems.at[at]))
        copies[at].start()
        if at == 0:
            squares[...], logits[...], total[0], total[1] = square, gates, *terms
        else:
            squares[...] += square
            logits[...] += gates
            total[0] += terms[0]
            total[1] += terms[1]
    for copy in copies:
        copy.wait()


def image_state_kernel(
    place_ref,
    ceiling_ref,
    forget_ref,
    far_a,
    far_b,
    total,
    logits,
    squares,
    gain_ref,
    weight,
    decay_ref,
    other_state,
    other_span,
    far_out,
    key_value_out,
    scale_out,
    columns,
    lanes,
    state_out,
    scaled,
    key_value,
    sems,
):
    half, width = far_a.shape
    chunk = columns_of(place_ref[0], 2, 4, width)
    square = []
    for at, ref in ((0, far_a), (half, far_b)):
        value = ref[...].astype(F32)
        square.append(jnp.sum(value * value, axis=-1, keepdims=True))
        scaled[at : at + half] = (value * gain_ref[:, chunk]).astype(BF16)
    square = squares[...] + jnp.concatenate(square, axis=0)
    scale = lax.rsqrt(square / (4 * width) + EPSILON)
    scale_out[...] = scale
    small = scaled[...]
    for at in range(2):
        term = jnp.dot(small, weight[at + 1, chunk, :], preferred_element_type=F32)
        key_value[at] = ((total[at] + term) * scale).astype(BF16)
    far_copy = pltpu.make_async_copy(scaled, far_out, sems.at[0])
    far_copy.start()
    decay_sums((logits[...] + decay_logits(small, decay_ref[:, chunk])) * scale, columns, lanes)
    key_value_copy = pltpu.make_async_copy(key_value, key_value_out, sems.at[1])
    key_value_copy.start()
    state_out[:, 0:16, :] = other_state[...]
    burst = jnp.log1p(jnp.full((1, 1), -forget_ref[place_ref[1]], F32))
    ids = lax.broadcasted_iota(jnp.int32, (8, HEAD_WIDTH), 0)
    for head in range(4):
        state, span = chunk_state(
            head, key_value.at[0], key_value.at[1], columns, ceiling_ref[head], burst
        )
        targets = slice(head * 8, (head + 1) * 8)
        state_out[targets, 16:32, :] = state
        tile = jnp.zeros((8, HEAD_WIDTH), F32)
        for kind, value in enumerate((other_span[head : head + 1, 0:1], span)):
            upper = value.astype(BF16).astype(F32)
            tile = jnp.where(ids == 2 * kind, upper, tile)
            tile = jnp.where(ids == 2 * kind + 1, value - upper, tile)
        state_out[targets, 32:40, :] = jnp.broadcast_to(
            tile.astype(BF16)[None], (8, 8, HEAD_WIDTH)
        )
    far_copy.wait()
    key_value_copy.wait()


def image_attend_kernel(
    place_ref,
    ceiling_ref,
    forget_ref,
    near_ref,
    far_ref,
    key_value_ref,
    weight_ref,
    scale_ref,
    columns,
    lanes,
    query_out,
    gate_out,
    inner_out,
    scaled,
    key_value,
    weight,
    query,
    sems,
):
    width = far_ref.shape[1]
    pieces = [
        (near_ref.at[at], scaled.at[:, columns_of(place_ref[0], step, 4, width)])
        for at, step in enumerate((0, 3, 1))
    ]
    pieces.append((far_ref, scaled.at[:, columns_of(place_ref[0], 2, 4, width)]))
    pieces += [
        (weight_ref.at[0], weight.at[0]),
        (weight_ref.at[1], weight.at[1]),
        (key_value_ref, key_value),
    ]
    copies = [
        pltpu.make_async_copy(source, target, sems.at[at])
        for at, (source, target) in enumerate(pieces)
    ]
    for copy in copies:
        copy.start()
    for copy in copies[:5]:
        copy.wait()
    scale = scale_ref[...]
    query[...] = (product(scaled, weight[0]) * scale).astype(BF16)
    copies[5].wait()
    gate_out[...] = silu_of(product(scaled, weight[1]) * scale)
    copies[6].wait()
    burst = jnp.log1p(jnp.full((1, 1), -forget_ref[place_ref[1]], F32))
    for head in range(4):
        attend(
            head,
            query,
            key_value.at[0],
            key_value.at[1],
            columns,
            lanes,
            ceiling_ref[head],
            burst,
            query_out,
            inner_out,
        )


def cost_of(rows, depth, width):
    return pl.CostEstimate(
        flops=2 * rows * depth * width, bytes_accessed=depth * width * 2, transcendentals=0
    )


def relay_kernel(source, out, blocks, sems):
    count, rows = blocks.shape[:2]
    copies = [
        pltpu.make_async_copy(source.at[pl.ds(at * rows, rows)], blocks.at[at], sems.at[at])
        for at in range(count)
    ]
    for copy in copies:
        copy.start()
    for at in range(count):
        copies[at].wait()
        out[:, at * rows : (at + 1) * rows, :] = jnp.swapaxes(blocks[at], 0, 1)


def relay_call(in_proj):
    depth, parts, width = in_proj.shape
    count = 8
    return pl.pallas_call(
        relay_kernel,
        out_shape=pltpu.VMEM((parts, depth, width), BF16),
        in_specs=[HBM],
        out_specs=VMEM,
        scratch_shapes=[
            pltpu.VMEM((count, depth // count, parts, width), BF16),
            pltpu.SemaphoreType.DMA((count,)),
        ],
        compiler_params=limit(20),
        cost_estimate=pl.CostEstimate(
            flops=0, bytes_accessed=2 * depth * parts * width, transcendentals=0
        ),
        name="relay",
    )(*in_hbm(in_proj))


def text_call(place, ceiling, chunks, gain, weights, decay):
    rows, width = chunks[0].shape
    depth = gain.shape[1]
    outs = (
        hbm_of(rows, width),
        hbm_of(rows, width),
        hbm_of(rows, width, dtype=F32),
        shape_of(32, 16, HEAD_WIDTH),
        shape_of(4, HEAD_WIDTH, dtype=F32),
        hbm_of(2, depth, width),
    )
    arrays = (*chunks, gain, weights, decay)
    return pl.pallas_call(
        text_kernel,
        grid=(1,),
        out_shape=outs,
        in_specs=[SMEM, SMEM] + [VMEM] * len(arrays),
        out_specs=tuple(fixed(*o.shape) for o in outs[:-1]) + (HBM,),
        scratch_shapes=[
            pltpu.VMEM((rows, depth), BF16),
            pltpu.VMEM((3, rows, width), BF16),
            pltpu.VMEM((rows, 4), F32),
            pltpu.VMEM((4, rows), F32),
            pltpu.SemaphoreType.DMA((2,)),
        ],
        compiler_params=limit(24, "arbitrary"),
        cost_estimate=cost_of(rows, depth, 4 * width),
        name="text_unit",
    )(place, ceiling, *arrays)


def image_near_call(place, near, gain, weights, decay):
    rows, width = near[0].shape
    outs = (
        hbm_of(3, rows, width),
        shape_of(2, rows, width, dtype=F32),
        shape_of(rows, HEAD_WIDTH, dtype=F32),
        shape_of(rows, 1, dtype=F32),
    )
    return pl.pallas_call(
        image_near_kernel,
        out_shape=outs,
        in_specs=[SMEM] + [VMEM] * 6,
        out_specs=(HBM,) + (VMEM,) * 3,
        scratch_shapes=[pltpu.VMEM((3, rows, width), BF16), pltpu.SemaphoreType.DMA((3,))],
        compiler_params=limit(16),
        cost_estimate=cost_of(rows, 3 * width, 2 * width),
        name="image_near",
    )(place, *near, gain, weights, decay)


def image_state_call(place, ceiling, forget, *arrays):
    half, width = arrays[0].shape
    rows = 2 * half
    outs = (
        hbm_of(rows, width),
        hbm_of(2, rows, width),
        shape_of(rows, 1, dtype=F32),
        shape_of(rows, 4, dtype=F32),
        shape_of(4, rows, dtype=F32),
        shape_of(32, 40, HEAD_WIDTH),
    )
    return pl.pallas_call(
        image_state_kernel,
        out_shape=outs,
        in_specs=[SMEM] * 3 + [VMEM] * len(arrays),
        out_specs=(HBM, HBM) + (VMEM,) * 4,
        scratch_shapes=[
            pltpu.VMEM((rows, width), BF16),
            pltpu.VMEM((2, rows, width), BF16),
            pltpu.SemaphoreType.DMA((2,)),
        ],
        compiler_params=limit(16),
        cost_estimate=cost_of(rows, width, 2 * width),
        name="image_state",
    )(place, ceiling, forget, *arrays)


def image_attend_call(place, ceiling, forget, weights, near, far, key_value, *small):
    rows, width = far.shape
    depth = 4 * width
    outs = (
        hbm_of(rows, width),
        hbm_of(rows, width),
        hbm_of(rows, width, dtype=F32),
    )
    return pl.pallas_call(
        image_attend_kernel,
        grid=(1,),
        out_shape=outs,
        in_specs=[SMEM] * 3 + [HBM] * 4 + [VMEM] * 3,
        out_specs=tuple(fixed(*o.shape) for o in outs),
        scratch_shapes=[
            pltpu.VMEM((rows, depth), BF16),
            pltpu.VMEM((2, rows, width), BF16),
            pltpu.VMEM((2, depth, width), BF16),
            pltpu.VMEM((rows, width), BF16),
            pltpu.SemaphoreType.DMA((7,)),
        ],
        compiler_params=limit(16, "arbitrary"),
        cost_estimate=cost_of(rows, depth, 2 * width),
        name="image_attend",
    )(place, ceiling, forget, *in_hbm(near, far, key_value, weights), *small)


def scan_kernel(start_ref, states, out, decay, image_at):
    count = start_ref.shape[0]
    for kind in range(2):
        spans = states[:, 32:40, :].astype(F32)
        span = spans[:, 2 * kind : 2 * kind + 1, :] + spans[:, 2 * kind + 1 : 2 * kind + 2, :]
        decay[:, kind] = jnp.broadcast_to(jnp.exp(span), (count, 16, HEAD_WIDTH))
    for position in range(2 * count):
        image_at[position] = -1
    for image in range(count):
        image_at[lax.shift_right_logical(start_ref[image], 1)] = image
    carry = jnp.zeros((16, HEAD_WIDTH), F32)
    texts = jnp.int32(0)
    for position in range(2 * count):
        found = image_at[position]
        kind = (found >= 0).astype(jnp.int32)
        source = jnp.where(found >= 0, found, jnp.minimum(texts, count - 1))
        texts += 1 - kind
        rows = pl.ds(pl.multiple_of(kind * 16, 16), 16)
        out[source, rows, :] = carry.astype(BF16)
        carry = decay[source, kind] * carry + states[source, rows, :].astype(F32)


def scan_call(starts, states):
    count = states.shape[0]
    return pl.pallas_call(
        scan_kernel,
        out_shape=shape_of(count, 32, HEAD_WIDTH),
        in_specs=[SMEM, VMEM],
        out_specs=VMEM,
        scratch_shapes=[
            pltpu.VMEM((count, 2, 16, HEAD_WIDTH), F32),
            pltpu.SMEM((2 * count,), jnp.int32),
        ],
        compiler_params=limit(6),
        name="state_scan",
    )(starts, states)


def gate_kernel(place_ref, entering, out_gain, out_proj, *refs):
    sources, (far_text, far_image, gated), buffers, sems = refs[:6], refs[6:9], refs[9:15], refs[15]
    copies = [
        pltpu.make_async_copy(source, buffer, sems.at[at])
        for at, (source, buffer) in enumerate(zip(sources, buffers))
    ]
    for copy in copies:
        copy.start()
    rows, width = far_text.shape
    for kind in range(2):
        for copy in copies[3 * kind : 3 * kind + 3]:
            copy.wait()
        query, gate, inner = buffers[3 * kind : 3 * kind + 3]
        for head in range(width // HEAD_WIDTH):
            lanes = slice(head * HEAD_WIDTH, (head + 1) * HEAD_WIDTH)
            state = entering[head * 8 : (head + 1) * 8, kind * 16 : (kind + 1) * 16, :]
            attended = inner[:, lanes] + jnp.dot(
                query[:, lanes], state.reshape(HEAD_WIDTH, HEAD_WIDTH), preferred_element_type=F32
            )
            scale = lax.rsqrt(jnp.mean(attended * attended, axis=-1, keepdims=True) + EPSILON)
            value = attended * scale * out_gain[head : head + 1, :] * gate[:, lanes].astype(F32)
            gated[kind * rows : (kind + 1) * rows, lanes] = value.astype(BF16)
    weight = out_proj[:, columns_of(place_ref[0], 2, 4, width)]
    block = jnp.dot(gated[...], weight, preferred_element_type=F32).astype(BF16)
    far_text[...] = block[:rows]
    far_image[...] = block[rows:]


def gate_call(place, entering, out_gain, out_proj, text_parts, image_parts):
    rows, width = text_parts[0].shape
    outs = (shape_of(rows, width), shape_of(rows, width), shape_of(2 * rows, width))
    parts = in_hbm(*text_parts, *image_parts)
    return pl.pallas_call(
        gate_kernel,
        out_shape=outs,
        in_specs=[SMEM] + [VMEM] * 3 + [HBM] * 6,
        out_specs=(VMEM,) * 3,
        scratch_shapes=[pltpu.VMEM(p.shape, p.dtype) for p in parts]
        + [pltpu.SemaphoreType.DMA((6,))],
        compiler_params=limit(16),
        name="gate_far",
    )(place, entering, out_gain, out_proj, *parts)


def near_kernel(place_ref, gated, out_proj, next_t, next_i, last_t, last_i, own_t, own_i):
    rows, width = next_t.shape
    for step, text, image in ((1, next_t, next_i), (3, last_t, last_i), (0, own_t, own_i)):
        weight = out_proj[:, columns_of(place_ref[0], step, 4, width)]
        block = jnp.dot(gated[...], weight, preferred_element_type=F32)
        text[...] = block[:rows].astype(text.dtype)
        image[...] = block[rows:].astype(image.dtype)


def near_call(place, gated, out_proj):
    rows, width = gated.shape[0] // 2, gated.shape[1]
    outs = (shape_of(rows, width),) * 4 + (shape_of(rows, width, dtype=F32),) * 2
    return pl.pallas_call(
        near_kernel,
        out_shape=outs,
        in_specs=[SMEM, VMEM, VMEM],
        out_specs=(VMEM,) * 6,
        compiler_params=limit(16),
        cost_estimate=cost_of(2 * rows, width, 3 * width),
        name="near_blocks",
    )(place, gated, out_proj)


def moved(array, step):
    return lax.ppermute(array, "head", [(i, (i + step) % 4) for i in range(4)])


def gathered(rows):
    half = rows.shape[0] // 2
    left = moved(rows, 1)
    right = moved(rows, 3)
    far_a = moved(left[:half], 1)
    far_b = moved(right[half:], 3)
    return (rows, left, right, far_a, far_b)


def added(one, two):
    return (one.astype(F32) + two.astype(F32)).astype(BF16)


def steps(
    image_patches,
    text_embed,
    image_start,
    image_forget,
    adapter,
    norm_gain,
    in_proj,
    decay_proj,
    head_decay_ceiling,
    out_gain,
    out_proj,
):
    place = jnp.stack([lax.axis_index("head"), lax.axis_index(SEQ)]).astype(jnp.int32)
    decay = decay_proj.T
    gain = norm_gain[None]
    ceiling = head_decay_ceiling

    text_chunks = gathered(text_embed)
    patches = image_patches.transpose(0, 2, 1)
    to_next, to_last, near_next, near_last = adapter_sums(place, patches, adapter)
    own = adapter_own(place, patches, adapter)
    weights = relay_call(in_proj)
    from_left = moved(to_next, 1)
    from_right = moved(to_last, 3)
    next_sum, last_sum = pass_call(from_left, from_right, near_next, near_last)
    left = moved(next_sum, 1)
    right = moved(last_sum, 3)
    embed = embed_call(own, from_left, from_right, left, right)
    image_chunks = gathered(embed)

    *text_parts, text_state, text_span, late_weights = text_call(
        place, ceiling, text_chunks, gain, weights, decay
    )
    near, *partial = image_near_call(place, image_chunks[:3], gain, weights, decay)
    *held, states = image_state_call(
        place,
        ceiling,
        image_forget,
        *image_chunks[3:],
        *partial,
        gain,
        weights,
        decay,
        text_state,
        text_span,
    )
    slices = lax.all_to_all(states, SEQ, 0, 0, tiled=True)
    image_parts = image_attend_call(
        place, ceiling, image_forget, late_weights, near, *held
    )
    entering = lax.all_to_all(scan_call(image_start, slices), SEQ, 0, 0, tiled=True)

    far_t, far_i, gated = gate_call(
        place, entering, out_gain, out_proj, text_parts, image_parts
    )
    next_t, next_i, last_t, last_i, own_t, own_i = near_call(place, gated, out_proj)
    far_from_left = moved(far_t, 1)
    far_from_right = moved(far_i, 3)
    left_i = moved(next_i, 1)
    right_t = moved(last_t, 3)
    left_t = moved(added(next_t, far_from_left), 1)
    right_i = moved(added(last_i, far_from_right), 3)
    text_out = text_embed.astype(F32) + (own_t + left_t.astype(F32) + right_t.astype(F32))
    image_out = embed.astype(F32) + (own_i + left_i.astype(F32) + right_i.astype(F32))
    return (image_out.astype(BF16)[None], text_out.astype(BF16))


def solution(mesh):
    split = Mesh(
        mesh.devices.reshape(4, 4, 2, mesh.shape["head"]), ("seq_0", "seq_1", "seq_2", "head")
    )
    return jax.shard_map(
        steps,
        mesh=split,
        in_specs=(
            P(SEQ, None, "head"),
            P(SEQ, "head"),
            P(),
            P(),
            P("head", None),
            P(),
            P(None, None, "head"),
            P(None, "head"),
            P("head"),
            P("head", None),
            P("head", None),
        ),
        out_specs=(P(SEQ, None, "head"), P(SEQ, "head")),
        check_vma=False,
    )
```

```python
import jax
import jax.numpy as jnp
from jax import lax
from jax.experimental import pallas as pl
from jax.experimental.pallas import tpu as pltpu
from jax.sharding import Mesh
from jax.sharding import PartitionSpec as P

SEQ = ("seq_0", "seq_1", "seq_2")
EPSILON = 1e-06
F32 = jnp.float32
BF16 = jnp.bfloat16
HEAD_WIDTH = 128


VMEM = pl.BlockSpec(memory_space=pltpu.VMEM)
SMEM = pl.BlockSpec(memory_space=pltpu.SMEM)
HBM = pl.BlockSpec(memory_space=pltpu.HBM)


def shape_of(*dims, dtype=BF16):
    return jax.ShapeDtypeStruct(dims, dtype)


def hbm_of(*dims, dtype=BF16):
    return pltpu.HBM(dims, dtype)


def in_hbm(*arrays):
    return [pltpu.with_memory_space_constraint(a, pltpu.HBM) for a in arrays]


def limit(mebibytes, *semantics):
    return pltpu.CompilerParams(
        dimension_semantics=semantics or None, vmem_limit_bytes=mebibytes << 20
    )


def fixed(*dims):
    return pl.BlockSpec(dims, lambda *_: (0,) * len(dims))


def columns_of(place_ref, slot, width):
    return pl.ds(pl.multiple_of(place_ref[slot] * width, width), width)


def adapter_blocks(place_ref, patches_ref, adapter_ref, patches, blocks, sems, slots):
    patches_copy = pltpu.make_async_copy(patches_ref.at[0], patches, sems.at[0])
    patches_copy.start()
    copies = []
    for at, slot in enumerate(slots):
        columns = columns_of(place_ref, slot, blocks.shape[2])
        copies.append(
            pltpu.make_async_copy(adapter_ref.at[:, columns], blocks.at[at], sems.at[at + 1])
        )
        copies[at].start()
    patches_copy.wait()
    rows = patches[...].T
    for at in range(len(slots)):
        copies[at].wait()
        yield jnp.dot(rows, blocks[at], preferred_element_type=F32)


def leave_kernel(place_ref, patches_ref, adapter_ref, out, *scratch):
    rows = out.shape[0] // 2
    for at, block in enumerate(adapter_blocks(place_ref, patches_ref, adapter_ref, *scratch, (1, 3))):
        out[at * rows : (at + 1) * rows] = block.astype(BF16)


def stay_kernel(place_ref, patches_ref, adapter_ref, out, *scratch):
    for at, block in enumerate(adapter_blocks(place_ref, patches_ref, adapter_ref, *scratch, (2, 0))):
        out[at] = block


def adapter_call(kernel, outs, count, place, patches, adapter):
    depth, rows = patches.shape[1:]
    return pl.pallas_call(
        kernel,
        out_shape=outs,
        in_specs=[SMEM, HBM, HBM],
        out_specs=jax.tree.map(lambda _: VMEM, outs),
        scratch_shapes=[
            pltpu.VMEM((depth, rows), BF16),
            pltpu.VMEM((count, depth, adapter.shape[1] // 4), BF16),
            pltpu.SemaphoreType.DMA((count + 1,)),
        ],
        compiler_params=limit(8),
        cost_estimate=cost_of(rows, depth, count * adapter.shape[1] // 4),
    )(place, *in_hbm(patches, adapter))


def adapter_leave(*arrays):
    rows, width = arrays[1].shape[2], arrays[2].shape[1] // 4
    return adapter_call(leave_kernel, shape_of(2 * rows, width), 2, *arrays)


def adapter_stay(*arrays):
    rows, width = arrays[1].shape[2], arrays[2].shape[1] // 4
    outs = shape_of(2, rows, width, dtype=F32)
    return adapter_call(stay_kernel, outs, 2, *arrays)


def small_call(kernel, out, *arrays):
    return pl.pallas_call(
        kernel,
        out_shape=out,
        in_specs=[VMEM] * len(arrays),
        out_specs=VMEM,
        compiler_params=limit(4),
    )(*arrays)


def pass_kernel(stay, arrived, out):
    rows = out.shape[0]
    out[...] = (stay[0] + arrived[rows:].astype(F32)).astype(BF16)


def embed_kernel(stay, arrived, last, out):
    rows = out.shape[0]
    out[...] = (stay[1] + arrived[:rows].astype(F32) + last[...].astype(F32)).astype(BF16)


def join_kernel(one, two, out):
    rows = one.shape[0]
    out[:rows] = one[...]
    out[rows:] = two[...]


def normalize(place_ref, chunks, gain_ref, normed):
    own, first, others = chunks
    rows, width = own.shape
    values = (own[...], first[...], others[:rows], others[rows:])
    total = 0.0
    for value in values:
        value = value.astype(F32)
        total += jnp.sum(value * value, axis=-1, keepdims=True)
    scale = lax.rsqrt(total / (4 * width) + EPSILON)
    for slot, value in enumerate(values):
        columns = columns_of(place_ref, slot, width)
        normed[:, columns] = (value.astype(F32) * scale * gain_ref[:, columns]).astype(BF16)


def product(normed, weight):
    return jnp.dot(normed[...], weight, preferred_element_type=F32)


def decay_logits(values, decay):
    decay = jnp.concatenate([decay.astype(F32)] * 4, axis=0).astype(BF16)
    decay = jnp.concatenate([decay, jnp.zeros((HEAD_WIDTH - 16, decay.shape[1]), BF16)], axis=0)
    return lax.dot_general(values, decay, (((1,), (1,)), ((), ())), preferred_element_type=F32)


def decay_sums(logits, columns, lanes):
    rows = logits.shape[0]
    gates = jax.nn.sigmoid(logits)
    ids = lax.broadcasted_iota(jnp.int32, gates.shape, 1)
    upper = gates.astype(BF16).astype(F32)
    middle = (gates - upper).astype(BF16).astype(F32)
    terms = jnp.where(ids < 4, upper, jnp.where(ids < 8, middle, gates - upper - middle))
    row_ids = lax.broadcasted_iota(jnp.int32, (rows, rows), 0)
    column_ids = lax.broadcasted_iota(jnp.int32, (rows, rows), 1)
    sums = jnp.dot(
        (row_ids >= column_ids).astype(BF16), terms.astype(BF16), preferred_element_type=F32
    )
    columns[...] = sums[:, 0:4] + sums[:, 4:8] + sums[:, 8:12]
    by_row = sums.T
    lanes[...] = by_row[0:4] + by_row[4:8] + by_row[8:12]


def silu_of(gates):
    gates = gates.astype(BF16).astype(F32)
    return (gates * jax.nn.sigmoid(gates)).astype(BF16)


def chunk_state(head, key, value, columns, ceiling, burst):
    rows = columns.shape[0]
    lanes = slice(head * HEAD_WIDTH, (head + 1) * HEAD_WIDTH)
    column = columns[:, head : head + 1]
    last = columns[rows - 1 :, head : head + 1]
    weighted = key[:, lanes].astype(F32) * jnp.exp(ceiling * (column - last))
    state = lax.dot_general(
        weighted.astype(BF16), value[:, lanes], (((0,), (0,)), ((), ())), preferred_element_type=F32
    )
    return state.astype(BF16).reshape(8, 16, HEAD_WIDTH), burst - ceiling * last


def attend(head, query, key, value, columns, lanes_ref, ceiling, burst, query_out, inner_out):
    rows = columns.shape[0]
    lanes = slice(head * HEAD_WIDTH, (head + 1) * HEAD_WIDTH)
    column = columns[:, head : head + 1]
    lagged = ceiling * (lanes_ref[head : head + 1, :] - column)
    row_ids = lax.broadcasted_iota(jnp.int32, (rows, rows), 0)
    column_ids = lax.broadcasted_iota(jnp.int32, (rows, rows), 1)
    scores = lax.dot_general(
        query[:, lanes], key[:, lanes], (((1,), (1,)), ((), ())), preferred_element_type=F32
    )
    weights = jnp.where(row_ids >= column_ids, scores * jnp.exp(jnp.minimum(lagged, 0.0)), 0.0)
    inner_out[:, lanes] = jnp.dot(weights.astype(BF16), value[:, lanes], preferred_element_type=F32)
    entry = jnp.exp(burst - ceiling * column)
    query_out[:, lanes] = (query[:, lanes].astype(F32) * entry).astype(BF16)


def text_kernel(
    place_ref,
    ceiling_ref,
    own,
    first,
    others,
    gain_ref,
    weight,
    decay_ref,
    query_out,
    gate_out,
    inner_out,
    state_out,
    span_out,
    late_out,
    normed,
    parts,
    columns,
    lanes,
    sems,
):
    copies = [
        pltpu.make_async_copy(weight.at[3 * at], late_out.at[at], sems.at[at]) for at in range(2)
    ]
    for copy in copies:
        copy.start()
    normalize(place_ref, (own, first, others), gain_ref, normed)
    decay_sums(decay_logits(normed[...], decay_ref[...]), columns, lanes)
    for part in range(3):
        parts[part] = product(normed, weight[part]).astype(BF16)
    gate_out[...] = silu_of(product(normed, weight[3]))
    for head in range(4):
        ceiling = ceiling_ref[head]
        state, span = chunk_state(head, parts.at[1], parts.at[2], columns, ceiling, 0.0)
        state_out[head * 8 : (head + 1) * 8] = state
        span_out[head : head + 1] = jnp.broadcast_to(span, (1, HEAD_WIDTH))
        attend(
            head,
            parts.at[0],
            parts.at[1],
            parts.at[2],
            columns,
            lanes,
            ceiling,
            0.0,
            query_out,
            inner_out,
        )
    for copy in copies:
        copy.wait()


def image_near_kernel(
    place_ref, own, first, gain_ref, weight, decay_ref, scaled_out, total, logits, squares, scaled, sems
):
    copies = []
    for at, ref in enumerate((own, first)):
        columns = columns_of(place_ref, at, own.shape[1])
        value = ref[...].astype(F32)
        square = jnp.sum(value * value, axis=-1, keepdims=True)
        small = (value * gain_ref[:, columns]).astype(BF16)
        scaled[at] = small
        gates = decay_logits(small, decay_ref[:, columns])
        terms = [
            jnp.dot(small, weight[part, columns, :], preferred_element_type=F32)
            for part in (1, 2)
        ]
        copies.append(pltpu.make_async_copy(scaled.at[at], scaled_out.at[at], sems.at[at]))
        copies[at].start()
        if at == 0:
            squares[...], logits[...], total[0], total[1] = square, gates, *terms
        else:
            squares[...] += square
            logits[...] += gates
            total[0] += terms[0]
            total[1] += terms[1]
    for copy in copies:
        copy.wait()


def image_state_kernel(
    place_ref,
    ceiling_ref,
    forget_ref,
    others,
    total,
    logits,
    squares,
    gain_ref,
    weight,
    decay_ref,
    other_state,
    other_span,
    far_out,
    key_value_out,
    scale_out,
    columns,
    lanes,
    state_out,
    scaled,
    key_value,
    sems,
):
    rows, width = others.shape[0] // 2, others.shape[1]
    square = squares[...]
    chunks = []
    for at in range(2):
        chunks.append(columns_of(place_ref, at + 2, width))
        value = others[at * rows : (at + 1) * rows].astype(F32)
        square += jnp.sum(value * value, axis=-1, keepdims=True)
        scaled[at] = (value * gain_ref[:, chunks[at]]).astype(BF16)
    scale = lax.rsqrt(square / (4 * width) + EPSILON)
    scale_out[...] = scale
    for at in range(2):
        term = total[at]
        for place, chunk in enumerate(chunks):
            term += jnp.dot(scaled[place], weight[at + 1, chunk, :], preferred_element_type=F32)
        key_value[at] = (term * scale).astype(BF16)
    far_copy = pltpu.make_async_copy(scaled, far_out, sems.at[0])
    far_copy.start()
    gates = logits[...]
    for place, chunk in enumerate(chunks):
        gates += decay_logits(scaled[place], decay_ref[:, chunk])
    decay_sums(gates * scale, columns, lanes)
    key_value_copy = pltpu.make_async_copy(key_value, key_value_out, sems.at[1])
    key_value_copy.start()
    state_out[:, 0:16, :] = other_state[...]
    burst = jnp.log1p(jnp.full((1, 1), -forget_ref[place_ref[4]], F32))
    ids = lax.broadcasted_iota(jnp.int32, (8, HEAD_WIDTH), 0)
    for head in range(4):
        state, span = chunk_state(
            head, key_value.at[0], key_value.at[1], columns, ceiling_ref[head], burst
        )
        targets = slice(head * 8, (head + 1) * 8)
        state_out[targets, 16:32, :] = state
        tile = jnp.zeros((8, HEAD_WIDTH), F32)
        for kind, value in enumerate((other_span[head : head + 1, 0:1], span)):
            upper = value.astype(BF16).astype(F32)
            tile = jnp.where(ids == 2 * kind, upper, tile)
            tile = jnp.where(ids == 2 * kind + 1, value - upper, tile)
        state_out[targets, 32:40, :] = jnp.broadcast_to(
            tile.astype(BF16)[None], (8, 8, HEAD_WIDTH)
        )
    far_copy.wait()
    key_value_copy.wait()


def image_attend_kernel(
    place_ref,
    ceiling_ref,
    forget_ref,
    near_ref,
    far_ref,
    key_value_ref,
    weight_ref,
    scale_ref,
    columns,
    lanes,
    query_out,
    gate_out,
    inner_out,
    scaled,
    key_value,
    weight,
    query,
    sems,
):
    width = far_ref.shape[2]
    pieces = []
    for slot in range(4):
        ref = (near_ref, far_ref)[slot // 2]
        pieces.append((ref.at[slot % 2], scaled.at[:, columns_of(place_ref, slot, width)]))
    pieces += [
        (weight_ref.at[0], weight.at[0]),
        (weight_ref.at[1], weight.at[1]),
        (key_value_ref, key_value),
    ]
    copies = [
        pltpu.make_async_copy(source, target, sems.at[at])
        for at, (source, target) in enumerate(pieces)
    ]
    for copy in copies:
        copy.start()
    for copy in copies[:5]:
        copy.wait()
    scale = scale_ref[...]
    query[...] = (product(scaled, weight[0]) * scale).astype(BF16)
    copies[5].wait()
    gate_out[...] = silu_of(product(scaled, weight[1]) * scale)
    copies[6].wait()
    burst = jnp.log1p(jnp.full((1, 1), -forget_ref[place_ref[4]], F32))
    for head in range(4):
        attend(
            head,
            query,
            key_value.at[0],
            key_value.at[1],
            columns,
            lanes,
            ceiling_ref[head],
            burst,
            query_out,
            inner_out,
        )


def cost_of(rows, depth, width):
    return pl.CostEstimate(
        flops=2 * rows * depth * width, bytes_accessed=depth * width * 2, transcendentals=0
    )


def relay_kernel(source, out, blocks, sems):
    count, rows = blocks.shape[:2]
    copies = [
        pltpu.make_async_copy(source.at[pl.ds(at * rows, rows)], blocks.at[at], sems.at[at])
        for at in range(count)
    ]
    for copy in copies:
        copy.start()
    for at in range(count):
        copies[at].wait()
        out[:, at * rows : (at + 1) * rows, :] = jnp.swapaxes(blocks[at], 0, 1)


def relay_call(in_proj):
    depth, parts, width = in_proj.shape
    count = 8
    return pl.pallas_call(
        relay_kernel,
        out_shape=pltpu.VMEM((parts, depth, width), BF16),
        in_specs=[HBM],
        out_specs=VMEM,
        scratch_shapes=[
            pltpu.VMEM((count, depth // count, parts, width), BF16),
            pltpu.SemaphoreType.DMA((count,)),
        ],
        compiler_params=limit(20),
        cost_estimate=pl.CostEstimate(
            flops=0, bytes_accessed=2 * depth * parts * width, transcendentals=0
        ),
        name="relay",
    )(*in_hbm(in_proj))


def text_call(place, ceiling, chunks, gain, weights, decay):
    rows, width = chunks[0].shape
    depth = gain.shape[1]
    outs = (
        hbm_of(rows, width),
        hbm_of(rows, width),
        hbm_of(rows, width, dtype=F32),
        shape_of(32, 16, HEAD_WIDTH),
        shape_of(4, HEAD_WIDTH, dtype=F32),
        hbm_of(2, depth, width),
    )
    arrays = (*chunks, gain, weights, decay)
    return pl.pallas_call(
        text_kernel,
        grid=(1,),
        out_shape=outs,
        in_specs=[SMEM, SMEM] + [VMEM] * len(arrays),
        out_specs=tuple(fixed(*o.shape) for o in outs[:-1]) + (HBM,),
        scratch_shapes=[
            pltpu.VMEM((rows, depth), BF16),
            pltpu.VMEM((3, rows, width), BF16),
            pltpu.VMEM((rows, 4), F32),
            pltpu.VMEM((4, rows), F32),
            pltpu.SemaphoreType.DMA((2,)),
        ],
        compiler_params=limit(24, "arbitrary"),
        cost_estimate=cost_of(rows, depth, 4 * width),
        name="text_unit",
    )(place, ceiling, *arrays)


def image_near_call(place, near, gain, weights, decay):
    rows, width = near[0].shape
    outs = (
        hbm_of(2, rows, width),
        shape_of(2, rows, width, dtype=F32),
        shape_of(rows, HEAD_WIDTH, dtype=F32),
        shape_of(rows, 1, dtype=F32),
    )
    return pl.pallas_call(
        image_near_kernel,
        out_shape=outs,
        in_specs=[SMEM] + [VMEM] * 5,
        out_specs=(HBM,) + (VMEM,) * 3,
        scratch_shapes=[pltpu.VMEM((2, rows, width), BF16), pltpu.SemaphoreType.DMA((2,))],
        compiler_params=limit(16),
        cost_estimate=cost_of(rows, 2 * width, 2 * width),
        name="image_near",
    )(place, *near, gain, weights, decay)


def image_state_call(place, ceiling, forget, *arrays):
    rows, width = arrays[0].shape[0] // 2, arrays[0].shape[1]
    outs = (
        hbm_of(2, rows, width),
        hbm_of(2, rows, width),
        shape_of(rows, 1, dtype=F32),
        shape_of(rows, 4, dtype=F32),
        shape_of(4, rows, dtype=F32),
        shape_of(32, 40, HEAD_WIDTH),
    )
    return pl.pallas_call(
        image_state_kernel,
        out_shape=outs,
        in_specs=[SMEM] * 3 + [VMEM] * len(arrays),
        out_specs=(HBM, HBM) + (VMEM,) * 4,
        scratch_shapes=[
            pltpu.VMEM((2, rows, width), BF16),
            pltpu.VMEM((2, rows, width), BF16),
            pltpu.SemaphoreType.DMA((2,)),
        ],
        compiler_params=limit(16),
        cost_estimate=cost_of(rows, width, 2 * width),
        name="image_state",
    )(place, ceiling, forget, *arrays)


def image_attend_call(place, ceiling, forget, weights, near, far, key_value, *small):
    rows, width = far.shape[1:]
    depth = 4 * width
    outs = (
        hbm_of(rows, width),
        hbm_of(rows, width),
        hbm_of(rows, width, dtype=F32),
    )
    return pl.pallas_call(
        image_attend_kernel,
        grid=(1,),
        out_shape=outs,
        in_specs=[SMEM] * 3 + [HBM] * 4 + [VMEM] * 3,
        out_specs=tuple(fixed(*o.shape) for o in outs),
        scratch_shapes=[
            pltpu.VMEM((rows, depth), BF16),
            pltpu.VMEM((2, rows, width), BF16),
            pltpu.VMEM((2, depth, width), BF16),
            pltpu.VMEM((rows, width), BF16),
            pltpu.SemaphoreType.DMA((7,)),
        ],
        compiler_params=limit(16, "arbitrary"),
        cost_estimate=cost_of(rows, depth, 2 * width),
        name="image_attend",
    )(place, ceiling, forget, *in_hbm(near, far, key_value, weights), *small)


def scan_kernel(start_ref, states, out, decay, image_at):
    count = start_ref.shape[0]
    for kind in range(2):
        spans = states[:, 32:40, :].astype(F32)
        span = spans[:, 2 * kind : 2 * kind + 1, :] + spans[:, 2 * kind + 1 : 2 * kind + 2, :]
        decay[:, kind] = jnp.broadcast_to(jnp.exp(span), (count, 16, HEAD_WIDTH))
    for position in range(2 * count):
        image_at[position] = -1
    for image in range(count):
        image_at[lax.shift_right_logical(start_ref[image], 1)] = image
    carry = jnp.zeros((16, HEAD_WIDTH), F32)
    texts = jnp.int32(0)
    for position in range(2 * count):
        found = image_at[position]
        kind = (found >= 0).astype(jnp.int32)
        source = jnp.where(found >= 0, found, jnp.minimum(texts, count - 1))
        texts += 1 - kind
        rows = pl.ds(pl.multiple_of(kind * 16, 16), 16)
        out[source, rows, :] = carry.astype(BF16)
        carry = decay[source, kind] * carry + states[source, rows, :].astype(F32)


def scan_call(starts, states):
    count = states.shape[0]
    return pl.pallas_call(
        scan_kernel,
        out_shape=shape_of(count, 32, HEAD_WIDTH),
        in_specs=[SMEM, VMEM],
        out_specs=VMEM,
        scratch_shapes=[
            pltpu.VMEM((count, 2, 16, HEAD_WIDTH), F32),
            pltpu.SMEM((2 * count,), jnp.int32),
        ],
        compiler_params=limit(6),
        name="state_scan",
    )(starts, states)


def gate_kernel(place_ref, entering, out_gain, out_proj, *refs):
    sources, (leave_t, leave_i, gated), buffers, sems = refs[:6], refs[6:9], refs[9:15], refs[15]
    copies = [
        pltpu.make_async_copy(source, buffer, sems.at[at])
        for at, (source, buffer) in enumerate(zip(sources, buffers))
    ]
    for copy in copies:
        copy.start()
    rows, width = leave_t.shape[0] // 2, leave_t.shape[1]
    for kind in range(2):
        for copy in copies[3 * kind : 3 * kind + 3]:
            copy.wait()
        query, gate, inner = buffers[3 * kind : 3 * kind + 3]
        for head in range(width // HEAD_WIDTH):
            lanes = slice(head * HEAD_WIDTH, (head + 1) * HEAD_WIDTH)
            state = entering[head * 8 : (head + 1) * 8, kind * 16 : (kind + 1) * 16, :]
            attended = inner[:, lanes] + jnp.dot(
                query[:, lanes], state.reshape(HEAD_WIDTH, HEAD_WIDTH), preferred_element_type=F32
            )
            scale = lax.rsqrt(jnp.mean(attended * attended, axis=-1, keepdims=True) + EPSILON)
            value = attended * scale * out_gain[head : head + 1, :] * gate[:, lanes].astype(F32)
            gated[kind * rows : (kind + 1) * rows, lanes] = value.astype(BF16)
    for at, slot in enumerate((1, 3)):
        weight = out_proj[:, columns_of(place_ref, slot, width)]
        block = jnp.dot(gated[...], weight, preferred_element_type=F32).astype(BF16)
        leave_t[at * rows : (at + 1) * rows] = block[:rows]
        leave_i[at * rows : (at + 1) * rows] = block[rows:]


def gate_call(place, entering, out_gain, out_proj, text_parts, image_parts):
    rows, width = text_parts[0].shape
    outs = (shape_of(2 * rows, width),) * 3
    parts = in_hbm(*text_parts, *image_parts)
    return pl.pallas_call(
        gate_kernel,
        out_shape=outs,
        in_specs=[SMEM] + [VMEM] * 3 + [HBM] * 6,
        out_specs=(VMEM,) * 3,
        scratch_shapes=[pltpu.VMEM(p.shape, p.dtype) for p in parts]
        + [pltpu.SemaphoreType.DMA((6,))],
        compiler_params=limit(16),
        name="gate_leave",
    )(place, entering, out_gain, out_proj, *parts)


def stay_blocks_kernel(place_ref, gated, out_proj, pass_t, pass_i, own_t, own_i):
    rows, width = own_t.shape
    for slot, text, image in ((2, pass_t, pass_i), (0, own_t, own_i)):
        weight = out_proj[:, columns_of(place_ref, slot, width)]
        block = jnp.dot(gated[...], weight, preferred_element_type=F32)
        text[...] = block[:rows]
        image[...] = block[rows:]


def stay_call(place, gated, out_proj):
    rows, width = gated.shape[0] // 2, gated.shape[1]
    return pl.pallas_call(
        stay_blocks_kernel,
        out_shape=(shape_of(rows, width, dtype=F32),) * 4,
        in_specs=[SMEM, VMEM, VMEM],
        out_specs=(VMEM,) * 4,
        compiler_params=limit(16),
        cost_estimate=cost_of(2 * rows, width, 2 * width),
        name="stay_blocks",
    )(place, gated, out_proj)


def moved(array, turn):
    pairs = []
    for core in range(2):
        for x in range(4):
            partner = x ^ 1 if (core + turn) % 2 == 0 else 3 - x
            pairs.append((4 * core + x, 4 * core + partner))
    return lax.ppermute(array, ("seq_2", "head"), pairs)


def gathered(rows):
    first = moved(rows, 0)
    joined = small_call(join_kernel, shape_of(2 * rows.shape[0], rows.shape[1]), rows, first)
    return (rows, first, moved(joined, 1))


def added(one, two):
    return (one.astype(F32) + two.astype(F32)).astype(BF16)


def steps(
    image_patches,
    text_embed,
    image_start,
    image_forget,
    adapter,
    norm_gain,
    in_proj,
    decay_proj,
    head_decay_ceiling,
    out_gain,
    out_proj,
):
    x = lax.axis_index("head")
    even = lax.axis_index("seq_2") == 0
    first, second = jnp.where(even, x ^ 1, 3 - x), jnp.where(even, 3 - x, x ^ 1)
    place = jnp.stack([x, first, second, x ^ 2, lax.axis_index(SEQ)]).astype(jnp.int32)
    decay = decay_proj.T
    gain = norm_gain[None]
    ceiling = head_decay_ceiling

    text_chunks = gathered(text_embed)
    patches = image_patches.transpose(0, 2, 1)
    leaving = adapter_leave(place, patches, adapter)
    stay = adapter_stay(place, patches, adapter)
    weights = relay_call(in_proj)
    block = shape_of(*text_embed.shape)
    arrived = moved(leaving, 0)
    last = moved(small_call(pass_kernel, block, stay, arrived), 1)
    embed = small_call(embed_kernel, block, stay, arrived, last)
    image_chunks = gathered(embed)

    *text_parts, text_state, text_span, late_weights = text_call(
        place, ceiling, text_chunks, gain, weights, decay
    )
    near, *partial = image_near_call(place, image_chunks[:2], gain, weights, decay)
    *held, states = image_state_call(
        place,
        ceiling,
        image_forget,
        image_chunks[2],
        *partial,
        gain,
        weights,
        decay,
        text_state,
        text_span,
    )
    slices = lax.all_to_all(states, SEQ, 0, 0, tiled=True)
    image_parts = image_attend_call(
        place, ceiling, image_forget, late_weights, near, *held
    )
    entering = lax.all_to_all(scan_call(image_start, slices), SEQ, 0, 0, tiled=True)

    leave_t, leave_i, gated = gate_call(
        place, entering, out_gain, out_proj, text_parts, image_parts
    )
    pass_t, pass_i, own_t, own_i = stay_call(place, gated, out_proj)
    rows = own_t.shape[0]
    arrived_t = moved(leave_t, 0)
    arrived_i = moved(leave_i, 0)
    last_t = moved(added(pass_t, arrived_t[rows:]), 1)
    last_i = moved(added(pass_i, arrived_i[rows:]), 1)
    text_out = text_embed.astype(F32) + (own_t + arrived_t[:rows].astype(F32) + last_t.astype(F32))
    image_out = embed.astype(F32) + (own_i + arrived_i[:rows].astype(F32) + last_i.astype(F32))
    return (image_out.astype(BF16)[None], text_out.astype(BF16))


def solution(mesh):
    split = Mesh(
        mesh.devices.reshape(4, 4, 2, mesh.shape["head"]), ("seq_0", "seq_1", "seq_2", "head")
    )
    return jax.shard_map(
        steps,
        mesh=split,
        in_specs=(
            P(SEQ, None, "head"),
            P(SEQ, "head"),
            P(),
            P(),
            P("head", None),
            P(),
            P(None, None, "head"),
            P(None, "head"),
            P("head"),
            P("head", None),
            P("head", None),
        ),
        out_specs=(P(SEQ, None, "head"), P(SEQ, "head")),
        check_vma=False,
    )
```

```python
import jax
import jax.numpy as jnp
from jax import lax
from jax.experimental import pallas as pl
from jax.experimental.pallas import tpu as pltpu
from jax.sharding import Mesh
from jax.sharding import PartitionSpec as P

SEQ = ("seq_0", "seq_1", "seq_2")
EPSILON = 1e-06
F32 = jnp.float32
BF16 = jnp.bfloat16
HEAD_WIDTH = 128


VMEM = pl.BlockSpec(memory_space=pltpu.VMEM)
SMEM = pl.BlockSpec(memory_space=pltpu.SMEM)
HBM = pl.BlockSpec(memory_space=pltpu.HBM)


def shape_of(*dims, dtype=BF16):
    return jax.ShapeDtypeStruct(dims, dtype)


def hbm_of(*dims, dtype=BF16):
    return pltpu.HBM(dims, dtype)


def in_hbm(*arrays):
    return [pltpu.with_memory_space_constraint(a, pltpu.HBM) for a in arrays]


def limit(mebibytes, *semantics):
    return pltpu.CompilerParams(
        dimension_semantics=semantics or None, vmem_limit_bytes=mebibytes << 20
    )


def fixed(*dims):
    return pl.BlockSpec(dims, lambda *_: (0,) * len(dims))


def columns_of(place_ref, slot, width):
    return pl.ds(pl.multiple_of(place_ref[slot] * width, width), width)


def ring_columns(place_ref, step, width):
    return pl.ds(pl.multiple_of(lax.rem(place_ref[0] + step, 4) * width, width), width)


def adapter_blocks(place_ref, patches_ref, adapter_ref, patches, blocks, sems, slots):
    patches_copy = pltpu.make_async_copy(patches_ref.at[0], patches, sems.at[0])
    patches_copy.start()
    copies = []
    for at, slot in enumerate(slots):
        columns = columns_of(place_ref, slot, blocks.shape[2])
        copies.append(
            pltpu.make_async_copy(adapter_ref.at[:, columns], blocks.at[at], sems.at[at + 1])
        )
        copies[at].start()
    patches_copy.wait()
    rows = patches[...].T
    for at in range(len(slots)):
        copies[at].wait()
        yield jnp.dot(rows, blocks[at], preferred_element_type=F32)


def leave_kernel(place_ref, patches_ref, adapter_ref, out, *scratch):
    rows = out.shape[0] // 2
    for at, block in enumerate(adapter_blocks(place_ref, patches_ref, adapter_ref, *scratch, (1, 3))):
        out[at * rows : (at + 1) * rows] = block.astype(BF16)


def stay_kernel(place_ref, patches_ref, adapter_ref, out, *scratch):
    for at, block in enumerate(adapter_blocks(place_ref, patches_ref, adapter_ref, *scratch, (2, 0))):
        out[at] = block


def adapter_call(kernel, outs, count, place, patches, adapter):
    depth, rows = patches.shape[1:]
    return pl.pallas_call(
        kernel,
        out_shape=outs,
        in_specs=[SMEM, HBM, HBM],
        out_specs=jax.tree.map(lambda _: VMEM, outs),
        scratch_shapes=[
            pltpu.VMEM((depth, rows), BF16),
            pltpu.VMEM((count, depth, adapter.shape[1] // 4), BF16),
            pltpu.SemaphoreType.DMA((count + 1,)),
        ],
        compiler_params=limit(8),
        cost_estimate=cost_of(rows, depth, count * adapter.shape[1] // 4),
    )(place, *in_hbm(patches, adapter))


def adapter_leave(*arrays):
    rows, width = arrays[1].shape[2], arrays[2].shape[1] // 4
    return adapter_call(leave_kernel, shape_of(2 * rows, width), 2, *arrays)


def adapter_stay(*arrays):
    rows, width = arrays[1].shape[2], arrays[2].shape[1] // 4
    outs = shape_of(2, rows, width, dtype=F32)
    return adapter_call(stay_kernel, outs, 2, *arrays)


def small_call(kernel, out, *arrays):
    return pl.pallas_call(
        kernel,
        out_shape=out,
        in_specs=[VMEM] * len(arrays),
        out_specs=VMEM,
        compiler_params=limit(4),
    )(*arrays)


def pass_kernel(stay, arrived, out):
    rows = out.shape[0]
    out[...] = (stay[0] + arrived[rows:].astype(F32)).astype(BF16)


def embed_kernel(stay, arrived, last, out):
    rows = out.shape[0]
    out[...] = (stay[1] + arrived[:rows].astype(F32) + last[...].astype(F32)).astype(BF16)


def join_kernel(one, two, out):
    rows = one.shape[0]
    out[:rows] = one[...]
    out[rows:] = two[...]


def normalize(place_ref, chunks, gain_ref, normed):
    own, first, others = chunks
    rows, width = own.shape
    values = (own[...], first[...], others[:rows], others[rows:])
    total = 0.0
    for value in values:
        value = value.astype(F32)
        total += jnp.sum(value * value, axis=-1, keepdims=True)
    scale = lax.rsqrt(total / (4 * width) + EPSILON)
    for slot, value in enumerate(values):
        columns = columns_of(place_ref, slot, width)
        normed[:, columns] = (value.astype(F32) * scale * gain_ref[:, columns]).astype(BF16)


def product(normed, weight):
    return jnp.dot(normed[...], weight, preferred_element_type=F32)


def decay_logits(values, decay):
    decay = jnp.concatenate([decay.astype(F32)] * 4, axis=0).astype(BF16)
    decay = jnp.concatenate([decay, jnp.zeros((HEAD_WIDTH - 16, decay.shape[1]), BF16)], axis=0)
    return lax.dot_general(values, decay, (((1,), (1,)), ((), ())), preferred_element_type=F32)


def decay_sums(logits, columns, lanes):
    rows = logits.shape[0]
    gates = jax.nn.sigmoid(logits)
    ids = lax.broadcasted_iota(jnp.int32, gates.shape, 1)
    upper = gates.astype(BF16).astype(F32)
    middle = (gates - upper).astype(BF16).astype(F32)
    terms = jnp.where(ids < 4, upper, jnp.where(ids < 8, middle, gates - upper - middle))
    row_ids = lax.broadcasted_iota(jnp.int32, (rows, rows), 0)
    column_ids = lax.broadcasted_iota(jnp.int32, (rows, rows), 1)
    sums = jnp.dot(
        (row_ids >= column_ids).astype(BF16), terms.astype(BF16), preferred_element_type=F32
    )
    columns[...] = sums[:, 0:4] + sums[:, 4:8] + sums[:, 8:12]
    by_row = sums.T
    lanes[...] = by_row[0:4] + by_row[4:8] + by_row[8:12]


def silu_of(gates):
    gates = gates.astype(BF16).astype(F32)
    return (gates * jax.nn.sigmoid(gates)).astype(BF16)


def chunk_state(head, key, value, columns, ceiling, burst):
    rows = columns.shape[0]
    lanes = slice(head * HEAD_WIDTH, (head + 1) * HEAD_WIDTH)
    column = columns[:, head : head + 1]
    last = columns[rows - 1 :, head : head + 1]
    weighted = key[:, lanes].astype(F32) * jnp.exp(ceiling * (column - last))
    state = lax.dot_general(
        weighted.astype(BF16), value[:, lanes], (((0,), (0,)), ((), ())), preferred_element_type=F32
    )
    return state.astype(BF16).reshape(8, 16, HEAD_WIDTH), burst - ceiling * last


def attend(head, query, key, value, columns, lanes_ref, ceiling, burst, query_out, inner_out):
    rows = columns.shape[0]
    lanes = slice(head * HEAD_WIDTH, (head + 1) * HEAD_WIDTH)
    column = columns[:, head : head + 1]
    lagged = ceiling * (lanes_ref[head : head + 1, :] - column)
    row_ids = lax.broadcasted_iota(jnp.int32, (rows, rows), 0)
    column_ids = lax.broadcasted_iota(jnp.int32, (rows, rows), 1)
    scores = lax.dot_general(
        query[:, lanes], key[:, lanes], (((1,), (1,)), ((), ())), preferred_element_type=F32
    )
    weights = jnp.where(row_ids >= column_ids, scores * jnp.exp(jnp.minimum(lagged, 0.0)), 0.0)
    inner_out[:, lanes] = jnp.dot(weights.astype(BF16), value[:, lanes], preferred_element_type=F32)
    entry = jnp.exp(burst - ceiling * column)
    query_out[:, lanes] = (query[:, lanes].astype(F32) * entry).astype(BF16)


def text_kernel(
    place_ref,
    ceiling_ref,
    own,
    first,
    others,
    gain_ref,
    weight,
    decay_ref,
    query_out,
    gate_out,
    inner_out,
    state_out,
    span_out,
    late_out,
    normed,
    parts,
    columns,
    lanes,
    sems,
):
    copies = [
        pltpu.make_async_copy(weight.at[3 * at], late_out.at[at], sems.at[at]) for at in range(2)
    ]
    for copy in copies:
        copy.start()
    normalize(place_ref, (own, first, others), gain_ref, normed)
    decay_sums(decay_logits(normed[...], decay_ref[...]), columns, lanes)
    for part in range(3):
        parts[part] = product(normed, weight[part]).astype(BF16)
    gate_out[...] = silu_of(product(normed, weight[3]))
    for head in range(4):
        ceiling = ceiling_ref[head]
        state, span = chunk_state(head, parts.at[1], parts.at[2], columns, ceiling, 0.0)
        state_out[head * 8 : (head + 1) * 8] = state
        span_out[head : head + 1] = jnp.broadcast_to(span, (1, HEAD_WIDTH))
        attend(
            head,
            parts.at[0],
            parts.at[1],
            parts.at[2],
            columns,
            lanes,
            ceiling,
            0.0,
            query_out,
            inner_out,
        )
    for copy in copies:
        copy.wait()


def image_near_kernel(
    place_ref, own, first, gain_ref, weight, decay_ref, scaled_out, total, logits, squares, scaled, sems
):
    copies = []
    for at, ref in enumerate((own, first)):
        columns = columns_of(place_ref, at, own.shape[1])
        value = ref[...].astype(F32)
        square = jnp.sum(value * value, axis=-1, keepdims=True)
        small = (value * gain_ref[:, columns]).astype(BF16)
        scaled[at] = small
        gates = decay_logits(small, decay_ref[:, columns])
        terms = [
            jnp.dot(small, weight[part, columns, :], preferred_element_type=F32)
            for part in (1, 2)
        ]
        copies.append(pltpu.make_async_copy(scaled.at[at], scaled_out.at[at], sems.at[at]))
        copies[at].start()
        if at == 0:
            squares[...], logits[...], total[0], total[1] = square, gates, *terms
        else:
            squares[...] += square
            logits[...] += gates
            total[0] += terms[0]
            total[1] += terms[1]
    for copy in copies:
        copy.wait()


def image_state_kernel(
    place_ref,
    ceiling_ref,
    forget_ref,
    others,
    total,
    logits,
    squares,
    gain_ref,
    weight,
    decay_ref,
    other_state,
    other_span,
    far_out,
    key_value_out,
    scale_out,
    columns,
    lanes,
    state_out,
    scaled,
    key_value,
    sems,
):
    rows, width = others.shape[0] // 2, others.shape[1]
    square = squares[...]
    chunks = []
    for at in range(2):
        chunks.append(columns_of(place_ref, at + 2, width))
        value = others[at * rows : (at + 1) * rows].astype(F32)
        square += jnp.sum(value * value, axis=-1, keepdims=True)
        scaled[at] = (value * gain_ref[:, chunks[at]]).astype(BF16)
    scale = lax.rsqrt(square / (4 * width) + EPSILON)
    scale_out[...] = scale
    for at in range(2):
        term = total[at]
        for place, chunk in enumerate(chunks):
            term += jnp.dot(scaled[place], weight[at + 1, chunk, :], preferred_element_type=F32)
        key_value[at] = (term * scale).astype(BF16)
    far_copy = pltpu.make_async_copy(scaled, far_out, sems.at[0])
    far_copy.start()
    gates = logits[...]
    for place, chunk in enumerate(chunks):
        gates += decay_logits(scaled[place], decay_ref[:, chunk])
    decay_sums(gates * scale, columns, lanes)
    key_value_copy = pltpu.make_async_copy(key_value, key_value_out, sems.at[1])
    key_value_copy.start()
    state_out[:, 0:16, :] = other_state[...]
    burst = jnp.log1p(jnp.full((1, 1), -forget_ref[place_ref[4]], F32))
    ids = lax.broadcasted_iota(jnp.int32, (8, HEAD_WIDTH), 0)
    for head in range(4):
        state, span = chunk_state(
            head, key_value.at[0], key_value.at[1], columns, ceiling_ref[head], burst
        )
        targets = slice(head * 8, (head + 1) * 8)
        state_out[targets, 16:32, :] = state
        tile = jnp.zeros((8, HEAD_WIDTH), F32)
        for kind, value in enumerate((other_span[head : head + 1, 0:1], span)):
            upper = value.astype(BF16).astype(F32)
            tile = jnp.where(ids == 2 * kind, upper, tile)
            tile = jnp.where(ids == 2 * kind + 1, value - upper, tile)
        state_out[targets, 32:40, :] = jnp.broadcast_to(
            tile.astype(BF16)[None], (8, 8, HEAD_WIDTH)
        )
    far_copy.wait()
    key_value_copy.wait()


def image_attend_kernel(
    place_ref,
    ceiling_ref,
    forget_ref,
    near_ref,
    far_ref,
    key_value_ref,
    weight_ref,
    scale_ref,
    columns,
    lanes,
    query_out,
    gate_out,
    inner_out,
    scaled,
    key_value,
    weight,
    query,
    sems,
):
    width = far_ref.shape[2]
    pieces = []
    for slot in range(4):
        ref = (near_ref, far_ref)[slot // 2]
        pieces.append((ref.at[slot % 2], scaled.at[:, columns_of(place_ref, slot, width)]))
    pieces += [
        (weight_ref.at[0], weight.at[0]),
        (weight_ref.at[1], weight.at[1]),
        (key_value_ref, key_value),
    ]
    copies = [
        pltpu.make_async_copy(source, target, sems.at[at])
        for at, (source, target) in enumerate(pieces)
    ]
    for copy in copies:
        copy.start()
    for copy in copies[:5]:
        copy.wait()
    scale = scale_ref[...]
    query[...] = (product(scaled, weight[0]) * scale).astype(BF16)
    copies[5].wait()
    gate_out[...] = silu_of(product(scaled, weight[1]) * scale)
    copies[6].wait()
    burst = jnp.log1p(jnp.full((1, 1), -forget_ref[place_ref[4]], F32))
    for head in range(4):
        attend(
            head,
            query,
            key_value.at[0],
            key_value.at[1],
            columns,
            lanes,
            ceiling_ref[head],
            burst,
            query_out,
            inner_out,
        )


def cost_of(rows, depth, width):
    return pl.CostEstimate(
        flops=2 * rows * depth * width, bytes_accessed=depth * width * 2, transcendentals=0
    )


def relay_kernel(source, out, blocks, sems):
    count, rows = blocks.shape[:2]
    copies = [
        pltpu.make_async_copy(source.at[pl.ds(at * rows, rows)], blocks.at[at], sems.at[at])
        for at in range(count)
    ]
    for copy in copies:
        copy.start()
    for at in range(count):
        copies[at].wait()
        out[:, at * rows : (at + 1) * rows, :] = jnp.swapaxes(blocks[at], 0, 1)


def relay_call(in_proj):
    depth, parts, width = in_proj.shape
    count = 8
    return pl.pallas_call(
        relay_kernel,
        out_shape=pltpu.VMEM((parts, depth, width), BF16),
        in_specs=[HBM],
        out_specs=VMEM,
        scratch_shapes=[
            pltpu.VMEM((count, depth // count, parts, width), BF16),
            pltpu.SemaphoreType.DMA((count,)),
        ],
        compiler_params=limit(20),
        cost_estimate=pl.CostEstimate(
            flops=0, bytes_accessed=2 * depth * parts * width, transcendentals=0
        ),
        name="relay",
    )(*in_hbm(in_proj))


def text_call(place, ceiling, chunks, gain, weights, decay):
    rows, width = chunks[0].shape
    depth = gain.shape[1]
    outs = (
        hbm_of(rows, width),
        hbm_of(rows, width),
        hbm_of(rows, width, dtype=F32),
        shape_of(32, 16, HEAD_WIDTH),
        shape_of(4, HEAD_WIDTH, dtype=F32),
        hbm_of(2, depth, width),
    )
    arrays = (*chunks, gain, weights, decay)
    return pl.pallas_call(
        text_kernel,
        grid=(1,),
        out_shape=outs,
        in_specs=[SMEM, SMEM] + [VMEM] * len(arrays),
        out_specs=tuple(fixed(*o.shape) for o in outs[:-1]) + (HBM,),
        scratch_shapes=[
            pltpu.VMEM((rows, depth), BF16),
            pltpu.VMEM((3, rows, width), BF16),
            pltpu.VMEM((rows, 4), F32),
            pltpu.VMEM((4, rows), F32),
            pltpu.SemaphoreType.DMA((2,)),
        ],
        compiler_params=limit(24, "arbitrary"),
        cost_estimate=cost_of(rows, depth, 4 * width),
        name="text_unit",
    )(place, ceiling, *arrays)


def image_near_call(place, near, gain, weights, decay):
    rows, width = near[0].shape
    outs = (
        hbm_of(2, rows, width),
        shape_of(2, rows, width, dtype=F32),
        shape_of(rows, HEAD_WIDTH, dtype=F32),
        shape_of(rows, 1, dtype=F32),
    )
    return pl.pallas_call(
        image_near_kernel,
        out_shape=outs,
        in_specs=[SMEM] + [VMEM] * 5,
        out_specs=(HBM,) + (VMEM,) * 3,
        scratch_shapes=[pltpu.VMEM((2, rows, width), BF16), pltpu.SemaphoreType.DMA((2,))],
        compiler_params=limit(16),
        cost_estimate=cost_of(rows, 2 * width, 2 * width),
        name="image_near",
    )(place, *near, gain, weights, decay)


def image_state_call(place, ceiling, forget, *arrays):
    rows, width = arrays[0].shape[0] // 2, arrays[0].shape[1]
    outs = (
        hbm_of(2, rows, width),
        hbm_of(2, rows, width),
        shape_of(rows, 1, dtype=F32),
        shape_of(rows, 4, dtype=F32),
        shape_of(4, rows, dtype=F32),
        shape_of(32, 40, HEAD_WIDTH),
    )
    return pl.pallas_call(
        image_state_kernel,
        out_shape=outs,
        in_specs=[SMEM] * 3 + [VMEM] * len(arrays),
        out_specs=(HBM, HBM) + (VMEM,) * 4,
        scratch_shapes=[
            pltpu.VMEM((2, rows, width), BF16),
            pltpu.VMEM((2, rows, width), BF16),
            pltpu.SemaphoreType.DMA((2,)),
        ],
        compiler_params=limit(16),
        cost_estimate=cost_of(rows, width, 2 * width),
        name="image_state",
    )(place, ceiling, forget, *arrays)


def image_attend_call(place, ceiling, forget, weights, near, far, key_value, *small):
    rows, width = far.shape[1:]
    depth = 4 * width
    outs = (
        hbm_of(rows, width),
        hbm_of(rows, width),
        hbm_of(rows, width, dtype=F32),
    )
    return pl.pallas_call(
        image_attend_kernel,
        grid=(1,),
        out_shape=outs,
        in_specs=[SMEM] * 3 + [HBM] * 4 + [VMEM] * 3,
        out_specs=tuple(fixed(*o.shape) for o in outs),
        scratch_shapes=[
            pltpu.VMEM((rows, depth), BF16),
            pltpu.VMEM((2, rows, width), BF16),
            pltpu.VMEM((2, depth, width), BF16),
            pltpu.VMEM((rows, width), BF16),
            pltpu.SemaphoreType.DMA((7,)),
        ],
        compiler_params=limit(16, "arbitrary"),
        cost_estimate=cost_of(rows, depth, 2 * width),
        name="image_attend",
    )(place, ceiling, forget, *in_hbm(near, far, key_value, weights), *small)


def scan_kernel(start_ref, states, out, decay, image_at):
    count = start_ref.shape[0]
    for kind in range(2):
        spans = states[:, 32:40, :].astype(F32)
        span = spans[:, 2 * kind : 2 * kind + 1, :] + spans[:, 2 * kind + 1 : 2 * kind + 2, :]
        decay[:, kind] = jnp.broadcast_to(jnp.exp(span), (count, 16, HEAD_WIDTH))
    for position in range(2 * count):
        image_at[position] = -1
    for image in range(count):
        image_at[lax.shift_right_logical(start_ref[image], 1)] = image
    carry = jnp.zeros((16, HEAD_WIDTH), F32)
    texts = jnp.int32(0)
    for position in range(2 * count):
        found = image_at[position]
        kind = (found >= 0).astype(jnp.int32)
        source = jnp.where(found >= 0, found, jnp.minimum(texts, count - 1))
        texts += 1 - kind
        rows = pl.ds(pl.multiple_of(kind * 16, 16), 16)
        out[source, rows, :] = carry.astype(BF16)
        carry = decay[source, kind] * carry + states[source, rows, :].astype(F32)


def scan_call(starts, states):
    count = states.shape[0]
    return pl.pallas_call(
        scan_kernel,
        out_shape=shape_of(count, 32, HEAD_WIDTH),
        in_specs=[SMEM, VMEM],
        out_specs=VMEM,
        scratch_shapes=[
            pltpu.VMEM((count, 2, 16, HEAD_WIDTH), F32),
            pltpu.SMEM((2 * count,), jnp.int32),
        ],
        compiler_params=limit(6),
        name="state_scan",
    )(starts, states)


def gate_kernel(place_ref, entering, out_gain, out_proj, *refs):
    sources, (far_text, far_image, gated), buffers, sems = refs[:6], refs[6:9], refs[9:15], refs[15]
    copies = [
        pltpu.make_async_copy(source, buffer, sems.at[at])
        for at, (source, buffer) in enumerate(zip(sources, buffers))
    ]
    for copy in copies:
        copy.start()
    rows, width = far_text.shape
    for kind in range(2):
        for copy in copies[3 * kind : 3 * kind + 3]:
            copy.wait()
        query, gate, inner = buffers[3 * kind : 3 * kind + 3]
        for head in range(width // HEAD_WIDTH):
            lanes = slice(head * HEAD_WIDTH, (head + 1) * HEAD_WIDTH)
            state = entering[head * 8 : (head + 1) * 8, kind * 16 : (kind + 1) * 16, :]
            attended = inner[:, lanes] + jnp.dot(
                query[:, lanes], state.reshape(HEAD_WIDTH, HEAD_WIDTH), preferred_element_type=F32
            )
            scale = lax.rsqrt(jnp.mean(attended * attended, axis=-1, keepdims=True) + EPSILON)
            value = attended * scale * out_gain[head : head + 1, :] * gate[:, lanes].astype(F32)
            gated[kind * rows : (kind + 1) * rows, lanes] = value.astype(BF16)
    weight = out_proj[:, ring_columns(place_ref, 2, width)]
    block = jnp.dot(gated[...], weight, preferred_element_type=F32).astype(BF16)
    far_text[...] = block[:rows]
    far_image[...] = block[rows:]


def gate_call(place, entering, out_gain, out_proj, text_parts, image_parts):
    rows, width = text_parts[0].shape
    outs = (shape_of(rows, width), shape_of(rows, width), shape_of(2 * rows, width))
    parts = in_hbm(*text_parts, *image_parts)
    return pl.pallas_call(
        gate_kernel,
        out_shape=outs,
        in_specs=[SMEM] + [VMEM] * 3 + [HBM] * 6,
        out_specs=(VMEM,) * 3,
        scratch_shapes=[pltpu.VMEM(p.shape, p.dtype) for p in parts]
        + [pltpu.SemaphoreType.DMA((6,))],
        compiler_params=limit(16),
        name="gate_far",
    )(place, entering, out_gain, out_proj, *parts)


def near_kernel(place_ref, gated, out_proj, next_t, next_i, last_t, last_i, own_t, own_i):
    rows, width = next_t.shape
    for step, text, image in ((1, next_t, next_i), (3, last_t, last_i), (0, own_t, own_i)):
        weight = out_proj[:, ring_columns(place_ref, step, width)]
        block = jnp.dot(gated[...], weight, preferred_element_type=F32)
        text[...] = block[:rows].astype(text.dtype)
        image[...] = block[rows:].astype(image.dtype)


def near_call(place, gated, out_proj):
    rows, width = gated.shape[0] // 2, gated.shape[1]
    outs = (shape_of(rows, width),) * 4 + (shape_of(rows, width, dtype=F32),) * 2
    return pl.pallas_call(
        near_kernel,
        out_shape=outs,
        in_specs=[SMEM, VMEM, VMEM],
        out_specs=(VMEM,) * 6,
        compiler_params=limit(16),
        cost_estimate=cost_of(2 * rows, width, 3 * width),
        name="near_blocks",
    )(place, gated, out_proj)


def moved(array, turn):
    pairs = []
    for core in range(2):
        for x in range(4):
            partner = x ^ 1 if (core + turn) % 2 == 0 else 3 - x
            pairs.append((4 * core + x, 4 * core + partner))
    return lax.ppermute(array, ("seq_2", "head"), pairs)


def passed(array, step):
    return lax.ppermute(array, "head", [(i, (i + step) % 4) for i in range(4)])


def gathered(rows):
    first = moved(rows, 0)
    joined = small_call(join_kernel, shape_of(2 * rows.shape[0], rows.shape[1]), rows, first)
    return (rows, first, moved(joined, 1))


def added(one, two):
    return (one.astype(F32) + two.astype(F32)).astype(BF16)


def steps(
    image_patches,
    text_embed,
    image_start,
    image_forget,
    adapter,
    norm_gain,
    in_proj,
    decay_proj,
    head_decay_ceiling,
    out_gain,
    out_proj,
):
    x = lax.axis_index("head")
    even = lax.axis_index("seq_2") == 0
    first, second = jnp.where(even, x ^ 1, 3 - x), jnp.where(even, 3 - x, x ^ 1)
    place = jnp.stack([x, first, second, x ^ 2, lax.axis_index(SEQ)]).astype(jnp.int32)
    decay = decay_proj.T
    gain = norm_gain[None]
    ceiling = head_decay_ceiling

    text_chunks = gathered(text_embed)
    patches = image_patches.transpose(0, 2, 1)
    leaving = adapter_leave(place, patches, adapter)
    stay = adapter_stay(place, patches, adapter)
    weights = relay_call(in_proj)
    block = shape_of(*text_embed.shape)
    arrived = moved(leaving, 0)
    last = moved(small_call(pass_kernel, block, stay, arrived), 1)
    embed = small_call(embed_kernel, block, stay, arrived, last)
    image_chunks = gathered(embed)

    *text_parts, text_state, text_span, late_weights = text_call(
        place, ceiling, text_chunks, gain, weights, decay
    )
    near, *partial = image_near_call(place, image_chunks[:2], gain, weights, decay)
    *held, states = image_state_call(
        place,
        ceiling,
        image_forget,
        image_chunks[2],
        *partial,
        gain,
        weights,
        decay,
        text_state,
        text_span,
    )
    slices = lax.all_to_all(states, SEQ, 0, 0, tiled=True)
    image_parts = image_attend_call(
        place, ceiling, image_forget, late_weights, near, *held
    )
    entering = lax.all_to_all(scan_call(image_start, slices), SEQ, 0, 0, tiled=True)

    far_t, far_i, gated = gate_call(
        place, entering, out_gain, out_proj, text_parts, image_parts
    )
    next_t, next_i, last_t, last_i, own_t, own_i = near_call(place, gated, out_proj)
    far_from_left = passed(far_t, 1)
    far_from_right = passed(far_i, 3)
    left_i = passed(next_i, 1)
    right_t = passed(last_t, 3)
    left_t = passed(added(next_t, far_from_left), 1)
    right_i = passed(added(last_i, far_from_right), 3)
    text_out = text_embed.astype(F32) + (own_t + left_t.astype(F32) + right_t.astype(F32))
    image_out = embed.astype(F32) + (own_i + left_i.astype(F32) + right_i.astype(F32))
    return (image_out.astype(BF16)[None], text_out.astype(BF16))


def solution(mesh):
    split = Mesh(
        mesh.devices.reshape(4, 4, 2, mesh.shape["head"]), ("seq_0", "seq_1", "seq_2", "head")
    )
    return jax.shard_map(
        steps,
        mesh=split,
        in_specs=(
            P(SEQ, None, "head"),
            P(SEQ, "head"),
            P(),
            P(),
            P("head", None),
            P(),
            P(None, None, "head"),
            P(None, "head"),
            P("head"),
            P("head", None),
            P("head", None),
        ),
        out_specs=(P(SEQ, None, "head"), P(SEQ, "head")),
        check_vma=False,
    )
```

```python
import jax
import jax.numpy as jnp
from jax import lax
from jax.experimental import pallas as pl
from jax.experimental.pallas import tpu as pltpu
from jax.sharding import Mesh
from jax.sharding import PartitionSpec as P

SEQ = ("seq_0", "seq_1", "seq_2")
EPSILON = 1e-06
F32 = jnp.float32
BF16 = jnp.bfloat16
HEAD_WIDTH = 128


VMEM = pl.BlockSpec(memory_space=pltpu.VMEM)
SMEM = pl.BlockSpec(memory_space=pltpu.SMEM)
HBM = pl.BlockSpec(memory_space=pltpu.HBM)


def shape_of(*dims, dtype=BF16):
    return jax.ShapeDtypeStruct(dims, dtype)


def hbm_of(*dims, dtype=BF16):
    return pltpu.HBM(dims, dtype)


def in_hbm(*arrays):
    return [pltpu.with_memory_space_constraint(a, pltpu.HBM) for a in arrays]


def limit(mebibytes, *semantics):
    return pltpu.CompilerParams(
        dimension_semantics=semantics or None, vmem_limit_bytes=mebibytes << 20
    )


def fixed(*dims):
    return pl.BlockSpec(dims, lambda *_: (0,) * len(dims))


def columns_of(place_ref, slot, width):
    return pl.ds(pl.multiple_of(place_ref[slot] * width, width), width)


def ring_columns(place_ref, step, width):
    return pl.ds(pl.multiple_of(lax.rem(place_ref[0] + step, 4) * width, width), width)


def adapter_blocks(place_ref, patches_ref, adapter_ref, patches, blocks, sems, slots):
    patches_copy = pltpu.make_async_copy(patches_ref.at[0], patches, sems.at[0])
    patches_copy.start()
    copies = []
    for at, slot in enumerate(slots):
        columns = columns_of(place_ref, slot, blocks.shape[2])
        copies.append(
            pltpu.make_async_copy(adapter_ref.at[:, columns], blocks.at[at], sems.at[at + 1])
        )
        copies[at].start()
    patches_copy.wait()
    rows = patches[...].T
    for at in range(len(slots)):
        copies[at].wait()
        yield jnp.dot(rows, blocks[at], preferred_element_type=F32)


def leave_kernel(place_ref, patches_ref, adapter_ref, out, *scratch):
    rows = out.shape[0] // 2
    for at, block in enumerate(adapter_blocks(place_ref, patches_ref, adapter_ref, *scratch, (1, 3))):
        out[at * rows : (at + 1) * rows] = block.astype(BF16)


def stay_kernel(place_ref, patches_ref, adapter_ref, out, *scratch):
    for at, block in enumerate(adapter_blocks(place_ref, patches_ref, adapter_ref, *scratch, (2, 0))):
        out[at] = block


def adapter_call(kernel, outs, count, place, patches, adapter):
    depth, rows = patches.shape[1:]
    return pl.pallas_call(
        kernel,
        out_shape=outs,
        in_specs=[SMEM, HBM, HBM],
        out_specs=jax.tree.map(lambda _: VMEM, outs),
        scratch_shapes=[
            pltpu.VMEM((depth, rows), BF16),
            pltpu.VMEM((count, depth, adapter.shape[1] // 4), BF16),
            pltpu.SemaphoreType.DMA((count + 1,)),
        ],
        compiler_params=limit(8),
        cost_estimate=cost_of(rows, depth, count * adapter.shape[1] // 4),
    )(place, *in_hbm(patches, adapter))


def adapter_leave(*arrays):
    rows, width = arrays[1].shape[2], arrays[2].shape[1] // 4
    return adapter_call(leave_kernel, shape_of(2 * rows, width), 2, *arrays)


def adapter_stay(*arrays):
    rows, width = arrays[1].shape[2], arrays[2].shape[1] // 4
    outs = shape_of(2, rows, width, dtype=F32)
    return adapter_call(stay_kernel, outs, 2, *arrays)


def small_call(kernel, out, *arrays):
    return pl.pallas_call(
        kernel,
        out_shape=out,
        in_specs=[VMEM] * len(arrays),
        out_specs=VMEM,
        compiler_params=limit(4),
    )(*arrays)


def pass_kernel(stay, arrived, out):
    rows = out.shape[0]
    out[...] = (stay[0] + arrived[rows:].astype(F32)).astype(BF16)


def embed_kernel(stay, arrived, last, out):
    rows = out.shape[0]
    out[...] = (stay[1] + arrived[:rows].astype(F32) + last[...].astype(F32)).astype(BF16)


def join_kernel(one, two, out):
    rows = one.shape[0]
    out[:rows] = one[...]
    out[rows:] = two[...]


def normalize(place_ref, chunks, gain_ref, normed):
    own, first, others = chunks
    rows, width = own.shape
    values = (own[...], first[...], others[:rows], others[rows:])
    total = 0.0
    for value in values:
        value = value.astype(F32)
        total += jnp.sum(value * value, axis=-1, keepdims=True)
    scale = lax.rsqrt(total / (4 * width) + EPSILON)
    for slot, value in enumerate(values):
        columns = columns_of(place_ref, slot, width)
        normed[:, columns] = (value.astype(F32) * scale * gain_ref[:, columns]).astype(BF16)


def product(normed, weight):
    return jnp.dot(normed[...], weight, preferred_element_type=F32)


def decay_logits(values, decay):
    decay = jnp.concatenate([decay.astype(F32)] * 4, axis=0).astype(BF16)
    decay = jnp.concatenate([decay, jnp.zeros((HEAD_WIDTH - 16, decay.shape[1]), BF16)], axis=0)
    return lax.dot_general(values, decay, (((1,), (1,)), ((), ())), preferred_element_type=F32)


def decay_sums(logits, columns, lanes):
    rows = logits.shape[0]
    gates = jax.nn.sigmoid(logits)
    ids = lax.broadcasted_iota(jnp.int32, gates.shape, 1)
    upper = gates.astype(BF16).astype(F32)
    middle = (gates - upper).astype(BF16).astype(F32)
    terms = jnp.where(ids < 4, upper, jnp.where(ids < 8, middle, gates - upper - middle))
    row_ids = lax.broadcasted_iota(jnp.int32, (rows, rows), 0)
    column_ids = lax.broadcasted_iota(jnp.int32, (rows, rows), 1)
    sums = jnp.dot(
        (row_ids >= column_ids).astype(BF16), terms.astype(BF16), preferred_element_type=F32
    )
    columns[...] = sums[:, 0:4] + sums[:, 4:8] + sums[:, 8:12]
    by_row = sums.T
    lanes[...] = by_row[0:4] + by_row[4:8] + by_row[8:12]


def silu_of(gates):
    gates = gates.astype(BF16).astype(F32)
    return (gates * jax.nn.sigmoid(gates)).astype(BF16)


def chunk_state(head, key, value, columns, ceiling, burst):
    rows = columns.shape[0]
    lanes = slice(head * HEAD_WIDTH, (head + 1) * HEAD_WIDTH)
    column = columns[:, head : head + 1]
    last = columns[rows - 1 :, head : head + 1]
    weighted = key[:, lanes].astype(F32) * jnp.exp(ceiling * (column - last))
    state = lax.dot_general(
        weighted.astype(BF16), value[:, lanes], (((0,), (0,)), ((), ())), preferred_element_type=F32
    )
    return state.astype(BF16).reshape(8, 16, HEAD_WIDTH), burst - ceiling * last


def attend(head, query, key, value, columns, lanes_ref, ceiling, burst, query_out, inner_out):
    rows = columns.shape[0]
    lanes = slice(head * HEAD_WIDTH, (head + 1) * HEAD_WIDTH)
    column = columns[:, head : head + 1]
    lagged = ceiling * (lanes_ref[head : head + 1, :] - column)
    row_ids = lax.broadcasted_iota(jnp.int32, (rows, rows), 0)
    column_ids = lax.broadcasted_iota(jnp.int32, (rows, rows), 1)
    scores = lax.dot_general(
        query[:, lanes], key[:, lanes], (((1,), (1,)), ((), ())), preferred_element_type=F32
    )
    weights = jnp.where(row_ids >= column_ids, scores * jnp.exp(jnp.minimum(lagged, 0.0)), 0.0)
    inner_out[:, lanes] = jnp.dot(weights.astype(BF16), value[:, lanes], preferred_element_type=F32)
    entry = jnp.exp(burst - ceiling * column)
    query_out[:, lanes] = (query[:, lanes].astype(F32) * entry).astype(BF16)


def text_kernel(
    place_ref,
    ceiling_ref,
    own,
    first,
    others,
    gain_ref,
    weight,
    decay_ref,
    query_out,
    gate_out,
    inner_out,
    state_out,
    span_out,
    late_out,
    normed,
    parts,
    columns,
    lanes,
    sems,
):
    copies = [
        pltpu.make_async_copy(weight.at[3 * at], late_out.at[at], sems.at[at]) for at in range(2)
    ]
    for copy in copies:
        copy.start()
    normalize(place_ref, (own, first, others), gain_ref, normed)
    decay_sums(decay_logits(normed[...], decay_ref[...]), columns, lanes)
    for part in range(3):
        parts[part] = product(normed, weight[part]).astype(BF16)
    gate_out[...] = silu_of(product(normed, weight[3]))
    for head in range(4):
        ceiling = ceiling_ref[head]
        state, span = chunk_state(head, parts.at[1], parts.at[2], columns, ceiling, 0.0)
        state_out[head * 8 : (head + 1) * 8] = state
        span_out[head : head + 1] = jnp.broadcast_to(span, (1, HEAD_WIDTH))
        attend(
            head,
            parts.at[0],
            parts.at[1],
            parts.at[2],
            columns,
            lanes,
            ceiling,
            0.0,
            query_out,
            inner_out,
        )
    for copy in copies:
        copy.wait()


def image_near_kernel(
    place_ref, own, first, gain_ref, weight, decay_ref, scaled_out, total, logits, squares, scaled, sems
):
    copies = []
    for at, ref in enumerate((own, first)):
        columns = columns_of(place_ref, at, own.shape[1])
        value = ref[...].astype(F32)
        square = jnp.sum(value * value, axis=-1, keepdims=True)
        small = (value * gain_ref[:, columns]).astype(BF16)
        scaled[at] = small
        gates = decay_logits(small, decay_ref[:, columns])
        terms = [
            jnp.dot(small, weight[part, columns, :], preferred_element_type=F32)
            for part in (1, 2)
        ]
        copies.append(pltpu.make_async_copy(scaled.at[at], scaled_out.at[at], sems.at[at]))
        copies[at].start()
        if at == 0:
            squares[...], logits[...], total[0], total[1] = square, gates, *terms
        else:
            squares[...] += square
            logits[...] += gates
            total[0] += terms[0]
            total[1] += terms[1]
    for copy in copies:
        copy.wait()


def image_state_kernel(
    place_ref,
    ceiling_ref,
    forget_ref,
    others,
    total,
    logits,
    squares,
    gain_ref,
    weight,
    decay_ref,
    other_state,
    other_span,
    far_out,
    key_value_out,
    scale_out,
    columns,
    lanes,
    state_out,
    scaled,
    key_value,
    sems,
):
    rows, width = others.shape[0] // 2, others.shape[1]
    square = squares[...]
    chunks = []
    for at in range(2):
        chunks.append(columns_of(place_ref, at + 2, width))
        value = others[at * rows : (at + 1) * rows].astype(F32)
        square += jnp.sum(value * value, axis=-1, keepdims=True)
        scaled[at] = (value * gain_ref[:, chunks[at]]).astype(BF16)
    scale = lax.rsqrt(square / (4 * width) + EPSILON)
    scale_out[...] = scale
    for at in range(2):
        term = total[at]
        for place, chunk in enumerate(chunks):
            term += jnp.dot(scaled[place], weight[at + 1, chunk, :], preferred_element_type=F32)
        key_value[at] = (term * scale).astype(BF16)
    far_copy = pltpu.make_async_copy(scaled, far_out, sems.at[0])
    far_copy.start()
    gates = logits[...]
    for place, chunk in enumerate(chunks):
        gates += decay_logits(scaled[place], decay_ref[:, chunk])
    decay_sums(gates * scale, columns, lanes)
    key_value_copy = pltpu.make_async_copy(key_value, key_value_out, sems.at[1])
    key_value_copy.start()
    state_out[:, 0:16, :] = other_state[...]
    burst = jnp.log1p(jnp.full((1, 1), -forget_ref[place_ref[4]], F32))
    ids = lax.broadcasted_iota(jnp.int32, (8, HEAD_WIDTH), 0)
    for head in range(4):
        state, span = chunk_state(
            head, key_value.at[0], key_value.at[1], columns, ceiling_ref[head], burst
        )
        targets = slice(head * 8, (head + 1) * 8)
        state_out[targets, 16:32, :] = state
        tile = jnp.zeros((8, HEAD_WIDTH), F32)
        for kind, value in enumerate((other_span[head : head + 1, 0:1], span)):
            upper = value.astype(BF16).astype(F32)
            tile = jnp.where(ids == 2 * kind, upper, tile)
            tile = jnp.where(ids == 2 * kind + 1, value - upper, tile)
        state_out[targets, 32:40, :] = jnp.broadcast_to(
            tile.astype(BF16)[None], (8, 8, HEAD_WIDTH)
        )
    far_copy.wait()
    key_value_copy.wait()


def image_attend_kernel(
    place_ref,
    ceiling_ref,
    forget_ref,
    near_ref,
    far_ref,
    key_value_ref,
    weight_ref,
    scale_ref,
    columns,
    lanes,
    query_out,
    gate_out,
    inner_out,
    scaled,
    key_value,
    weight,
    query,
    sems,
):
    width = far_ref.shape[2]
    pieces = []
    for slot in range(4):
        ref = (near_ref, far_ref)[slot // 2]
        pieces.append((ref.at[slot % 2], scaled.at[:, columns_of(place_ref, slot, width)]))
    pieces += [
        (weight_ref.at[0], weight.at[0]),
        (weight_ref.at[1], weight.at[1]),
        (key_value_ref, key_value),
    ]
    copies = [
        pltpu.make_async_copy(source, target, sems.at[at])
        for at, (source, target) in enumerate(pieces)
    ]
    for copy in copies:
        copy.start()
    for copy in copies[:5]:
        copy.wait()
    scale = scale_ref[...]
    query[...] = (product(scaled, weight[0]) * scale).astype(BF16)
    copies[5].wait()
    gate_out[...] = silu_of(product(scaled, weight[1]) * scale)
    copies[6].wait()
    burst = jnp.log1p(jnp.full((1, 1), -forget_ref[place_ref[4]], F32))
    for head in range(4):
        attend(
            head,
            query,
            key_value.at[0],
            key_value.at[1],
            columns,
            lanes,
            ceiling_ref[head],
            burst,
            query_out,
            inner_out,
        )


def cost_of(rows, depth, width):
    return pl.CostEstimate(
        flops=2 * rows * depth * width, bytes_accessed=depth * width * 2, transcendentals=0
    )


def relay_kernel(source, out, blocks, sems):
    count, rows = blocks.shape[:2]
    copies = [
        pltpu.make_async_copy(source.at[pl.ds(at * rows, rows)], blocks.at[at], sems.at[at])
        for at in range(count)
    ]
    for copy in copies:
        copy.start()
    for at in range(count):
        copies[at].wait()
        out[:, at * rows : (at + 1) * rows, :] = jnp.swapaxes(blocks[at], 0, 1)


def relay_call(in_proj):
    depth, parts, width = in_proj.shape
    count = 8
    return pl.pallas_call(
        relay_kernel,
        out_shape=pltpu.VMEM((parts, depth, width), BF16),
        in_specs=[HBM],
        out_specs=VMEM,
        scratch_shapes=[
            pltpu.VMEM((count, depth // count, parts, width), BF16),
            pltpu.SemaphoreType.DMA((count,)),
        ],
        compiler_params=limit(20),
        cost_estimate=pl.CostEstimate(
            flops=0, bytes_accessed=2 * depth * parts * width, transcendentals=0
        ),
        name="relay",
    )(*in_hbm(in_proj))


def text_call(place, ceiling, chunks, gain, weights, decay):
    rows, width = chunks[0].shape
    depth = gain.shape[1]
    outs = (
        hbm_of(rows, width),
        hbm_of(rows, width),
        hbm_of(rows, width, dtype=F32),
        shape_of(32, 16, HEAD_WIDTH),
        shape_of(4, HEAD_WIDTH, dtype=F32),
        hbm_of(2, depth, width),
    )
    arrays = (*chunks, gain, weights, decay)
    return pl.pallas_call(
        text_kernel,
        grid=(1,),
        out_shape=outs,
        in_specs=[SMEM, SMEM] + [VMEM] * len(arrays),
        out_specs=tuple(fixed(*o.shape) for o in outs[:-1]) + (HBM,),
        scratch_shapes=[
            pltpu.VMEM((rows, depth), BF16),
            pltpu.VMEM((3, rows, width), BF16),
            pltpu.VMEM((rows, 4), F32),
            pltpu.VMEM((4, rows), F32),
            pltpu.SemaphoreType.DMA((2,)),
        ],
        compiler_params=limit(24, "arbitrary"),
        cost_estimate=cost_of(rows, depth, 4 * width),
        name="text_unit",
    )(place, ceiling, *arrays)


def image_near_call(place, near, gain, weights, decay):
    rows, width = near[0].shape
    outs = (
        hbm_of(2, rows, width),
        shape_of(2, rows, width, dtype=F32),
        shape_of(rows, HEAD_WIDTH, dtype=F32),
        shape_of(rows, 1, dtype=F32),
    )
    return pl.pallas_call(
        image_near_kernel,
        out_shape=outs,
        in_specs=[SMEM] + [VMEM] * 5,
        out_specs=(HBM,) + (VMEM,) * 3,
        scratch_shapes=[pltpu.VMEM((2, rows, width), BF16), pltpu.SemaphoreType.DMA((2,))],
        compiler_params=limit(16),
        cost_estimate=cost_of(rows, 2 * width, 2 * width),
        name="image_near",
    )(place, *near, gain, weights, decay)


def image_state_call(place, ceiling, forget, *arrays):
    rows, width = arrays[0].shape[0] // 2, arrays[0].shape[1]
    outs = (
        hbm_of(2, rows, width),
        hbm_of(2, rows, width),
        shape_of(rows, 1, dtype=F32),
        shape_of(rows, 4, dtype=F32),
        shape_of(4, rows, dtype=F32),
        shape_of(32, 40, HEAD_WIDTH),
    )
    return pl.pallas_call(
        image_state_kernel,
        out_shape=outs,
        in_specs=[SMEM] * 3 + [VMEM] * len(arrays),
        out_specs=(HBM, HBM) + (VMEM,) * 4,
        scratch_shapes=[
            pltpu.VMEM((2, rows, width), BF16),
            pltpu.VMEM((2, rows, width), BF16),
            pltpu.SemaphoreType.DMA((2,)),
        ],
        compiler_params=limit(16),
        cost_estimate=cost_of(rows, width, 2 * width),
        name="image_state",
    )(place, ceiling, forget, *arrays)


def image_attend_call(place, ceiling, forget, weights, near, far, key_value, *small):
    rows, width = far.shape[1:]
    depth = 4 * width
    outs = (
        hbm_of(rows, width),
        hbm_of(rows, width),
        hbm_of(rows, width, dtype=F32),
    )
    return pl.pallas_call(
        image_attend_kernel,
        grid=(1,),
        out_shape=outs,
        in_specs=[SMEM] * 3 + [HBM] * 4 + [VMEM] * 3,
        out_specs=tuple(fixed(*o.shape) for o in outs),
        scratch_shapes=[
            pltpu.VMEM((rows, depth), BF16),
            pltpu.VMEM((2, rows, width), BF16),
            pltpu.VMEM((2, depth, width), BF16),
            pltpu.VMEM((rows, width), BF16),
            pltpu.SemaphoreType.DMA((7,)),
        ],
        compiler_params=limit(16, "arbitrary"),
        cost_estimate=cost_of(rows, depth, 2 * width),
        name="image_attend",
    )(place, ceiling, forget, *in_hbm(near, far, key_value, weights), *small)


def scan_kernel(start_ref, states, out, decay, image_at):
    count = start_ref.shape[0]
    for position in range(2 * count):
        image_at[position] = -1
    for image in range(count):
        image_at[lax.shift_right_logical(start_ref[image], 1)] = image
    spans = states[:, 32:40, :].astype(F32)
    for kind in range(2):
        span = spans[:, 2 * kind : 2 * kind + 1, :] + spans[:, 2 * kind + 1 : 2 * kind + 2, :]
        decay[:, kind] = jnp.broadcast_to(jnp.exp(span), (count, 8, HEAD_WIDTH))
    upper = lower = jnp.zeros((8, HEAD_WIDTH), F32)
    texts = jnp.int32(0)
    for position in range(2 * count):
        found = image_at[position]
        kind = (found >= 0).astype(jnp.int32)
        source = jnp.where(found >= 0, found, jnp.minimum(texts, count - 1))
        texts += 1 - kind
        rows = pl.ds(pl.multiple_of(kind * 16, 16), 16)
        out[source, rows, :] = jnp.concatenate([upper, lower], axis=0).astype(BF16)
        state = states[source, rows, :].astype(F32)
        factor = decay[source, kind]
        upper = factor * upper + state[:8]
        lower = factor * lower + state[8:]


def scan_call(starts, states):
    count = states.shape[0]
    return pl.pallas_call(
        scan_kernel,
        out_shape=shape_of(count, 32, HEAD_WIDTH),
        in_specs=[SMEM, VMEM],
        out_specs=VMEM,
        scratch_shapes=[
            pltpu.VMEM((count, 2, 8, HEAD_WIDTH), F32),
            pltpu.SMEM((2 * count,), jnp.int32),
        ],
        compiler_params=limit(6),
        name="state_scan",
    )(starts, states)


def gate_kernel(place_ref, entering, out_gain, out_proj, *refs):
    sources, (far_text, far_image, gated), buffers, sems = refs[:6], refs[6:9], refs[9:15], refs[15]
    copies = [
        pltpu.make_async_copy(source, buffer, sems.at[at])
        for at, (source, buffer) in enumerate(zip(sources, buffers))
    ]
    for copy in copies:
        copy.start()
    rows, width = far_text.shape
    for kind in range(2):
        for copy in copies[3 * kind : 3 * kind + 3]:
            copy.wait()
        query, gate, inner = buffers[3 * kind : 3 * kind + 3]
        for head in range(width // HEAD_WIDTH):
            lanes = slice(head * HEAD_WIDTH, (head + 1) * HEAD_WIDTH)
            state = entering[head * 8 : (head + 1) * 8, kind * 16 : (kind + 1) * 16, :]
            attended = inner[:, lanes] + jnp.dot(
                query[:, lanes], state.reshape(HEAD_WIDTH, HEAD_WIDTH), preferred_element_type=F32
            )
            scale = lax.rsqrt(jnp.mean(attended * attended, axis=-1, keepdims=True) + EPSILON)
            value = attended * scale * out_gain[head : head + 1, :] * gate[:, lanes].astype(F32)
            gated[kind * rows : (kind + 1) * rows, lanes] = value.astype(BF16)
    weight = out_proj[:, ring_columns(place_ref, 2, width)]
    block = jnp.dot(gated[...], weight, preferred_element_type=F32).astype(BF16)
    far_text[...] = block[:rows]
    far_image[...] = block[rows:]


def gate_call(place, entering, out_gain, out_proj, text_parts, image_parts):
    rows, width = text_parts[0].shape
    outs = (shape_of(rows, width), shape_of(rows, width), shape_of(2 * rows, width))
    parts = in_hbm(*text_parts, *image_parts)
    return pl.pallas_call(
        gate_kernel,
        out_shape=outs,
        in_specs=[SMEM] + [VMEM] * 3 + [HBM] * 6,
        out_specs=(VMEM,) * 3,
        scratch_shapes=[pltpu.VMEM(p.shape, p.dtype) for p in parts]
        + [pltpu.SemaphoreType.DMA((6,))],
        compiler_params=limit(16),
        name="gate_far",
    )(place, entering, out_gain, out_proj, *parts)


def near_kernel(place_ref, gated, out_proj, next_t, next_i, last_t, last_i, own_t, own_i):
    rows, width = next_t.shape
    for step, text, image in ((1, next_t, next_i), (3, last_t, last_i), (0, own_t, own_i)):
        weight = out_proj[:, ring_columns(place_ref, step, width)]
        block = jnp.dot(gated[...], weight, preferred_element_type=F32)
        text[...] = block[:rows].astype(text.dtype)
        image[...] = block[rows:].astype(image.dtype)


def near_call(place, gated, out_proj):
    rows, width = gated.shape[0] // 2, gated.shape[1]
    outs = (shape_of(rows, width),) * 4 + (shape_of(rows, width, dtype=F32),) * 2
    return pl.pallas_call(
        near_kernel,
        out_shape=outs,
        in_specs=[SMEM, VMEM, VMEM],
        out_specs=(VMEM,) * 6,
        compiler_params=limit(16),
        cost_estimate=cost_of(2 * rows, width, 3 * width),
        name="near_blocks",
    )(place, gated, out_proj)


def moved(array, turn):
    pairs = []
    for core in range(2):
        for x in range(4):
            partner = x ^ 1 if (core + turn) % 2 == 0 else 3 - x
            pairs.append((4 * core + x, 4 * core + partner))
    return lax.ppermute(array, ("seq_2", "head"), pairs)


def passed(array, step):
    return lax.ppermute(array, "head", [(i, (i + step) % 4) for i in range(4)])


def gathered(rows):
    first = moved(rows, 0)
    joined = small_call(join_kernel, shape_of(2 * rows.shape[0], rows.shape[1]), rows, first)
    return (rows, first, moved(joined, 1))


def added(one, two):
    return (one.astype(F32) + two.astype(F32)).astype(BF16)


def steps(
    image_patches,
    text_embed,
    image_start,
    image_forget,
    adapter,
    norm_gain,
    in_proj,
    decay_proj,
    head_decay_ceiling,
    out_gain,
    out_proj,
):
    x = lax.axis_index("head")
    even = lax.axis_index("seq_2") == 0
    first, second = jnp.where(even, x ^ 1, 3 - x), jnp.where(even, 3 - x, x ^ 1)
    place = jnp.stack([x, first, second, x ^ 2, lax.axis_index(SEQ)]).astype(jnp.int32)
    decay = decay_proj.T
    gain = norm_gain[None]
    ceiling = head_decay_ceiling

    text_chunks = gathered(text_embed)
    patches = image_patches.transpose(0, 2, 1)
    leaving = adapter_leave(place, patches, adapter)
    stay = adapter_stay(place, patches, adapter)
    weights = relay_call(in_proj)
    block = shape_of(*text_embed.shape)
    arrived = moved(leaving, 0)
    last = moved(small_call(pass_kernel, block, stay, arrived), 1)
    embed = small_call(embed_kernel, block, stay, arrived, last)
    image_chunks = gathered(embed)

    *text_parts, text_state, text_span, late_weights = text_call(
        place, ceiling, text_chunks, gain, weights, decay
    )
    near, *partial = image_near_call(place, image_chunks[:2], gain, weights, decay)
    *held, states = image_state_call(
        place,
        ceiling,
        image_forget,
        image_chunks[2],
        *partial,
        gain,
        weights,
        decay,
        text_state,
        text_span,
    )
    slices = lax.all_to_all(states, SEQ, 0, 0, tiled=True)
    image_parts = image_attend_call(
        place, ceiling, image_forget, late_weights, near, *held
    )
    entering = lax.all_to_all(scan_call(image_start, slices), SEQ, 0, 0, tiled=True)

    far_t, far_i, gated = gate_call(
        place, entering, out_gain, out_proj, text_parts, image_parts
    )
    next_t, next_i, last_t, last_i, own_t, own_i = near_call(place, gated, out_proj)
    far_from_left = passed(far_t, 1)
    far_from_right = passed(far_i, 3)
    left_i = passed(next_i, 1)
    right_t = passed(last_t, 3)
    left_t = passed(added(next_t, far_from_left), 1)
    right_i = passed(added(last_i, far_from_right), 3)
    text_out = text_embed.astype(F32) + (own_t + left_t.astype(F32) + right_t.astype(F32))
    image_out = embed.astype(F32) + (own_i + left_i.astype(F32) + right_i.astype(F32))
    return (image_out.astype(BF16)[None], text_out.astype(BF16))


def solution(mesh):
    split = Mesh(
        mesh.devices.reshape(4, 4, 2, mesh.shape["head"]), ("seq_0", "seq_1", "seq_2", "head")
    )
    return jax.shard_map(
        steps,
        mesh=split,
        in_specs=(
            P(SEQ, None, "head"),
            P(SEQ, "head"),
            P(),
            P(),
            P("head", None),
            P(),
            P(None, None, "head"),
            P(None, "head"),
            P("head"),
            P("head", None),
            P("head", None),
        ),
        out_specs=(P(SEQ, None, "head"), P(SEQ, "head")),
        check_vma=False,
    )
```
